32 devices in a mesh: fsdp: 2 (over y), ctx: 4 (over z), tp: 4 (over x, core).
Axes of the slice: x: 2, y: 2, z: 4, core: 2. Of those that a mesh axis runs over, the one named last changes fastest.
Arguments:
- tokens: bfloat16 [4, 8192, 576], P('fsdp', ('ctx', 'tp')), may hold values from -6 to 6
- teacher: bfloat16 [4, 8192, 576], P('fsdp', ('ctx', 'tp')), may hold values from -6 to 6
- lengths: int32 [4], P('fsdp'), may hold values from 2048 to 8192, as said below
- gain_one: bfloat16 [576], P('fsdp'), may hold values from 0.5 to 1.5
- w_query: bfloat16 [576, 576], P('fsdp'), may hold values from -0.5 to 0.5
- w_key: bfloat16 [576, 192], P('fsdp'), may hold values from -0.25 to 0.25
- w_value: bfloat16 [576, 192], P('fsdp'), may hold values from -0.25 to 0.25
- w_out: bfloat16 [576, 576], P('fsdp'), may hold values from -1 to 1
- gain_two: bfloat16 [576], P('fsdp'), may hold values from 0.5 to 1.5
- w_gate: bfloat16 [576, 1536], P('fsdp', 'tp'), may hold values from -0.25 to 0.25
- w_up: bfloat16 [576, 1536], P('fsdp', 'tp'), may hold values from -0.25 to 0.25
- w_down: bfloat16 [1536, 576], P('tp', 'fsdp'), may hold values from -0.3125 to 0.3125
Outputs:
- output: float32 [4, 8192, 576], P('fsdp', ('ctx', 'tp'))
- loss_value: float32 [], replicated
- tokens_grad: float32 [4, 8192, 576], P('fsdp', ('ctx', 'tp'))
- gain_one_grad: float32 [576], P('fsdp')
- w_query_grad: float32 [576, 576], P('fsdp')
- w_key_grad: float32 [576, 192], P('fsdp')
- w_value_grad: float32 [576, 192], P('fsdp')
- w_out_grad: float32 [576, 576], P('fsdp')
- gain_two_grad: float32 [576], P('fsdp')
- w_gate_grad: float32 [576, 1536], P('fsdp', 'tp')
- w_up_grad: float32 [576, 1536], P('fsdp', 'tp')
- w_down_grad: float32 [1536, 576], P('tp', 'fsdp')
The draws below stay inside these ranges and needn't reach their ends.
Inputs may be any that keep to these rules, and one draw needn't show every extreme that they name: `lengths`: each sequence's valid slots come first. Some sequence has exactly 8192 valid slots and some exactly 2048.
All inputs are finite; a program needn't handle non-finite values.
Results may differ from the reference program's by a relative error of at most 0.033.
Values may be sent and summed in bfloat16 or wider, within the bound.
No kernel may reach another device: no remote copies, remote signals or barrier semaphores. Data moves between devices by JAX's collectives and lax.ppermute only.
A program may use at most 192 MiB of HBM per device.

```python
import jax
import jax.numpy as jnp
from jax import lax

D = 576
HEADS = 9
KV_HEADS = 3
HEAD_DIM = 64
FF = 1536
L = 8192
MIN_LEN = 2048
SEQS = 4


def draw_lengths(key, part):
    first_key, second_key = jax.random.split(key)
    values = jax.random.randint(first_key, (SEQS,), MIN_LEN, L + 1, dtype=jnp.int32)
    order = jax.random.permutation(second_key, SEQS)
    values = values.at[order[0]].set(L)
    values = values.at[order[1]].set(MIN_LEN)
    return values


def block_levels(stream_key, shape, cuts, smallest, top_value):
    def one(axis_at, shards_of):
        heights = jax.random.uniform(jax.random.fold_in(jax.random.fold_in(stream_key, 6), axis_at), (shards_of,), jnp.float32, smallest / len(cuts), top_value / len(cuts))
        return jnp.repeat(jnp.exp(heights), shape[axis_at] // shards_of).reshape((-1,) + (1,) * (len(shape) - axis_at - 1))

    loudness = one(*cuts[0])
    for cut in cuts[1:]:
        loudness = loudness * one(*cut)
    return loudness


def normal_values(key, shape, width, most, pieces=(), kind=jnp.bfloat16):
    values = width * jax.random.normal(key, shape, jnp.float32)
    if pieces:
        values = values * block_levels(key, shape, pieces, -0.22, 0.18)
    return jnp.clip(values, -most, most).astype(kind)


def setup_inputs(seed: int = 0) -> dict:
    keys = jax.random.split(jax.random.key(seed), 13)
    return {
        "tokens": normal_values(keys[0], (SEQS, L, D), 1.0, 6.0, ((0, 2), (1, 16))),
        "teacher": normal_values(keys[1], (SEQS, L, D), 1.0, 6.0, ((0, 2), (1, 16))),
        "lengths": draw_lengths(jax.random.fold_in(keys[12], 71), 0),
        "gain_one": jnp.clip(1.0 + 0.1 * jax.random.normal(keys[3], (D,), jnp.float32), 0.5, 1.5).astype(jnp.bfloat16),
        "w_query": normal_values(keys[4], (D, D), (D // 4) ** -0.5, 0.5, ((0, 2),)),
        "w_key": normal_values(keys[5], (D, KV_HEADS * HEAD_DIM), D ** -0.5, 0.25, ((0, 2),)),
        "w_value": normal_values(keys[6], (D, KV_HEADS * HEAD_DIM), D ** -0.5, 0.25, ((0, 2),)),
        "w_out": normal_values(keys[7], (D, D), (D // 16) ** -0.5, 1.0, ((0, 2),)),
        "gain_two": jnp.clip(1.0 + 0.1 * jax.random.normal(keys[8], (D,), jnp.float32), 0.5, 1.5).astype(jnp.bfloat16),
        "w_gate": normal_values(keys[9], (D, FF), D ** -0.5, 0.25, ((0, 2), (1, 4))),
        "w_up": normal_values(keys[10], (D, FF), D ** -0.5, 0.25, ((0, 2), (1, 4))),
        "w_down": normal_values(keys[11], (FF, D), (FF // 4) ** -0.5, 0.3125, ((0, 4), (1, 2))),
    }


EPS = 1e-05
ROPE_BASE = 10000.0
NEG = -1e+30
PRECISE = lax.Precision.HIGHEST

@jax.custom_vjp
def low(v):
    return lax.optimization_barrier(v.astype(jnp.bfloat16)).astype(jnp.float32)

@jax.custom_vjp
def low_back(v):
    return v

def low_keep(v):
    return (low(v), None)

def low_pass(kept, grad):
    return (grad,)

def back_keep(v):
    return (v, None)

def back_low(kept, grad):
    return (low(grad),)
low.defvjp(low_keep, low_pass)
low_back.defvjp(back_keep, back_low)

def matmul(left, right):
    return jnp.dot(left, right, precision=PRECISE, preferred_element_type=jnp.float32)

def norm_rows(values, gain):
    return values * lax.rsqrt(lax.optimization_barrier(jnp.mean(values * values, axis=-1, keepdims=True)) + EPS) * gain

def rope_angles(positions):
    half_width = HEAD_DIM // 2
    frequency = ROPE_BASE ** (-(jnp.arange(half_width, dtype=jnp.float32) * 2.0) / HEAD_DIM)
    angles = positions.astype(jnp.float32)[:, None] * frequency[None, :]
    return (jnp.cos(angles), jnp.sin(angles))

def rotate(values, cosine, sine_table):
    half_width = values.shape[-1] // 2
    lower_half = values[..., :half_width]
    upper_half = values[..., half_width:]
    cos_wide = cosine[:, None, :]
    sin_wide = sine_table[:, None, :]
    return jnp.concatenate([lower_half * cos_wide - upper_half * sin_wide, upper_half * cos_wide + lower_half * sin_wide], axis=-1)

def sequence_forward(params, seq_tokens, seq_teacher, length):
    gain_one, w_query, w_key, w_value, w_out, gain_two, w_gate, w_up, w_down = params
    group_size = HEADS // KV_HEADS
    score_scale = HEAD_DIM ** (-0.5)
    block_rows = min(512, L)
    cosine, sine_table = rope_angles(jnp.arange(L, dtype=jnp.int32))
    normed = low(norm_rows(seq_tokens, gain_one))
    queries = low(rotate(low_back(matmul(normed, w_query)).reshape(L, HEADS, HEAD_DIM), cosine, sine_table))
    key_rows = low(rotate(low_back(matmul(normed, w_key)).reshape(L, KV_HEADS, HEAD_DIM), cosine, sine_table))
    value_rows = low(low_back(matmul(normed, w_value))).reshape(L, KV_HEADS, HEAD_DIM)
    grouped = queries.reshape(L // block_rows, block_rows, KV_HEADS, group_size, HEAD_DIM)
    key_pos = jnp.arange(L, dtype=jnp.int32)

    def attend(block_item):
        query_block, block_start = block_item
        raw_scores = jnp.einsum('qkgd,tkd->kgqt', query_block, key_rows, precision=PRECISE)
        raw_scores = low_back(raw_scores)
        query_pos = block_start + jnp.arange(block_rows, dtype=jnp.int32)
        allowed = (key_pos[None, :] <= query_pos[:, None]) & (key_pos[None, :] < length)
        scores = jnp.where(allowed, raw_scores * score_scale, NEG)
        row_max = lax.optimization_barrier(jnp.max(scores, axis=-1, keepdims=True))
        weights = jnp.where(allowed, jnp.exp(scores - row_max), 0.0)
        probs = low(weights / lax.optimization_barrier(jnp.sum(weights, axis=-1, keepdims=True)))
        mixture = jnp.einsum('kgqt,tkd->qkgd', probs, value_rows, precision=PRECISE)
        return mixture.reshape(block_rows, D)
    block_starts = jnp.arange(L // block_rows, dtype=jnp.int32) * block_rows
    attended = lax.map(jax.checkpoint(attend), (grouped, block_starts)).reshape(L, D)
    attended = low(low_back(attended))
    middle = seq_tokens + low_back(matmul(attended, w_out))
    normed_two = low(norm_rows(middle, gain_two))
    gate_pre = low_back(matmul(normed_two, w_gate))
    up_pre = low_back(matmul(normed_two, w_up))
    hidden = low(jax.nn.silu(gate_pre) * up_pre)
    result = middle + low_back(matmul(hidden, w_down))
    valid_mask = (jnp.arange(L, dtype=jnp.int32) < length).astype(jnp.float32)
    squared = jnp.sum(valid_mask[:, None] * (result - seq_teacher) ** 2)
    return (result, squared)

def reference(tokens, teacher, lengths, gain_one, w_query, w_key, w_value, w_out, gain_two, w_gate, w_up, w_down):
    floats = [a.astype(jnp.float32) for a in (gain_one, w_query, w_key, w_value, w_out, gain_two, w_gate, w_up, w_down)]
    token_wide = tokens.astype(jnp.float32)
    teacher_wide = teacher.astype(jnp.float32)
    count_total = jnp.sum(lengths).astype(jnp.float32)

    def whole_layer(inputs, *params):

        def seq_step(running, seq_items):
            seq_tokens, seq_teacher, length = seq_items
            result, squared = sequence_forward(params, seq_tokens, seq_teacher, length)
            return (running + squared, result)
        running, results = lax.scan(seq_step, jnp.zeros((), jnp.float32), (inputs, teacher_wide, lengths))
        return (running / (count_total * D), results)
    loss_value, pullback, output = jax.vjp(whole_layer, token_wide, *floats, has_aux=True)
    gradients = pullback(jnp.asarray(SEQS * L * D / 2.0, jnp.float32))
    return (output, loss_value, gradients[0], gradients[1], gradients[2], gradients[3], gradients[4], gradients[5], gradients[6], gradients[7], gradients[8], gradients[9])
```

```python
import functools

import jax
import jax.numpy as jnp
from jax import lax
from jax.experimental import pallas as pl
from jax.experimental.pallas import tpu as pltpu
from jax.sharding import PartitionSpec as P

HEADS = 9
KV_HEADS = 3
GROUP = HEADS // KV_HEADS
HEAD_DIM = 64
AUG = HEAD_DIM + 16

EPS = 1e-05
ROPE_BASE = 10000.0
NEG = -1e30
LOG2E = 1.4426950408889634
EXP2_SCALE = LOG2E * HEAD_DIM ** (-0.5)

f32 = jnp.float32
bf16 = jnp.bfloat16
NN = ((1,), (0,))
TN = ((0,), (0,))
NT = ((1,), (1,))


def dot(left, right, dims):
    return lax.dot_general(left, right, (dims, ((), ())), preferred_element_type=f32)


def norm_rows(values, gain):
    return values * lax.rsqrt(jnp.mean(values * values, axis=-1, keepdims=True) + EPS) * gain


def rope_tables(positions):
    half_width = HEAD_DIM // 2
    frequency = ROPE_BASE ** (-(jnp.arange(half_width, dtype=f32) * 2.0) / HEAD_DIM)
    angles = frequency[:, None] * positions.astype(f32)[None, :]
    return (jnp.cos(angles), jnp.sin(angles))


def rotate_cols(values, cosine, sine):
    half_width = HEAD_DIM // 2
    lower = values[..., :half_width, :]
    upper = values[..., half_width:, :]
    return jnp.concatenate([lower * cosine - upper * sine, upper * cosine + lower * sine], axis=-2)


def three_pieces(row):
    first = row.astype(bf16)
    rest = row - first.astype(f32)
    second = rest.astype(bf16)
    third = (rest - second.astype(f32)).astype(bf16)
    return (first, second, third)


def penalty_row(block_start, width, length):
    key_pos = block_start + lax.broadcasted_iota(jnp.int32, (1, width), 1)
    return jnp.where(key_pos < length, 0.0, NEG).astype(bf16)


def extra_rows(rows, width):
    wide = jnp.zeros((16, width), f32)
    index = lax.broadcasted_iota(jnp.int32, (16, width), 0)
    for place, row in enumerate(rows):
        wide = jnp.where(index == place, row.astype(f32), wide)
    return wide.astype(bf16)


def forward_kernel(info, q_ref, kv_ref, out_ref, lse_ref, qa_ref, max_ref, acc_ref):
    seq = pl.program_id(0)
    slots = q_ref.shape[-1]
    cols = GROUP * slots
    length = info[seq]
    own = info[2]
    ones_row = jnp.ones((1, cols), f32)
    qa_ref[0:HEAD_DIM] = jnp.concatenate([q_ref[0, h] for h in range(GROUP)], axis=1)
    qa_ref[HEAD_DIM:AUG] = extra_rows([ones_row], cols)
    max_ref[...] = jnp.full(max_ref.shape, NEG, f32)
    acc_ref[...] = jnp.zeros(acc_ref.shape, f32)
    value_ones = extra_rows([jnp.ones((1, slots), f32)], slots)

    def step(block, diagonal):
        key_cols = jnp.concatenate(
            [
                kv_ref[block, 0, 0:HEAD_DIM],
                extra_rows([penalty_row(block * slots, slots, length)], slots),
            ],
            axis=0,
        )
        value_cols = jnp.concatenate([kv_ref[block, 0, HEAD_DIM:], value_ones], axis=0)
        scores = dot(key_cols, qa_ref[...], TN) * EXP2_SCALE
        if diagonal:
            key_at = lax.broadcasted_iota(jnp.int32, (slots, cols), 0)
            query_at = lax.broadcasted_iota(jnp.int32, (slots, cols), 1) % slots
            scores = jnp.where(key_at <= query_at, scores, NEG)
        old_max = max_ref[...]
        new_max = jnp.maximum(old_max, jnp.max(scores, axis=0, keepdims=True))
        weights = jnp.exp2(scores - new_max).astype(bf16)
        max_ref[...] = new_max
        acc_ref[...] = acc_ref[...] * jnp.exp2(old_max - new_max) + dot(value_cols, weights, NN)

    blocks_valid = (length + slots - 1) // slots
    lax.fori_loop(0, jnp.minimum(own, blocks_valid), lambda b, c: (step(b, False), c)[1], 0)

    @pl.when(own < blocks_valid)
    def _():
        step(own, True)

    total = acc_ref[HEAD_DIM : HEAD_DIM + 1]
    heads_out = acc_ref[0:HEAD_DIM] / total
    lse = (max_ref[...] + jnp.log2(total)) * (1.0 / EXP2_SCALE)
    for h in range(GROUP):
        out_ref[0, h] = heads_out[:, h * slots : (h + 1) * slots].astype(bf16)
        lse_ref[0, h : h + 1] = lse[:, h * slots : (h + 1) * slots]


def backward_kernel(info, q_ref, do_ref, o_ref, lse_ref, kv_ref, dq_ref, dkv_ref, qa_ref, da_ref, acc_ref):
    seq = pl.program_id(0)
    slots = q_ref.shape[-1]
    cols = GROUP * slots
    length = info[seq]
    own = info[2]
    block_count = kv_ref.shape[0]
    ones_row = jnp.ones((1, cols), f32)
    ones_key = jnp.ones((1, slots), f32)
    lse = jnp.concatenate([lse_ref[0, h : h + 1] for h in range(GROUP)], axis=1)
    grads = jnp.concatenate([do_ref[0, h] for h in range(GROUP)], axis=1)
    heads_out = jnp.concatenate([o_ref[0, h] for h in range(GROUP)], axis=1)
    delta = jnp.sum(grads.astype(f32) * heads_out.astype(f32), axis=0, keepdims=True)
    qa_ref[0:HEAD_DIM] = jnp.concatenate([q_ref[0, h] for h in range(GROUP)], axis=1)
    qa_ref[HEAD_DIM:AUG] = extra_rows(three_pieces(-lse) + (ones_row,), cols)
    da_ref[0:HEAD_DIM] = grads
    da_ref[HEAD_DIM:AUG] = extra_rows(three_pieces(-delta), cols)
    acc_ref[...] = jnp.zeros(acc_ref.shape, f32)
    value_ones = extra_rows([ones_key] * 3, slots)

    def step(block, diagonal):
        keys = kv_ref[block, 0, 0:HEAD_DIM]
        key_cols = jnp.concatenate(
            [keys, extra_rows([ones_key] * 3 + [penalty_row(block * slots, slots, length)], slots)],
            axis=0,
        )
        value_cols = jnp.concatenate([kv_ref[block, 0, HEAD_DIM:], value_ones], axis=0)
        scores = dot(qa_ref[...], key_cols, TN) * EXP2_SCALE
        if diagonal:
            query_at = lax.broadcasted_iota(jnp.int32, (cols, slots), 0) % slots
            key_at = lax.broadcasted_iota(jnp.int32, (cols, slots), 1)
            scores = jnp.where(key_at <= query_at, scores, NEG)
        weights = jnp.exp2(scores)
        d_scores = (weights * dot(da_ref[...], value_cols, TN)).astype(bf16)
        d_value = dot(da_ref[0:HEAD_DIM], weights.astype(bf16), NN)
        d_key = dot(qa_ref[0:HEAD_DIM], d_scores, NN) * (HEAD_DIM ** (-0.5))
        acc_ref[...] += dot(keys, d_scores, NT)
        dkv_ref[block, 0, 0:HEAD_DIM] = d_key.astype(bf16)
        dkv_ref[block, 0, HEAD_DIM:] = d_value.astype(bf16)

    active = own * slots < length
    below = jnp.where(active, own, 0)
    lax.fori_loop(0, below, lambda b, c: (step(b, False), c)[1], 0)

    @pl.when(active)
    def _():
        step(own, True)

    def clear(block, carry):
        dkv_ref[block, 0] = jnp.zeros(dkv_ref.shape[2:], bf16)
        return carry

    lax.fori_loop(jnp.where(active, own + 1, 0), block_count, clear, 0)
    d_query = acc_ref[...] * (HEAD_DIM ** (-0.5))
    for h in range(GROUP):
        dq_ref[0, h] = d_query[:, h * slots : (h + 1) * slots]


def vmem_spec(shape, seq_axis):
    def index(seq):
        return tuple(seq if axis == seq_axis else 0 for axis in range(len(shape)))

    block = tuple(1 if axis == seq_axis else size for axis, size in enumerate(shape))
    return pl.BlockSpec(block, index)


PARAMS = pltpu.CompilerParams(vmem_limit_bytes=60 * 2**20)


def attend(info, queries, kv):
    seqs, _, _, slots = queries.shape
    cols = GROUP * slots
    head_shape = (seqs, GROUP, HEAD_DIM, slots)
    row_shape = (seqs, GROUP, slots)
    return pl.pallas_call(
        forward_kernel,
        grid=(seqs,),
        in_specs=[
            pl.BlockSpec(memory_space=pltpu.SMEM),
            vmem_spec(head_shape, 0),
            vmem_spec(kv.shape, 1),
        ],
        out_specs=[vmem_spec(head_shape, 0), vmem_spec(row_shape, 0)],
        out_shape=[
            jax.ShapeDtypeStruct(head_shape, bf16),
            jax.ShapeDtypeStruct(row_shape, f32),
        ],
        scratch_shapes=[
            pltpu.VMEM((AUG, cols), bf16),
            pltpu.VMEM((1, cols), f32),
            pltpu.VMEM((AUG, cols), f32),
        ],
        compiler_params=PARAMS,
        name="attend",
    )(info, queries, kv)


def attend_back(info, queries, grads, heads_out, lse, kv):
    seqs, _, _, slots = queries.shape
    cols = GROUP * slots
    head_shape = (seqs, GROUP, HEAD_DIM, slots)
    row_shape = (seqs, GROUP, slots)
    return pl.pallas_call(
        backward_kernel,
        grid=(seqs,),
        in_specs=[
            pl.BlockSpec(memory_space=pltpu.SMEM),
            vmem_spec(head_shape, 0),
            vmem_spec(head_shape, 0),
            vmem_spec(head_shape, 0),
            vmem_spec(row_shape, 0),
            vmem_spec(kv.shape, 1),
        ],
        out_specs=[vmem_spec(head_shape, 0), vmem_spec(kv.shape, 1)],
        out_shape=[
            jax.ShapeDtypeStruct(head_shape, f32),
            jax.ShapeDtypeStruct(kv.shape, bf16),
        ],
        scratch_shapes=[
            pltpu.VMEM((AUG, cols), bf16),
            pltpu.VMEM((AUG, cols), bf16),
            pltpu.VMEM((HEAD_DIM, cols), f32),
        ],
        compiler_params=PARAMS,
        name="attend_back",
    )(info, queries, grads, heads_out, lse, kv)


def shards(
    tokens,
    teacher,
    lengths,
    gain_one,
    w_query,
    w_key,
    w_value,
    w_out,
    gain_two,
    w_gate,
    w_up,
    w_down,
):
    seqs, slots, width = tokens.shape
    rows = seqs * slots
    kv_width = KV_HEADS * HEAD_DIM
    qkv_width = width + 2 * kv_width
    out_at = -(-qkv_width // 128) * 128
    gain_at = out_at + width
    pack_width = -(-(gain_at + 4) // 128) * 128
    half = w_query.shape[0]
    hidden_part = w_gate.shape[1]
    fsdp_size = lax.axis_size("fsdp")
    tp_size = lax.axis_size("tp")
    ring = ("ctx", "tp")

    valid_here = jnp.sum(lengths)
    length_cols = jnp.stack([valid_here // 128, valid_here % 128]).astype(bf16)
    packed = jnp.concatenate(
        [
            w_query,
            w_key,
            w_value,
            jnp.zeros((half, out_at - qkv_width), bf16),
            w_out,
            gain_one[:, None],
            gain_two[:, None],
            jnp.broadcast_to(length_cols[None], (half, 2)),
            jnp.zeros((half, pack_width - gain_at - 4), bf16),
        ],
        axis=1,
    )
    packed = lax.all_gather(packed, "fsdp", axis=0, tiled=False)
    count_total = jnp.sum(
        packed[:, 0, gain_at + 2].astype(f32) * 128.0 + packed[:, 0, gain_at + 3].astype(f32)
    )
    packed = packed.reshape(width, pack_width)
    w_qkv = packed[:, :qkv_width]
    w_o = packed[:, out_at : out_at + width]
    g_one = packed[:, gain_at].astype(f32)
    g_two = packed[:, gain_at + 1].astype(f32)

    own = lax.axis_index(ring)
    positions = own * slots + jnp.arange(slots, dtype=jnp.int32)
    cosine, sine = rope_tables(positions)
    info = jnp.concatenate([lengths.astype(jnp.int32), own.astype(jnp.int32)[None]])
    valid_mask = (positions[None, :] < lengths[:, None]).astype(f32)

    inputs = tokens.astype(f32)
    normed = norm_rows(inputs, g_one).astype(bf16)
    qkv = jnp.einsum("df,sld->sfl", w_qkv, normed, preferred_element_type=f32)
    qk = qkv[:, : width + kv_width].reshape(seqs, HEADS + KV_HEADS, HEAD_DIM, slots)
    qk = rotate_cols(qk, cosine, sine).astype(bf16)
    queries = qk[:, :HEADS]
    values = qkv[:, width + kv_width :].astype(bf16).reshape(seqs, KV_HEADS, HEAD_DIM, slots)
    kv_own = jnp.concatenate([qk[:, HEADS:], values], axis=2)

    kv_all = [
        lax.all_gather(kv_own[:, g], ring, axis=0, tiled=False) for g in range(KV_HEADS)
    ]
    ffn_pack = jnp.concatenate([w_gate, w_up, w_down.T], axis=1)
    ffn_all = lax.all_gather(ffn_pack, ("tp", "fsdp"), axis=0, tiled=False)
    ffn_all = ffn_all.reshape(tp_size, width, 3 * hidden_part)

    attended = []
    lses = []
    for g in range(KV_HEADS):
        out, lse = attend(info, queries[:, g * GROUP : (g + 1) * GROUP], kv_all[g])
        attended.append(out)
        lses.append(lse)
    attended_t = jnp.concatenate(attended, axis=1).reshape(seqs, width, slots)

    middle = inputs + jnp.einsum("sfl,fd->sld", attended_t, w_o, preferred_element_type=f32)
    normed_two = norm_rows(middle, g_two).astype(bf16)
    flat_two = normed_two.reshape(rows, width)
    gate_up_w = ffn_all[:, :, : 2 * hidden_part]
    down_wt = ffn_all[:, :, 2 * hidden_part :]
    gate_up = jnp.einsum("rd,tdf->trf", flat_two, gate_up_w, preferred_element_type=f32)
    gate_pre = gate_up[..., :hidden_part]
    up_pre = gate_up[..., hidden_part:]
    gate_sigmoid = jax.nn.sigmoid(gate_pre)
    hidden = (gate_pre * gate_sigmoid * up_pre).astype(bf16)
    branch = jnp.einsum("trf,tdf->rd", hidden, down_wt, preferred_element_type=f32)
    result = middle + branch.reshape(seqs, slots, width)
    mismatch = result - teacher.astype(f32)
    squared_part = jnp.sum(valid_mask[..., None] * mismatch * mismatch)
    squared_total = lax.psum(squared_part, ("fsdp", "ctx", "tp"))
    loss_value = squared_total / (count_total * width)
    slots_all = seqs * fsdp_size * slots * lax.axis_size(ring)
    d_result = valid_mask[..., None] * mismatch * (slots_all / count_total)
    d_branch = d_result.astype(bf16).reshape(rows, width)
    d_hidden = jnp.einsum("rd,tdf->trf", d_branch, down_wt, preferred_element_type=f32)
    d_down_wt = jnp.einsum("rd,trf->tdf", d_branch, hidden, preferred_element_type=f32)
    d_gate = (d_hidden * up_pre * gate_sigmoid * (1.0 + gate_pre * (1.0 - gate_sigmoid))).astype(bf16)
    d_up = (d_hidden * gate_pre * gate_sigmoid).astype(bf16)
    d_gate_up = jnp.concatenate([d_gate, d_up], axis=-1)
    d_gate_up_w = jnp.einsum("rd,trf->tdf", flat_two, d_gate_up, preferred_element_type=f32)
    d_normed_two = jnp.einsum("trf,tdf->rd", d_gate_up, gate_up_w, preferred_element_type=f32)
    norm_two_pull = jax.vjp(norm_rows, middle, g_two)[1]
    d_middle_norm, d_gain_two = norm_two_pull(d_normed_two.reshape(seqs, slots, width))
    d_middle = d_result + d_middle_norm
    d_attn_branch = d_middle.astype(bf16)
    d_attended_t = jnp.einsum("fd,sld->sfl", w_o, d_attn_branch, preferred_element_type=f32)
    d_attended_t = d_attended_t.astype(bf16).reshape(seqs, HEADS, HEAD_DIM, slots)
    d_out_w = jnp.einsum("sfl,sld->fd", attended_t, d_attn_branch, preferred_element_type=f32)

    d_query_parts = []
    d_kv_parts = []
    for g in range(KV_HEADS):
        heads = slice(g * GROUP, (g + 1) * GROUP)
        d_query, d_kv = attend_back(
            info, queries[:, heads], d_attended_t[:, heads], attended[g], lses[g], kv_all[g]
        )
        d_query_parts.append(d_query)
        d_kv_parts.append(lax.psum_scatter(d_kv, ring, scatter_dimension=0, tiled=False))
    d_ffn = jnp.concatenate([d_gate_up_w, d_down_wt], axis=-1).astype(bf16)
    d_ffn = d_ffn.reshape(tp_size * fsdp_size, half, 3 * hidden_part)
    d_ffn = lax.psum_scatter(d_ffn, ("tp", "fsdp"), scatter_dimension=0, tiled=False)
    d_ffn = lax.psum(d_ffn, "ctx").astype(f32)

    d_kv = jnp.stack(d_kv_parts, axis=1).astype(f32)
    d_qk = jnp.concatenate(d_query_parts + [d_kv[:, :, :HEAD_DIM]], axis=1)
    d_qk = rotate_cols(d_qk, cosine, -sine).astype(bf16).reshape(seqs, width + kv_width, slots)
    d_values = d_kv[:, :, HEAD_DIM:].astype(bf16).reshape(seqs, kv_width, slots)
    d_qkv = jnp.concatenate([d_qk, d_values], axis=1)
    d_normed = jnp.einsum("sfl,df->sld", d_qkv, w_qkv, preferred_element_type=f32)
    d_qkv_w = jnp.einsum("sld,sfl->df", normed, d_qkv, preferred_element_type=f32)
    norm_one_pull = jax.vjp(norm_rows, inputs, g_one)[1]
    d_inputs_norm, d_gain_one = norm_one_pull(d_normed)
    tokens_grad = d_middle + d_inputs_norm
    d_packed = jnp.concatenate(
        [
            d_qkv_w,
            jnp.zeros((width, out_at - qkv_width), f32),
            d_out_w,
            d_gain_one[:, None],
            d_gain_two[:, None],
            jnp.zeros((width, pack_width - gain_at - 2), f32),
        ],
        axis=1,
    ).astype(bf16)
    d_packed = d_packed.reshape(fsdp_size, half, pack_width)
    d_packed = lax.psum_scatter(d_packed, "fsdp", scatter_dimension=0, tiled=False)
    d_packed = lax.psum(d_packed, ring).astype(f32)
    return (
        result,
        loss_value,
        tokens_grad,
        d_packed[:, gain_at],
        d_packed[:, :width],
        d_packed[:, width : width + kv_width],
        d_packed[:, width + kv_width : qkv_width],
        d_packed[:, out_at : out_at + width],
        d_packed[:, gain_at + 1],
        d_ffn[:, :hidden_part],
        d_ffn[:, hidden_part : 2 * hidden_part],
        d_ffn[:, 2 * hidden_part :].T,
    )


def solution(mesh):
    slots_spec = P("fsdp", ("ctx", "tp"), None)
    rows_spec = P("fsdp", None)
    return jax.shard_map(
        shards,
        mesh=mesh,
        in_specs=(
            slots_spec,
            slots_spec,
            P("fsdp"),
            P("fsdp"),
            rows_spec,
            rows_spec,
            rows_spec,
            rows_spec,
            P("fsdp"),
            P("fsdp", "tp"),
            P("fsdp", "tp"),
            P("tp", "fsdp"),
        ),
        out_specs=(
            slots_spec,
            P(),
            slots_spec,
            P("fsdp"),
            rows_spec,
            rows_spec,
            rows_spec,
            rows_spec,
            P("fsdp"),
            P("fsdp", "tp"),
            P("fsdp", "tp"),
            P("tp", "fsdp"),
        ),
        check_vma=False,
    )
```

```python
import functools

import jax
import jax.numpy as jnp
from jax import lax
from jax.experimental import pallas as pl
from jax.experimental.pallas import tpu as pltpu
from jax.sharding import PartitionSpec as P

HEADS = 9
KV_HEADS = 3
GROUP = HEADS // KV_HEADS
HEAD_DIM = 64
AUG = HEAD_DIM + 16

EPS = 1e-05
ROPE_BASE = 10000.0
NEG = -1e30
LOG2E = 1.4426950408889634
EXP2_SCALE = LOG2E * HEAD_DIM ** (-0.5)

f32 = jnp.float32
bf16 = jnp.bfloat16
NN = ((1,), (0,))
TN = ((0,), (0,))
NT = ((1,), (1,))


def dot(left, right, dims):
    return lax.dot_general(left, right, (dims, ((), ())), preferred_element_type=f32)


def norm_rows(values, gain):
    return values * lax.rsqrt(jnp.mean(values * values, axis=-1, keepdims=True) + EPS) * gain


def rope_tables(positions):
    half_width = HEAD_DIM // 2
    frequency = ROPE_BASE ** (-(jnp.arange(half_width, dtype=f32) * 2.0) / HEAD_DIM)
    angles = frequency[None, None, :, None] * positions.astype(f32)[:, None, None, :]
    return (jnp.cos(angles), jnp.sin(angles))


def rotate_cols(values, cosine, sine):
    half_width = HEAD_DIM // 2
    lower = values[..., :half_width, :]
    upper = values[..., half_width:, :]
    return jnp.concatenate([lower * cosine - upper * sine, upper * cosine + lower * sine], axis=-2)


def three_pieces(row):
    first = row.astype(bf16)
    rest = row - first.astype(f32)
    second = rest.astype(bf16)
    third = (rest - second.astype(f32)).astype(bf16)
    return (first, second, third)


def penalty_row(block_start, width, length):
    key_pos = block_start + lax.broadcasted_iota(jnp.int32, (1, width), 1)
    return jnp.where(key_pos < length, 0.0, NEG).astype(bf16)


def extra_rows(rows, width):
    wide = jnp.zeros((16, width), f32)
    index = lax.broadcasted_iota(jnp.int32, (16, width), 0)
    for place, row in enumerate(rows):
        wide = jnp.where(index == place, row.astype(f32), wide)
    return wide.astype(bf16)


def block_of(device, seq, ring_size):
    return jnp.where(seq % 2 == 1, ring_size - 1 - device, device)


def forward_kernel(ring_size, masks, first, last, *refs):
    count = len(masks)
    info, q_ref = refs[:2]
    kv_refs = refs[2 : 2 + count]
    rest = refs[2 + count :]
    seq = pl.program_id(0)
    slots = kv_refs[0].shape[-1]
    cols = GROUP * slots
    if first:
        qa_ref, max_ref, acc_ref = rest
        qa_ref[0, 0, 0:HEAD_DIM] = jnp.concatenate([q_ref[0, h] for h in range(GROUP)], axis=1)
        qa_ref[0, 0, HEAD_DIM:AUG] = extra_rows([jnp.ones((1, cols), f32)], cols)
        max_ref[...] = jnp.full(max_ref.shape, NEG, f32)
        acc_ref[...] = jnp.zeros(acc_ref.shape, f32)
    else:
        qa_ref = q_ref
        if last:
            max_in, acc_in, out_ref, lse_ref, max_ref, acc_ref = rest
        else:
            max_in, acc_in, max_ref, acc_ref = rest
        max_ref[...] = max_in[...]
        acc_ref[...] = acc_in[...]
    device = info[info.shape[0] - 1]
    length = info[seq]
    own_block = block_of(device, seq, ring_size)

    def step(kv_ref, block, diagonal):
        key_cols = jnp.concatenate(
            [
                kv_ref[0, 0, 0:HEAD_DIM],
                extra_rows([penalty_row(block * slots, slots, length)], slots),
            ],
            axis=0,
        )
        value_ones = extra_rows([jnp.ones((1, slots), f32)], slots)
        value_cols = jnp.concatenate([kv_ref[0, 0, HEAD_DIM:], value_ones], axis=0)
        scores = dot(key_cols, qa_ref[0, 0], TN) * EXP2_SCALE
        if diagonal:
            key_at = lax.broadcasted_iota(jnp.int32, (slots, cols), 0)
            query_at = lax.broadcasted_iota(jnp.int32, (slots, cols), 1) % slots
            scores = jnp.where(key_at <= query_at, scores, NEG)
        old_max = max_ref[0, 0]
        new_max = jnp.maximum(old_max, jnp.max(scores, axis=0, keepdims=True))
        weights = jnp.exp2(scores - new_max).astype(bf16)
        max_ref[0, 0] = new_max
        acc_ref[0, 0] = acc_ref[0, 0] * jnp.exp2(old_max - new_max) + dot(value_cols, weights, NN)

    for kv_ref, mask in zip(kv_refs, masks):
        block = block_of(device ^ mask, seq, ring_size)
        below = block < own_block if mask else block == own_block

        @pl.when(below & (block * slots < length))
        def _():
            step(kv_ref, block, mask == 0)

    if last:
        total = acc_ref[0, 0, HEAD_DIM : HEAD_DIM + 1]
        heads_out = acc_ref[0, 0, 0:HEAD_DIM] / total
        lse_ref[0, 0] = (max_ref[0, 0] + jnp.log2(total)) * (1.0 / EXP2_SCALE)
        for h in range(GROUP):
            out_ref[0, h] = heads_out[:, h * slots : (h + 1) * slots].astype(bf16)


def backward_kernel(ring_size, masks, first, last, *refs):
    count = len(masks)
    info = refs[0]
    kv_refs = refs[1 : 1 + count]
    rest = refs[1 + count :]
    seq = pl.program_id(0)
    slots = kv_refs[0].shape[-1]
    cols = GROUP * slots
    if first:
        q_ref, do_ref, o_ref, lse_ref = rest[:4]
        dkv_refs = rest[4 : 4 + count]
        acc_ref, qa_ref, da_ref = rest[4 + count :]
        grads = jnp.concatenate([do_ref[0, h] for h in range(GROUP)], axis=1)
        heads_out = jnp.concatenate([o_ref[0, h] for h in range(GROUP)], axis=1)
        delta = jnp.sum(grads.astype(f32) * heads_out.astype(f32), axis=0, keepdims=True)
        qa_ref[0, 0, 0:HEAD_DIM] = jnp.concatenate([q_ref[0, h] for h in range(GROUP)], axis=1)
        qa_ref[0, 0, HEAD_DIM:AUG] = extra_rows(
            three_pieces(-lse_ref[0, 0]) + (jnp.ones((1, cols), f32),), cols
        )
        da_ref[0, 0, 0:HEAD_DIM] = grads
        da_ref[0, 0, HEAD_DIM:AUG] = extra_rows(three_pieces(-delta), cols)
        acc_ref[...] = jnp.zeros(acc_ref.shape, f32)
    else:
        qa_ref, da_ref, acc_in = rest[:3]
        dkv_refs = rest[3 : 3 + count]
        if last:
            dq_ref, acc_ref = rest[3 + count :]
        else:
            (acc_ref,) = rest[3 + count :]
        acc_ref[...] = acc_in[...]
    device = info[info.shape[0] - 1]
    length = info[seq]
    own_block = block_of(device, seq, ring_size)

    def step(kv_ref, dkv_ref, block, diagonal):
        ones_key = jnp.ones((1, slots), f32)
        keys = kv_ref[0, 0, 0:HEAD_DIM]
        key_cols = jnp.concatenate(
            [keys, extra_rows([ones_key] * 3 + [penalty_row(block * slots, slots, length)], slots)],
            axis=0,
        )
        value_cols = jnp.concatenate(
            [kv_ref[0, 0, HEAD_DIM:], extra_rows([ones_key] * 3, slots)], axis=0
        )
        scores = dot(qa_ref[0, 0], key_cols, TN) * EXP2_SCALE
        if diagonal:
            query_at = lax.broadcasted_iota(jnp.int32, (cols, slots), 0) % slots
            key_at = lax.broadcasted_iota(jnp.int32, (cols, slots), 1)
            scores = jnp.where(key_at <= query_at, scores, NEG)
        weights = jnp.exp2(scores)
        d_scores = (weights * dot(da_ref[0, 0], value_cols, TN)).astype(bf16)
        d_value = dot(da_ref[0, 0, 0:HEAD_DIM], weights.astype(bf16), NN)
        d_key = dot(qa_ref[0, 0, 0:HEAD_DIM], d_scores, NN) * (HEAD_DIM ** (-0.5))
        acc_ref[0, 0] += dot(keys, d_scores, NT)
        dkv_ref[0, 0, 0:HEAD_DIM] = d_key.astype(bf16)
        dkv_ref[0, 0, HEAD_DIM:] = d_value.astype(bf16)

    active = own_block * slots < length
    for kv_ref, dkv_ref, mask in zip(kv_refs, dkv_refs, masks):
        block = block_of(device ^ mask, seq, ring_size)
        run = active & (block < own_block if mask else block == own_block)

        @pl.when(run)
        def _():
            step(kv_ref, dkv_ref, block, mask == 0)

        @pl.when(jnp.logical_not(run))
        def _():
            dkv_ref[...] = jnp.zeros(dkv_ref.shape, bf16)

    if last:
        d_query = acc_ref[0, 0] * (HEAD_DIM ** (-0.5))
        for h in range(GROUP):
            dq_ref[0, h] = d_query[:, h * slots : (h + 1) * slots]


def head_spec(rows, lanes, heads=1):
    return pl.BlockSpec((1, heads, rows, lanes), lambda seq, group: (seq, group, 0, 0))


SMEM_SPEC = pl.BlockSpec(memory_space=pltpu.SMEM)
PARAMS = pltpu.CompilerParams(vmem_limit_bytes=60 * 2**20)


def attend(ring_size, masks, info, queries, kvs, state, last):
    seqs, groups, _, slots = kvs[0].shape
    cols = GROUP * slots
    first = state is None
    kv_spec = head_spec(2 * HEAD_DIM, slots)
    wide_spec = head_spec(AUG, cols)
    row_spec = head_spec(1, cols)
    wide_shape = (seqs, groups, AUG, cols)
    row_shape = jax.ShapeDtypeStruct((seqs, groups, 1, cols), f32)
    state_specs = [row_spec, wide_spec]
    state_shapes = [row_shape, jax.ShapeDtypeStruct(wide_shape, f32)]
    query_spec = wide_spec
    scratch = []
    if first:
        query_spec = head_spec(HEAD_DIM, slots, GROUP)
        out_specs = [wide_spec] + state_specs
        out_shape = [jax.ShapeDtypeStruct(wide_shape, bf16)] + state_shapes
    elif last:
        out_specs = [head_spec(HEAD_DIM, slots, GROUP), row_spec]
        out_shape = [jax.ShapeDtypeStruct((seqs, groups * GROUP, HEAD_DIM, slots), bf16), row_shape]
        scratch = [pltpu.VMEM((1, 1, 1, cols), f32), pltpu.VMEM((1, 1, AUG, cols), f32)]
    else:
        out_specs = state_specs
        out_shape = state_shapes
    return pl.pallas_call(
        functools.partial(forward_kernel, ring_size, masks, first, last),
        grid=(seqs, groups),
        in_specs=[SMEM_SPEC, query_spec]
        + [kv_spec] * len(masks)
        + ([] if first else state_specs),
        out_specs=out_specs,
        out_shape=out_shape,
        scratch_shapes=scratch,
        compiler_params=PARAMS,
        name="attend",
    )(info, queries, *kvs, *([] if first else state))


def attend_back(ring_size, masks, info, kvs, operands, first, last):
    seqs, groups, _, slots = kvs[0].shape
    cols = GROUP * slots
    kv_spec = head_spec(2 * HEAD_DIM, slots)
    heads_spec = head_spec(HEAD_DIM, slots, GROUP)
    wide_spec = head_spec(AUG, cols)
    acc_spec = head_spec(HEAD_DIM, cols)
    kv_shape = jax.ShapeDtypeStruct(kvs[0].shape, bf16)
    wide_shape = jax.ShapeDtypeStruct((seqs, groups, AUG, cols), bf16)
    acc_shape = jax.ShapeDtypeStruct((seqs, groups, HEAD_DIM, cols), f32)
    scratch = []
    if first:
        operand_specs = [heads_spec] * 3 + [head_spec(1, cols)]
        out_specs = [acc_spec, wide_spec, wide_spec]
        out_shape = [acc_shape, wide_shape, wide_shape]
    else:
        operand_specs = [wide_spec, wide_spec, acc_spec]
        if last:
            out_specs = [heads_spec]
            out_shape = [jax.ShapeDtypeStruct((seqs, groups * GROUP, HEAD_DIM, slots), f32)]
            scratch = [pltpu.VMEM((1, 1, HEAD_DIM, cols), f32)]
        else:
            out_specs = [acc_spec]
            out_shape = [acc_shape]
    outs = pl.pallas_call(
        functools.partial(backward_kernel, ring_size, masks, first, last),
        grid=(seqs, groups),
        in_specs=[SMEM_SPEC] + [kv_spec] * len(masks) + operand_specs,
        out_specs=[kv_spec] * len(masks) + out_specs,
        out_shape=[kv_shape] * len(masks) + out_shape,
        scratch_shapes=scratch,
        compiler_params=PARAMS,
        name="attend_back",
    )(info, *kvs, *operands)
    return (outs[: len(masks)], outs[len(masks) :])


RING = ("ctx", "tp")


def swap(value, mask):
    size = lax.axis_size(RING)
    return lax.ppermute(value, RING, [(i, i ^ mask) for i in range(size)])


def mirror(value):
    size = lax.axis_size(RING)
    return lax.ppermute(value, RING, [(i, size - 1 - i) for i in range(size)])


def mirror_odd(value):
    moved = mirror(value[1::2])
    seqs = value.shape[0]
    return jnp.concatenate(
        [moved[s // 2][None] if s % 2 else value[s][None] for s in range(seqs)], axis=0
    )


def move_back(value):
    moved = mirror(value[1::2].astype(bf16)).astype(f32)
    seqs = value.shape[0]
    return jnp.concatenate(
        [moved[s // 2][None] if s % 2 else value[s][None] for s in range(seqs)], axis=0
    )


def add_low(*parts):
    total = parts[0].astype(f32)
    for part in parts[1:]:
        total = total + part.astype(f32)
    return total.astype(bf16)


def gather_fsdp(value):
    if lax.axis_size("fsdp") != 2:
        return lax.all_gather(value, "fsdp", axis=0, tiled=False)
    other = lax.ppermute(value, "fsdp", [(0, 1), (1, 0)])
    at_zero = lax.axis_index("fsdp") == 0
    return jnp.stack([jnp.where(at_zero, value, other), jnp.where(at_zero, other, value)])


def pick_half(value, axis, index):
    half = value.shape[axis] // 2
    return lax.dynamic_slice_in_dim(value, index * half, half, axis)


def join_halves(mine, other, axis, index):
    return jnp.where(
        index == 0,
        jnp.concatenate([mine, other], axis=axis),
        jnp.concatenate([other, mine], axis=axis),
    )


def reduce_all(value, own):
    fsdp_size, rows, columns = value.shape
    outer = lax.axis_size(RING) // 4
    core = own % 2
    column = (own // 2) % 2
    plane = own // 4
    value = value.astype(bf16)
    value = add_low(pick_half(value, 2, core), swap(pick_half(value, 2, 1 - core), 1))
    if fsdp_size == 2:
        here = lax.axis_index("fsdp")
        away = lax.dynamic_index_in_dim(value, 1 - here, 0, False)
        mine = lax.dynamic_index_in_dim(value, here, 0, False)
        value = add_low(mine, lax.ppermute(away, "fsdp", [(0, 1), (1, 0)]))
    else:
        value = lax.psum_scatter(value, "fsdp", scatter_dimension=0, tiled=False)
    value = add_low(pick_half(value, 1, column), swap(pick_half(value, 1, 1 - column), 2))
    piece = rows // outer

    def rows_of(index):
        return lax.dynamic_slice_in_dim(value, index * piece, piece, 0)

    mine = add_low(
        rows_of(plane), *[swap(rows_of(plane ^ k), 4 * k) for k in range(1, outer)]
    )
    whole = jnp.zeros((rows, columns // 4), bf16)
    whole = lax.dynamic_update_slice_in_dim(whole, mine, plane * piece, 0)
    for k in range(1, outer):
        whole = lax.dynamic_update_slice_in_dim(whole, swap(mine, 4 * k), (plane ^ k) * piece, 0)
    whole = join_halves(whole, swap(whole, 2), 1, column)
    return join_halves(whole, swap(whole, 1), 1, core).astype(f32)


def sum_scalar(value):
    value = jnp.full((1, 128), value, f32)
    mask = 1
    while mask < lax.axis_size(RING):
        value = value + swap(value, mask)
        mask *= 2
    if lax.axis_size("fsdp") == 2:
        value = value + lax.ppermute(value, "fsdp", [(0, 1), (1, 0)])
    else:
        value = lax.psum(value, "fsdp")
    return value[0, 0]


def shards(
    tokens,
    teacher,
    lengths,
    gain_one,
    w_query,
    w_key,
    w_value,
    w_out,
    gain_two,
    w_gate,
    w_up,
    w_down,
):
    seqs, slots, width = tokens.shape
    rows = seqs * slots
    kv_width = KV_HEADS * HEAD_DIM
    qkv_width = width + 2 * kv_width
    gain_at = qkv_width
    pack_width = -(-(gain_at + 4) // 512) * 512
    half = w_query.shape[0]
    hidden_part = w_gate.shape[1]
    fsdp_size = lax.axis_size("fsdp")
    tp_size = lax.axis_size("tp")
    ring_size = lax.axis_size(RING)
    outer = ring_size // 4

    tokens_here = mirror_odd(tokens)
    valid_here = jnp.sum(lengths)
    length_cols = jnp.stack([valid_here // 128, valid_here % 128]).astype(bf16)
    packed = jnp.concatenate(
        [
            w_query,
            w_key,
            w_value,
            gain_one[:, None],
            gain_two[:, None],
            jnp.broadcast_to(length_cols[None], (half, 2)),
            jnp.zeros((half, pack_width - gain_at - 4), bf16),
        ],
        axis=1,
    )
    packed = gather_fsdp(packed)
    count_total = jnp.sum(
        packed[:, 0, gain_at + 2].astype(f32) * 128.0 + packed[:, 0, gain_at + 3].astype(f32)
    )
    packed = packed.reshape(width, pack_width)
    w_qkv = packed[:, :qkv_width]
    g_one = packed[:, gain_at].astype(f32)
    g_two = packed[:, gain_at + 1].astype(f32)
    ffn_pack = jnp.concatenate([w_gate, w_up, w_down.T], axis=1)
    ffn_all = lax.all_gather(ffn_pack, ("tp", "fsdp"), axis=0, tiled=False)
    ffn_all = ffn_all.reshape(tp_size, width, 3 * hidden_part)

    own = lax.axis_index(RING).astype(jnp.int32)
    blocks = jnp.stack([block_of(own, s, ring_size) for s in range(seqs)])
    positions = blocks[:, None] * slots + jnp.arange(slots, dtype=jnp.int32)[None]
    cosine, sine = rope_tables(positions)
    info = jnp.concatenate([lengths.astype(jnp.int32), own[None]])
    valid_mask = (positions < lengths[:, None]).astype(f32)

    inputs = tokens_here.astype(f32)
    normed = norm_rows(inputs, g_one).astype(bf16)
    qkv = jnp.einsum("df,sld->sfl", w_qkv, normed, preferred_element_type=f32)
    qk = qkv[:, : width + kv_width].reshape(seqs, HEADS + KV_HEADS, HEAD_DIM, slots)
    qk = rotate_cols(qk, cosine, sine).astype(bf16)
    queries = qk[:, :HEADS]
    values = qkv[:, width + kv_width :].astype(bf16).reshape(seqs, KV_HEADS, HEAD_DIM, slots)

    kv = {0: jnp.concatenate([qk[:, HEADS:], values], axis=2)}
    kv[1] = swap(kv[0], 1)
    for k in range(1, outer):
        kv[4 * k] = swap(kv[0], 4 * k)
    for k in range(outer):
        kv[4 * k + 2] = swap(kv[4 * k], 2)
    for k in range(outer):
        if k:
            kv[4 * k + 1] = swap(kv[4 * k], 1)
        kv[4 * k + 3] = swap(kv[4 * k + 2], 1)

    calls = [(0, 1)]
    for k in range(1, outer):
        calls.append((4 * k - 2, 4 * k - 1, 4 * k, 4 * k + 1))
    calls.append((4 * outer - 2, 4 * outer - 1))
    query_rows, *state = attend(ring_size, calls[0], info, queries, [kv[m] for m in calls[0]], None, False)
    for masks in calls[1:-1]:
        state = attend(ring_size, masks, info, query_rows, [kv[m] for m in masks], state, False)
    attended, lse = attend(
        ring_size, calls[-1], info, query_rows, [kv[m] for m in calls[-1]], state, True
    )
    attended_t = attended.reshape(seqs, width, slots)
    w_o = gather_fsdp(w_out).reshape(width, width)
    teacher_here = mirror_odd(teacher)

    middle = inputs + jnp.einsum("sfl,fd->sld", attended_t, w_o, preferred_element_type=f32)
    normed_two = norm_rows(middle, g_two).astype(bf16)
    flat_two = normed_two.reshape(rows, width)
    gate_up_w = ffn_all[:, :, : 2 * hidden_part]
    down_wt = ffn_all[:, :, 2 * hidden_part :]
    gate_up = jnp.einsum("rd,tdf->trf", flat_two, gate_up_w, preferred_element_type=f32)
    gate_pre = gate_up[..., :hidden_part]
    up_pre = gate_up[..., hidden_part:]
    gate_sigmoid = jax.nn.sigmoid(gate_pre)
    hidden = (gate_pre * gate_sigmoid * up_pre).astype(bf16)
    branch = jnp.einsum("trf,tdf->rd", hidden, down_wt, preferred_element_type=f32)
    result = middle + branch.reshape(seqs, slots, width)
    mismatch = result - teacher_here.astype(f32)
    squared_part = jnp.sum(valid_mask[..., None] * mismatch * mismatch)
    squared_total = sum_scalar(squared_part)
    loss_value = squared_total / (count_total * width)
    slots_all = seqs * fsdp_size * slots * ring_size
    d_result = valid_mask[..., None] * mismatch * (slots_all / count_total)
    d_branch = d_result.astype(bf16).reshape(rows, width)
    d_hidden = jnp.einsum("rd,tdf->trf", d_branch, down_wt, preferred_element_type=f32)
    d_down_wt = jnp.einsum("rd,trf->tdf", d_branch, hidden, preferred_element_type=f32)
    d_gate = (d_hidden * up_pre * gate_sigmoid * (1.0 + gate_pre * (1.0 - gate_sigmoid))).astype(bf16)
    d_up = (d_hidden * gate_pre * gate_sigmoid).astype(bf16)
    d_gate_up = jnp.concatenate([d_gate, d_up], axis=-1)
    d_gate_up_w = jnp.einsum("rd,trf->tdf", flat_two, d_gate_up, preferred_element_type=f32)
    d_normed_two = jnp.einsum("trf,tdf->rd", d_gate_up, gate_up_w, preferred_element_type=f32)
    norm_two_pull = jax.vjp(norm_rows, middle, g_two)[1]
    d_middle_norm, d_gain_two = norm_two_pull(d_normed_two.reshape(seqs, slots, width))
    d_middle = d_result + d_middle_norm
    d_attn_branch = d_middle.astype(bf16)
    d_attended_t = jnp.einsum("fd,sld->sfl", w_o, d_attn_branch, preferred_element_type=f32)
    d_attended_t = d_attended_t.astype(bf16).reshape(seqs, HEADS, HEAD_DIM, slots)
    d_out_w = jnp.einsum("sfl,sld->fd", attended_t, d_attn_branch, preferred_element_type=f32)

    output = move_back(result)
    d_kv_terms = []
    operands = [queries, d_attended_t, attended, lse]
    for k in reversed(range(outer)):
        masks = (4 * k, 4 * k + 1, 4 * k + 2, 4 * k + 3)
        first = k == outer - 1
        parts, outs = attend_back(
            ring_size, masks, info, [kv[m] for m in masks], operands, first, k == 0
        )
        if first:
            operands = [outs[1], outs[2], outs[0]]
        elif k:
            operands = operands[:2] + [outs[0]]
        near = add_low(parts[0], swap(parts[1], 1))
        away = swap(add_low(parts[2], swap(parts[3], 1)), 2)
        if k:
            d_kv_terms.append(swap(add_low(near, away), 4 * k))
        else:
            d_kv_terms += [near, away]
    d_query = outs[0]
    d_kv = sum(term.astype(f32) for term in d_kv_terms)

    d_ffn = jnp.concatenate([d_gate_up_w, d_down_wt], axis=-1).astype(bf16)
    d_ffn = d_ffn.reshape(tp_size * fsdp_size, half, 3 * hidden_part)
    d_ffn = lax.psum_scatter(d_ffn, ("tp", "fsdp"), scatter_dimension=0, tiled=False)
    d_ffn = lax.psum(d_ffn, "ctx").astype(f32)
    out_width = -(-width // 512) * 512
    d_out_w = jnp.pad(d_out_w, ((0, 0), (0, out_width - width))).reshape(fsdp_size, half, out_width)
    d_out_w = reduce_all(d_out_w, own)

    d_qk = jnp.concatenate([d_query, d_kv[:, :, :HEAD_DIM]], axis=1)
    d_qk = rotate_cols(d_qk, cosine, -sine).astype(bf16).reshape(seqs, width + kv_width, slots)
    d_values = d_kv[:, :, HEAD_DIM:].astype(bf16).reshape(seqs, kv_width, slots)
    d_qkv = jnp.concatenate([d_qk, d_values], axis=1)
    d_normed = jnp.einsum("sfl,df->sld", d_qkv, w_qkv, preferred_element_type=f32)
    d_qkv_w = jnp.einsum("sld,sfl->df", normed, d_qkv, preferred_element_type=f32)
    norm_one_pull = jax.vjp(norm_rows, inputs, g_one)[1]
    d_inputs_norm, d_gain_one = norm_one_pull(d_normed)
    tokens_grad = move_back(d_middle + d_inputs_norm)
    d_packed = jnp.concatenate(
        [
            d_qkv_w,
            d_gain_one[:, None],
            d_gain_two[:, None],
            jnp.zeros((width, pack_width - gain_at - 2), f32),
        ],
        axis=1,
    )
    d_packed = reduce_all(d_packed.reshape(fsdp_size, half, pack_width), own)
    return (
        output,
        loss_value,
        tokens_grad,
        d_packed[:, gain_at],
        d_packed[:, :width],
        d_packed[:, width : width + kv_width],
        d_packed[:, width + kv_width : qkv_width],
        d_out_w[:, :width],
        d_packed[:, gain_at + 1],
        d_ffn[:, :hidden_part],
        d_ffn[:, hidden_part : 2 * hidden_part],
        d_ffn[:, 2 * hidden_part :].T,
    )


def solution(mesh):
    slots_spec = P("fsdp", ("ctx", "tp"), None)
    rows_spec = P("fsdp", None)
    return jax.shard_map(
        shards,
        mesh=mesh,
        in_specs=(
            slots_spec,
            slots_spec,
            P("fsdp"),
            P("fsdp"),
            rows_spec,
            rows_spec,
            rows_spec,
            rows_spec,
            P("fsdp"),
            P("fsdp", "tp"),
            P("fsdp", "tp"),
            P("tp", "fsdp"),
        ),
        out_specs=(
            slots_spec,
            P(),
            slots_spec,
            P("fsdp"),
            rows_spec,
            rows_spec,
            rows_spec,
            rows_spec,
            P("fsdp"),
            P("fsdp", "tp"),
            P("fsdp", "tp"),
            P("tp", "fsdp"),
        ),
        check_vma=False,
    )
```

```python
import functools

import jax
import jax.numpy as jnp
from jax import lax
from jax.experimental import pallas as pl
from jax.experimental.pallas import tpu as pltpu
from jax.sharding import PartitionSpec as P

HEADS = 9
KV_HEADS = 3
GROUP = HEADS // KV_HEADS
HEAD_DIM = 64
AUG = HEAD_DIM + 16

EPS = 1e-05
ROPE_BASE = 10000.0
NEG = -1e30
LOG2E = 1.4426950408889634
EXP2_SCALE = LOG2E * HEAD_DIM ** (-0.5)

f32 = jnp.float32
bf16 = jnp.bfloat16
NN = ((1,), (0,))
TN = ((0,), (0,))
NT = ((1,), (1,))


def dot(left, right, dims):
    return lax.dot_general(left, right, (dims, ((), ())), preferred_element_type=f32)


def norm_rows(values, gain):
    return values * lax.rsqrt(jnp.mean(values * values, axis=-1, keepdims=True) + EPS) * gain


def rope_tables(positions):
    half_width = HEAD_DIM // 2
    frequency = ROPE_BASE ** (-(jnp.arange(half_width, dtype=f32) * 2.0) / HEAD_DIM)
    angles = frequency[None, None, :, None] * positions.astype(f32)[:, None, None, :]
    return (jnp.cos(angles), jnp.sin(angles))


def rotate_cols(values, cosine, sine):
    half_width = HEAD_DIM // 2
    lower = values[..., :half_width, :]
    upper = values[..., half_width:, :]
    return jnp.concatenate([lower * cosine - upper * sine, upper * cosine + lower * sine], axis=-2)


def three_pieces(row):
    first = row.astype(bf16)
    rest = row - first.astype(f32)
    second = rest.astype(bf16)
    third = (rest - second.astype(f32)).astype(bf16)
    return (first, second, third)


def penalty_row(block_start, width, length):
    key_pos = block_start + lax.broadcasted_iota(jnp.int32, (1, width), 1)
    return jnp.where(key_pos < length, 0.0, NEG).astype(bf16)


def extra_rows(rows, width):
    wide = jnp.zeros((16, width), f32)
    index = lax.broadcasted_iota(jnp.int32, (16, width), 0)
    for place, row in enumerate(rows):
        wide = jnp.where(index == place, row.astype(f32), wide)
    return wide.astype(bf16)


def block_of(device, seq, ring_size):
    return jnp.where(seq % 2 == 1, ring_size - 1 - device, device)


def forward_kernel(ring_size, masks, first, last, *refs):
    count = len(masks)
    info, q_ref = refs[:2]
    kv_refs = refs[2 : 2 + count]
    rest = refs[2 + count :]
    seq = pl.program_id(0)
    slots = kv_refs[0].shape[-1]
    cols = GROUP * slots
    if first:
        qa_ref, max_ref, acc_ref = rest
        qa_ref[0, 0, 0:HEAD_DIM] = jnp.concatenate([q_ref[0, h] for h in range(GROUP)], axis=1)
        qa_ref[0, 0, HEAD_DIM:AUG] = extra_rows([jnp.ones((1, cols), f32)], cols)
        max_ref[...] = jnp.full(max_ref.shape, NEG, f32)
        acc_ref[...] = jnp.zeros(acc_ref.shape, f32)
    else:
        qa_ref = q_ref
        if last:
            max_in, acc_in, out_ref, lse_ref, max_ref, acc_ref = rest
        else:
            max_in, acc_in, max_ref, acc_ref = rest
        max_ref[...] = max_in[...]
        acc_ref[...] = acc_in[...]
    device = info[info.shape[0] - 1]
    length = info[seq]
    own_block = block_of(device, seq, ring_size)

    def step(kv_ref, block, diagonal):
        key_cols = jnp.concatenate(
            [
                kv_ref[0, 0, 0:HEAD_DIM],
                extra_rows([penalty_row(block * slots, slots, length)], slots),
            ],
            axis=0,
        )
        value_ones = extra_rows([jnp.ones((1, slots), f32)], slots)
        value_cols = jnp.concatenate([kv_ref[0, 0, HEAD_DIM:], value_ones], axis=0)
        scores = dot(key_cols, qa_ref[0, 0], TN) * EXP2_SCALE
        if diagonal:
            key_at = lax.broadcasted_iota(jnp.int32, (slots, cols), 0)
            query_at = lax.broadcasted_iota(jnp.int32, (slots, cols), 1) % slots
            scores = jnp.where(key_at <= query_at, scores, NEG)
        old_max = max_ref[0, 0]
        new_max = jnp.maximum(old_max, jnp.max(scores, axis=0, keepdims=True))
        weights = jnp.exp2(scores - new_max).astype(bf16)
        max_ref[0, 0] = new_max
        acc_ref[0, 0] = acc_ref[0, 0] * jnp.exp2(old_max - new_max) + dot(value_cols, weights, NN)

    for kv_ref, mask in zip(kv_refs, masks):
        block = block_of(device ^ mask, seq, ring_size)
        below = block < own_block if mask else block == own_block

        @pl.when(below & (block * slots < length))
        def _():
            step(kv_ref, block, mask == 0)

    if last:
        total = acc_ref[0, 0, HEAD_DIM : HEAD_DIM + 1]
        heads_out = acc_ref[0, 0, 0:HEAD_DIM] / total
        lse_ref[0, 0] = (max_ref[0, 0] + jnp.log2(total)) * (1.0 / EXP2_SCALE)
        for h in range(GROUP):
            out_ref[0, h] = heads_out[:, h * slots : (h + 1) * slots].astype(bf16)


def backward_kernel(ring_size, masks, first, last, *refs):
    count = len(masks)
    info = refs[0]
    kv_refs = refs[1 : 1 + count]
    rest = refs[1 + count :]
    seq = pl.program_id(0)
    slots = kv_refs[0].shape[-1]
    cols = GROUP * slots
    if first:
        q_ref, do_ref, o_ref, lse_ref = rest[:4]
        dkv_refs = rest[4 : 4 + count]
        acc_ref, qa_ref, da_ref = rest[4 + count :]
        grads = jnp.concatenate([do_ref[0, h] for h in range(GROUP)], axis=1)
        heads_out = jnp.concatenate([o_ref[0, h] for h in range(GROUP)], axis=1)
        delta = jnp.sum(grads.astype(f32) * heads_out.astype(f32), axis=0, keepdims=True)
        qa_ref[0, 0, 0:HEAD_DIM] = jnp.concatenate([q_ref[0, h] for h in range(GROUP)], axis=1)
        qa_ref[0, 0, HEAD_DIM:AUG] = extra_rows(
            three_pieces(-lse_ref[0, 0]) + (jnp.ones((1, cols), f32),), cols
        )
        da_ref[0, 0, 0:HEAD_DIM] = grads
        da_ref[0, 0, HEAD_DIM:AUG] = extra_rows(three_pieces(-delta), cols)
        acc_ref[...] = jnp.zeros(acc_ref.shape, f32)
    else:
        qa_ref, da_ref, acc_in = rest[:3]
        dkv_refs = rest[3 : 3 + count]
        if last:
            dq_ref, acc_ref = rest[3 + count :]
        else:
            (acc_ref,) = rest[3 + count :]
        acc_ref[...] = acc_in[...]
    device = info[info.shape[0] - 1]
    length = info[seq]
    own_block = block_of(device, seq, ring_size)

    def step(kv_ref, dkv_ref, block, diagonal):
        ones_key = jnp.ones((1, slots), f32)
        keys = kv_ref[0, 0, 0:HEAD_DIM]
        key_cols = jnp.concatenate(
            [keys, extra_rows([ones_key] * 3 + [penalty_row(block * slots, slots, length)], slots)],
            axis=0,
        )
        value_cols = jnp.concatenate(
            [kv_ref[0, 0, HEAD_DIM:], extra_rows([ones_key] * 3, slots)], axis=0
        )
        scores = dot(qa_ref[0, 0], key_cols, TN) * EXP2_SCALE
        if diagonal:
            query_at = lax.broadcasted_iota(jnp.int32, (cols, slots), 0) % slots
            key_at = lax.broadcasted_iota(jnp.int32, (cols, slots), 1)
            scores = jnp.where(key_at <= query_at, scores, NEG)
        weights = jnp.exp2(scores)
        d_scores = (weights * dot(da_ref[0, 0], value_cols, TN)).astype(bf16)
        d_value = dot(da_ref[0, 0, 0:HEAD_DIM], weights.astype(bf16), NN)
        d_key = dot(qa_ref[0, 0, 0:HEAD_DIM], d_scores, NN) * (HEAD_DIM ** (-0.5))
        acc_ref[0, 0] += dot(keys, d_scores, NT)
        dkv_ref[0, 0, 0:HEAD_DIM] = d_key.astype(bf16)
        dkv_ref[0, 0, HEAD_DIM:] = d_value.astype(bf16)

    active = own_block * slots < length
    for kv_ref, dkv_ref, mask in zip(kv_refs, dkv_refs, masks):
        block = block_of(device ^ mask, seq, ring_size)
        run = active & (block < own_block if mask else block == own_block)

        @pl.when(run)
        def _():
            step(kv_ref, dkv_ref, block, mask == 0)

        @pl.when(jnp.logical_not(run))
        def _():
            dkv_ref[...] = jnp.zeros(dkv_ref.shape, bf16)

    if last:
        d_query = acc_ref[0, 0] * (HEAD_DIM ** (-0.5))
        for h in range(GROUP):
            dq_ref[0, h] = d_query[:, h * slots : (h + 1) * slots]


def head_spec(rows, lanes, heads=1):
    return pl.BlockSpec((1, heads, rows, lanes), lambda seq, group: (seq, group, 0, 0))


SMEM_SPEC = pl.BlockSpec(memory_space=pltpu.SMEM)
PARAMS = pltpu.CompilerParams(vmem_limit_bytes=60 * 2**20)


def call_cost(kv_shape, count, products):
    seqs, groups, _, slots = kv_shape
    pairs = seqs * groups * GROUP * slots * slots * count
    return pl.CostEstimate(
        flops=pairs * HEAD_DIM * products * 4,
        transcendentals=pairs,
        bytes_accessed=seqs * groups * count * 4 * HEAD_DIM * slots,
    )


def attend(ring_size, masks, info, queries, kvs, state, last):
    seqs, groups, _, slots = kvs[0].shape
    cols = GROUP * slots
    first = state is None
    kv_spec = head_spec(2 * HEAD_DIM, slots)
    wide_spec = head_spec(AUG, cols)
    row_spec = head_spec(1, cols)
    wide_shape = (seqs, groups, AUG, cols)
    row_shape = jax.ShapeDtypeStruct((seqs, groups, 1, cols), f32)
    state_specs = [row_spec, wide_spec]
    state_shapes = [row_shape, jax.ShapeDtypeStruct(wide_shape, f32)]
    query_spec = wide_spec
    scratch = []
    if first:
        query_spec = head_spec(HEAD_DIM, slots, GROUP)
        out_specs = [wide_spec] + state_specs
        out_shape = [jax.ShapeDtypeStruct(wide_shape, bf16)] + state_shapes
    elif last:
        out_specs = [head_spec(HEAD_DIM, slots, GROUP), row_spec]
        out_shape = [jax.ShapeDtypeStruct((seqs, groups * GROUP, HEAD_DIM, slots), bf16), row_shape]
        scratch = [pltpu.VMEM((1, 1, 1, cols), f32), pltpu.VMEM((1, 1, AUG, cols), f32)]
    else:
        out_specs = state_specs
        out_shape = state_shapes
    return pl.pallas_call(
        functools.partial(forward_kernel, ring_size, masks, first, last),
        grid=(seqs, groups),
        in_specs=[SMEM_SPEC, query_spec]
        + [kv_spec] * len(masks)
        + ([] if first else state_specs),
        out_specs=out_specs,
        out_shape=out_shape,
        scratch_shapes=scratch,
        compiler_params=PARAMS,
        cost_estimate=call_cost(kvs[0].shape, len(masks), 4),
        name="attend",
    )(info, queries, *kvs, *([] if first else state))


def attend_back(ring_size, masks, info, kvs, operands, first, last):
    seqs, groups, _, slots = kvs[0].shape
    cols = GROUP * slots
    kv_spec = head_spec(2 * HEAD_DIM, slots)
    heads_spec = head_spec(HEAD_DIM, slots, GROUP)
    wide_spec = head_spec(AUG, cols)
    acc_spec = head_spec(HEAD_DIM, cols)
    kv_shape = jax.ShapeDtypeStruct(kvs[0].shape, bf16)
    wide_shape = jax.ShapeDtypeStruct((seqs, groups, AUG, cols), bf16)
    acc_shape = jax.ShapeDtypeStruct((seqs, groups, HEAD_DIM, cols), f32)
    scratch = []
    if first:
        operand_specs = [heads_spec] * 3 + [head_spec(1, cols)]
        out_specs = [acc_spec, wide_spec, wide_spec]
        out_shape = [acc_shape, wide_shape, wide_shape]
    else:
        operand_specs = [wide_spec, wide_spec, acc_spec]
        if last:
            out_specs = [heads_spec]
            out_shape = [jax.ShapeDtypeStruct((seqs, groups * GROUP, HEAD_DIM, slots), f32)]
            scratch = [pltpu.VMEM((1, 1, HEAD_DIM, cols), f32)]
        else:
            out_specs = [acc_spec]
            out_shape = [acc_shape]
    outs = pl.pallas_call(
        functools.partial(backward_kernel, ring_size, masks, first, last),
        grid=(seqs, groups),
        in_specs=[SMEM_SPEC] + [kv_spec] * len(masks) + operand_specs,
        out_specs=[kv_spec] * len(masks) + out_specs,
        out_shape=[kv_shape] * len(masks) + out_shape,
        scratch_shapes=scratch,
        compiler_params=PARAMS,
        cost_estimate=call_cost(kvs[0].shape, len(masks), 10),
        name="attend_back",
    )(info, *kvs, *operands)
    return (outs[: len(masks)], outs[len(masks) :])


RING = ("ctx", "tp")


def swap(value, mask):
    size = lax.axis_size(RING)
    return lax.ppermute(value, RING, [(i, i ^ mask) for i in range(size)])


def mirror(value):
    size = lax.axis_size(RING)
    return lax.ppermute(value, RING, [(i, size - 1 - i) for i in range(size)])


def mirror_odd(value):
    moved = mirror(value[1::2])
    seqs = value.shape[0]
    return jnp.concatenate(
        [moved[s // 2][None] if s % 2 else value[s][None] for s in range(seqs)], axis=0
    )


def move_back(value):
    moved = mirror(value[1::2].astype(bf16)).astype(f32)
    seqs = value.shape[0]
    return jnp.concatenate(
        [moved[s // 2][None] if s % 2 else value[s][None] for s in range(seqs)], axis=0
    )


def add_low(*parts):
    total = parts[0].astype(f32)
    for part in parts[1:]:
        total = total + part.astype(f32)
    return total.astype(bf16)


def gather_fsdp(value):
    if lax.axis_size("fsdp") != 2:
        return lax.all_gather(value, "fsdp", axis=0, tiled=False)
    other = lax.ppermute(value, "fsdp", [(0, 1), (1, 0)])
    at_zero = lax.axis_index("fsdp") == 0
    return jnp.stack([jnp.where(at_zero, value, other), jnp.where(at_zero, other, value)])


def pick_half(value, axis, index):
    half = value.shape[axis] // 2
    return lax.dynamic_slice_in_dim(value, index * half, half, axis)


def join_halves(mine, other, axis, index):
    return jnp.where(
        index == 0,
        jnp.concatenate([mine, other], axis=axis),
        jnp.concatenate([other, mine], axis=axis),
    )


def reduce_steps(value, own):
    fsdp_size, rows, columns = value.shape
    outer = lax.axis_size(RING) // 4
    core = own % 2
    column = (own // 2) % 2
    plane = own // 4
    value = value.astype(bf16)
    value = add_low(pick_half(value, 2, core), swap(pick_half(value, 2, 1 - core), 1))
    value = yield value
    if fsdp_size == 2:
        here = lax.axis_index("fsdp")
        away = lax.dynamic_index_in_dim(value, 1 - here, 0, False)
        mine = lax.dynamic_index_in_dim(value, here, 0, False)
        value = add_low(mine, lax.ppermute(away, "fsdp", [(0, 1), (1, 0)]))
    else:
        value = lax.psum_scatter(value, "fsdp", scatter_dimension=0, tiled=False)
    value = yield value
    value = add_low(pick_half(value, 1, column), swap(pick_half(value, 1, 1 - column), 2))
    value = yield value
    piece = rows // outer

    def rows_of(index):
        return lax.dynamic_slice_in_dim(value, index * piece, piece, 0)

    mine = add_low(
        rows_of(plane), *[swap(rows_of(plane ^ k), 4 * k) for k in range(1, outer)]
    )
    mine = yield mine
    whole = jnp.zeros((rows, columns // 4), bf16)
    whole = lax.dynamic_update_slice_in_dim(whole, mine, plane * piece, 0)
    for k in range(1, outer):
        whole = lax.dynamic_update_slice_in_dim(whole, swap(mine, 4 * k), (plane ^ k) * piece, 0)
    whole = yield whole
    whole = join_halves(whole, swap(whole, 2), 1, column)
    whole = yield whole
    yield join_halves(whole, swap(whole, 1), 1, core).astype(f32)


def sum_steps(value):
    value = jnp.full((1, 128), value, f32)
    mask = 1
    while mask < lax.axis_size(RING):
        value = yield value + swap(value, mask)
        mask *= 2
    if lax.axis_size("fsdp") == 2:
        value = value + lax.ppermute(value, "fsdp", [(0, 1), (1, 0)])
    else:
        value = lax.psum(value, "fsdp")
    yield value


def advance(steps, value):
    try:
        return steps.send(value)
    except StopIteration:
        return value


def run_steps(steps, value=None):
    while True:
        try:
            value = steps.send(value)
        except StopIteration:
            return value


def shards(
    tokens,
    teacher,
    lengths,
    gain_one,
    w_query,
    w_key,
    w_value,
    w_out,
    gain_two,
    w_gate,
    w_up,
    w_down,
):
    seqs, slots, width = tokens.shape
    rows = seqs * slots
    kv_width = KV_HEADS * HEAD_DIM
    qkv_width = width + 2 * kv_width
    out_at = -(-qkv_width // 128) * 128
    gain_at = out_at + width
    pack_width = -(-(gain_at + 4) // 128) * 128
    grad_width = -(-(qkv_width + 2) // 512) * 512
    half = w_query.shape[0]
    hidden_part = w_gate.shape[1]
    fsdp_size = lax.axis_size("fsdp")
    tp_size = lax.axis_size("tp")
    ring_size = lax.axis_size(RING)
    outer = ring_size // 4

    tokens_here = mirror_odd(tokens)
    valid_here = jnp.sum(lengths)
    length_cols = jnp.stack([valid_here // 128, valid_here % 128]).astype(bf16)
    packed = jnp.concatenate(
        [
            w_query,
            w_key,
            w_value,
            jnp.zeros((half, out_at - qkv_width), bf16),
            w_out,
            gain_one[:, None],
            gain_two[:, None],
            jnp.broadcast_to(length_cols[None], (half, 2)),
            jnp.zeros((half, pack_width - gain_at - 4), bf16),
        ],
        axis=1,
    )
    packed = gather_fsdp(packed)
    count_total = jnp.sum(
        packed[:, 0, gain_at + 2].astype(f32) * 128.0 + packed[:, 0, gain_at + 3].astype(f32)
    )
    packed = packed.reshape(width, pack_width)
    w_qkv = packed[:, :qkv_width]
    w_o = packed[:, out_at:gain_at]
    g_one = packed[:, gain_at].astype(f32)
    g_two = packed[:, gain_at + 1].astype(f32)
    ffn_pack = jnp.concatenate([w_gate, w_up, w_down.T], axis=1)
    ffn_all = lax.all_gather(ffn_pack, ("tp", "fsdp"), axis=0, tiled=False)
    ffn_all = ffn_all.reshape(tp_size, width, 3 * hidden_part)

    own = lax.axis_index(RING).astype(jnp.int32)
    blocks = jnp.stack([block_of(own, s, ring_size) for s in range(seqs)])
    positions = blocks[:, None] * slots + jnp.arange(slots, dtype=jnp.int32)[None]
    cosine, sine = rope_tables(positions)
    info = jnp.concatenate([lengths.astype(jnp.int32), own[None]])
    valid_mask = (positions < lengths[:, None]).astype(f32)

    inputs = tokens_here.astype(f32)
    normed = norm_rows(inputs, g_one).astype(bf16)
    qkv = jnp.einsum("df,sld->sfl", w_qkv, normed, preferred_element_type=f32)
    qk = qkv[:, : width + kv_width].reshape(seqs, HEADS + KV_HEADS, HEAD_DIM, slots)
    qk = rotate_cols(qk, cosine, sine).astype(bf16)
    queries = qk[:, :HEADS]
    values = qkv[:, width + kv_width :].astype(bf16).reshape(seqs, KV_HEADS, HEAD_DIM, slots)

    kv = {0: jnp.concatenate([qk[:, HEADS:], values], axis=2)}
    coming = {1: swap(kv[0], 1), 2: swap(kv[0], 2)}
    for k in range(1, outer):
        coming[4 * k] = swap(kv[0], 4 * k)
    calls = [(0,), (1, 2, 4)]
    for k in range(1, outer - 1):
        calls.append((4 * k - 1, 4 * k + 1, 4 * k + 2, 4 * k + 4))
    calls.append((4 * outer - 5, 4 * outer - 3, 4 * outer - 2, 4 * outer - 1))
    query_rows, *state = attend(ring_size, calls[0], info, queries, [kv[0]], None, False)
    for number, masks in enumerate(calls[1:], 1):
        if masks[-1] not in coming:
            coming[masks[-1]] = swap(coming[masks[-1] - 1], 1)
        *arrived, first_state = lax.optimization_barrier([coming[m] for m in masks] + [state[0]])
        kv.update(zip(masks, arrived))
        state = [first_state, state[1]]
        for mask in masks:
            if mask % 4 == 0:
                coming[mask + 2] = swap(kv[mask], 2)
                coming[mask + 1] = swap(kv[mask], 1)
            elif mask % 4 == 2 and mask + 1 not in coming:
                coming[mask + 1] = swap(kv[mask], 1)
        state = attend(
            ring_size, masks, info, query_rows, arrived, state, number == len(calls) - 1
        )
    attended, lse = state
    attended_t = attended.reshape(seqs, width, slots)
    teacher_here = mirror_odd(teacher)

    middle = inputs + jnp.einsum("sfl,fd->sld", attended_t, w_o, preferred_element_type=f32)
    normed_two = norm_rows(middle, g_two).astype(bf16)
    flat_two = normed_two.reshape(rows, width)
    gate_up_w = ffn_all[:, :, : 2 * hidden_part]
    down_wt = ffn_all[:, :, 2 * hidden_part :]
    gate_up = jnp.einsum("rd,tdf->trf", flat_two, gate_up_w, preferred_element_type=f32)
    gate_pre = gate_up[..., :hidden_part]
    up_pre = gate_up[..., hidden_part:]
    gate_sigmoid = jax.nn.sigmoid(gate_pre)
    hidden = (gate_pre * gate_sigmoid * up_pre).astype(bf16)
    branch = jnp.einsum("trf,tdf->rd", hidden, down_wt, preferred_element_type=f32)
    result = middle + branch.reshape(seqs, slots, width)
    mismatch = result - teacher_here.astype(f32)
    squared_part = jnp.sum(valid_mask[..., None] * mismatch * mismatch)
    slots_all = seqs * fsdp_size * slots * ring_size
    d_result = valid_mask[..., None] * mismatch * (slots_all / count_total)
    d_branch = d_result.astype(bf16).reshape(rows, width)
    d_hidden = jnp.einsum("rd,tdf->trf", d_branch, down_wt, preferred_element_type=f32)
    d_down_wt = jnp.einsum("rd,trf->tdf", d_branch, hidden, preferred_element_type=f32)
    d_gate = (d_hidden * up_pre * gate_sigmoid * (1.0 + gate_pre * (1.0 - gate_sigmoid))).astype(bf16)
    d_up = (d_hidden * gate_pre * gate_sigmoid).astype(bf16)
    d_gate_up = jnp.concatenate([d_gate, d_up], axis=-1)
    d_gate_up_w = jnp.einsum("rd,trf->tdf", flat_two, d_gate_up, preferred_element_type=f32)
    d_normed_two = jnp.einsum("trf,tdf->rd", d_gate_up, gate_up_w, preferred_element_type=f32)
    norm_two_pull = jax.vjp(norm_rows, middle, g_two)[1]
    d_middle_norm, d_gain_two = norm_two_pull(d_normed_two.reshape(seqs, slots, width))
    d_middle = d_result + d_middle_norm
    d_attn_branch = d_middle.astype(bf16)
    d_attended_t = jnp.einsum("fd,sld->sfl", w_o, d_attn_branch, preferred_element_type=f32)
    d_attended_t = d_attended_t.astype(bf16).reshape(seqs, HEADS, HEAD_DIM, slots)
    d_out_w = jnp.einsum("sfl,sld->fd", attended_t, d_attn_branch, preferred_element_type=f32)

    d_ffn = jnp.concatenate([d_gate_up_w, d_down_wt], axis=-1).astype(bf16)
    d_ffn = d_ffn.reshape(tp_size * fsdp_size, half, 3 * hidden_part)
    d_ffn = lax.psum_scatter(d_ffn, ("tp", "fsdp"), scatter_dimension=0, tiled=False)
    out_width = -(-width // 512) * 512
    d_out_w = jnp.pad(d_out_w, ((0, 0), (0, out_width - width))).reshape(fsdp_size, half, out_width)
    output = move_back(result)
    out_steps = reduce_steps(d_out_w, own)
    loss_steps = sum_steps(squared_part)
    d_out_w = next(out_steps)
    loss_sum = next(loss_steps)

    calls = [(4 * outer - 2, 4 * outer - 1)]
    for k in reversed(range(1, outer)):
        calls.append((4 * k, 4 * k + 1, 4 * k - 2, 4 * k - 1))
    calls.append((0, 1))
    operands = [queries, d_attended_t, attended, lse]
    core_sums = {}
    sums = {}
    d_kv_terms = []
    for number, masks in enumerate(calls):
        last = number == len(calls) - 1
        if number:
            if number >= 2:
                due = list(calls[number - 2][::2])
            else:
                due = []
            held = [core_sums[m] for m in due] + [d_out_w, loss_sum]
            if number == 2:
                held.append(output)
            if number == 3:
                held.append(d_ffn)
            held = list(lax.optimization_barrier([info] + held))
            info = held.pop(0)
            if number == 3:
                d_ffn = lax.psum(held.pop(), "ctx")
            if number == 2:
                output = held.pop()
            loss_sum = advance(loss_steps, held.pop())
            d_out_w = advance(out_steps, held.pop())
            for mask, value in zip(due, held):
                core_sums[mask] = value
                if mask % 4:
                    sums[mask - 2] = swap(value, 2)
                else:
                    d_kv_terms.append(swap(add_low(value, sums[mask]), mask))
        parts, outs = attend_back(
            ring_size, masks, info, [kv[m] for m in masks], operands, number == 0, last
        )
        for place in range(0, len(masks), 2):
            core_sums[masks[place]] = add_low(parts[place], swap(parts[place + 1], 1))
        if number == 0:
            operands = [outs[1], outs[2], outs[0]]
        else:
            operands = operands[:2] + [outs[0]]
    d_query = outs[0]
    for mask in calls[-2][::2] + calls[-1][::2]:
        if mask % 4:
            sums[mask - 2] = swap(core_sums[mask], 2)
        elif mask:
            d_kv_terms.append(swap(add_low(core_sums[mask], sums[mask]), mask))
    d_kv_terms += [core_sums[0], sums[0]]
    d_kv = sum(term.astype(f32) for term in d_kv_terms)
    loss_sum = run_steps(loss_steps, loss_sum)
    loss_value = loss_sum[0, 0] / (count_total * width)
    d_out_w = run_steps(out_steps, d_out_w)
    d_ffn = d_ffn.astype(f32)

    d_qk = jnp.concatenate([d_query, d_kv[:, :, :HEAD_DIM]], axis=1)
    d_qk = rotate_cols(d_qk, cosine, -sine).astype(bf16).reshape(seqs, width + kv_width, slots)
    d_values = d_kv[:, :, HEAD_DIM:].astype(bf16).reshape(seqs, kv_width, slots)
    d_qkv = jnp.concatenate([d_qk, d_values], axis=1)
    d_normed = jnp.einsum("sfl,df->sld", d_qkv, w_qkv, preferred_element_type=f32)
    d_qkv_w = jnp.einsum("sld,sfl->df", normed, d_qkv, preferred_element_type=f32)
    norm_one_pull = jax.vjp(norm_rows, inputs, g_one)[1]
    d_inputs_norm, d_gain_one = norm_one_pull(d_normed)
    tokens_grad = move_back(d_middle + d_inputs_norm)
    d_packed = jnp.concatenate(
        [
            d_qkv_w,
            d_gain_one[:, None],
            d_gain_two[:, None],
            jnp.zeros((width, grad_width - qkv_width - 2), f32),
        ],
        axis=1,
    )
    d_packed = run_steps(reduce_steps(d_packed.reshape(fsdp_size, half, grad_width), own))
    return (
        output,
        loss_value,
        tokens_grad,
        d_packed[:, qkv_width],
        d_packed[:, :width],
        d_packed[:, width : width + kv_width],
        d_packed[:, width + kv_width : qkv_width],
        d_out_w[:, :width],
        d_packed[:, qkv_width + 1],
        d_ffn[:, :hidden_part],
        d_ffn[:, hidden_part : 2 * hidden_part],
        d_ffn[:, 2 * hidden_part :].T,
    )


def solution(mesh):
    slots_spec = P("fsdp", ("ctx", "tp"), None)
    rows_spec = P("fsdp", None)
    return jax.shard_map(
        shards,
        mesh=mesh,
        in_specs=(
            slots_spec,
            slots_spec,
            P("fsdp"),
            P("fsdp"),
            rows_spec,
            rows_spec,
            rows_spec,
            rows_spec,
            P("fsdp"),
            P("fsdp", "tp"),
            P("fsdp", "tp"),
            P("tp", "fsdp"),
        ),
        out_specs=(
            slots_spec,
            P(),
            slots_spec,
            P("fsdp"),
            rows_spec,
            rows_spec,
            rows_spec,
            rows_spec,
            P("fsdp"),
            P("fsdp", "tp"),
            P("fsdp", "tp"),
            P("tp", "fsdp"),
        ),
        check_vma=False,
    )
```

```python
import functools

import jax
import jax.numpy as jnp
from jax import lax
from jax.experimental import pallas as pl
from jax.experimental.pallas import tpu as pltpu
from jax.sharding import PartitionSpec as P

HEADS = 9
KV_HEADS = 3
GROUP = HEADS // KV_HEADS
HEAD_DIM = 64
AUG = HEAD_DIM + 16

EPS = 1e-05
ROPE_BASE = 10000.0
NEG = -1e30
LOG2E = 1.4426950408889634
EXP2_SCALE = LOG2E * HEAD_DIM ** (-0.5)

f32 = jnp.float32
bf16 = jnp.bfloat16
NN = ((1,), (0,))
TN = ((0,), (0,))
NT = ((1,), (1,))


def dot(left, right, dims):
    return lax.dot_general(left, right, (dims, ((), ())), preferred_element_type=f32)


def norm_rows(values, gain):
    return values * lax.rsqrt(jnp.mean(values * values, axis=-1, keepdims=True) + EPS) * gain


def rope_tables(positions):
    half_width = HEAD_DIM // 2
    frequency = ROPE_BASE ** (-(jnp.arange(half_width, dtype=f32) * 2.0) / HEAD_DIM)
    angles = frequency[None, None, :, None] * positions.astype(f32)[:, None, None, :]
    return (jnp.cos(angles), jnp.sin(angles))


def rotate_cols(values, cosine, sine):
    half_width = HEAD_DIM // 2
    lower = values[..., :half_width, :]
    upper = values[..., half_width:, :]
    return jnp.concatenate([lower * cosine - upper * sine, upper * cosine + lower * sine], axis=-2)


def three_pieces(row):
    first = row.astype(bf16)
    rest = row - first.astype(f32)
    second = rest.astype(bf16)
    third = (rest - second.astype(f32)).astype(bf16)
    return (first, second, third)


def penalty_row(block_start, width, length):
    key_pos = block_start + lax.broadcasted_iota(jnp.int32, (1, width), 1)
    return jnp.where(key_pos < length, 0.0, NEG).astype(bf16)


def extra_rows(rows, width):
    wide = jnp.zeros((16, width), f32)
    index = lax.broadcasted_iota(jnp.int32, (16, width), 0)
    for place, row in enumerate(rows):
        wide = jnp.where(index == place, row.astype(f32), wide)
    return wide.astype(bf16)


def block_of(device, seq, ring_size):
    return jnp.where(seq % 2 == 1, ring_size - 1 - device, device)


def needed(device, mask, seq):
    if mask == 0:
        return seq >= 0
    return (device ^ mask > device) == (seq % 2 == 1)


def forward_kernel(ring_size, masks, first, last, *refs):
    count = len(masks)
    info, q_ref = refs[:2]
    kv_refs = refs[2 : 2 + count]
    rest = refs[2 + count :]
    seq = pl.program_id(1)
    slots = kv_refs[0].shape[-1]
    cols = GROUP * slots
    if first:
        qa_ref, max_ref, acc_ref = rest
        qa_ref[0, 0, 0:HEAD_DIM] = jnp.concatenate([q_ref[0, h] for h in range(GROUP)], axis=1)
        qa_ref[0, 0, HEAD_DIM:AUG] = extra_rows([jnp.ones((1, cols), f32)], cols)
        max_ref[...] = jnp.full(max_ref.shape, NEG, f32)
        acc_ref[...] = jnp.zeros(acc_ref.shape, f32)
    else:
        qa_ref = q_ref
        if last:
            max_in, acc_in, out_ref, lse_ref, max_ref, acc_ref = rest
        else:
            max_in, acc_in, max_ref, acc_ref = rest
        max_ref[...] = max_in[...]
        acc_ref[...] = acc_in[...]
    device = info[info.shape[0] - 1]
    length = info[seq]
    own_block = block_of(device, seq, ring_size)

    def step(kv_ref, block, diagonal):
        key_cols = jnp.concatenate(
            [
                kv_ref[0, 0, 0:HEAD_DIM],
                extra_rows([penalty_row(block * slots, slots, length)], slots),
            ],
            axis=0,
        )
        value_ones = extra_rows([jnp.ones((1, slots), f32)], slots)
        value_cols = jnp.concatenate([kv_ref[0, 0, HEAD_DIM:], value_ones], axis=0)
        scores = dot(key_cols, qa_ref[0, 0], TN) * EXP2_SCALE
        if diagonal:
            key_at = lax.broadcasted_iota(jnp.int32, (slots, cols), 0)
            query_at = lax.broadcasted_iota(jnp.int32, (slots, cols), 1) % slots
            scores = jnp.where(key_at <= query_at, scores, NEG)
        old_max = max_ref[0, 0]
        new_max = jnp.maximum(old_max, jnp.max(scores, axis=0, keepdims=True))
        weights = jnp.exp2(scores - new_max).astype(bf16)
        max_ref[0, 0] = new_max
        acc_ref[0, 0] = acc_ref[0, 0] * jnp.exp2(old_max - new_max) + dot(value_cols, weights, NN)

    for kv_ref, mask in zip(kv_refs, masks):
        block = block_of(device ^ mask, seq, ring_size)

        @pl.when(needed(device, mask, seq) & (block * slots < length))
        def _():
            step(kv_ref, block, mask == 0)

    if last:
        total = acc_ref[0, 0, HEAD_DIM : HEAD_DIM + 1]
        heads_out = acc_ref[0, 0, 0:HEAD_DIM] / total
        lse_ref[0, 0] = (max_ref[0, 0] + jnp.log2(total)) * (1.0 / EXP2_SCALE)
        for h in range(GROUP):
            out_ref[0, h] = heads_out[:, h * slots : (h + 1) * slots].astype(bf16)


def backward_kernel(ring_size, masks, first, last, *refs):
    count = len(masks)
    info = refs[0]
    kv_refs = refs[1 : 1 + count]
    rest = refs[1 + count :]
    seq = pl.program_id(1)
    slots = kv_refs[0].shape[-1]
    cols = GROUP * slots
    if first:
        q_ref, do_ref, o_ref, lse_ref = rest[:4]
        dkv_refs = rest[4 : 4 + count]
        acc_ref, qa_ref, da_ref = rest[4 + count :]
        grads = jnp.concatenate([do_ref[0, h] for h in range(GROUP)], axis=1)
        heads_out = jnp.concatenate([o_ref[0, h] for h in range(GROUP)], axis=1)
        delta = jnp.sum(grads.astype(f32) * heads_out.astype(f32), axis=0, keepdims=True)
        qa_ref[0, 0, 0:HEAD_DIM] = jnp.concatenate([q_ref[0, h] for h in range(GROUP)], axis=1)
        qa_ref[0, 0, HEAD_DIM:AUG] = extra_rows(
            three_pieces(-lse_ref[0, 0]) + (jnp.ones((1, cols), f32),), cols
        )
        da_ref[0, 0, 0:HEAD_DIM] = grads
        da_ref[0, 0, HEAD_DIM:AUG] = extra_rows(three_pieces(-delta), cols)
        acc_ref[...] = jnp.zeros(acc_ref.shape, f32)
    else:
        qa_ref, da_ref, acc_in = rest[:3]
        dkv_refs = rest[3 : 3 + count]
        if last:
            dq_ref, acc_ref = rest[3 + count :]
        else:
            (acc_ref,) = rest[3 + count :]
        acc_ref[...] = acc_in[...]
    device = info[info.shape[0] - 1]
    length = info[seq]
    own_block = block_of(device, seq, ring_size)

    def step(kv_ref, dkv_ref, block, diagonal):
        ones_key = jnp.ones((1, slots), f32)
        keys = kv_ref[0, 0, 0:HEAD_DIM]
        key_cols = jnp.concatenate(
            [keys, extra_rows([ones_key] * 3 + [penalty_row(block * slots, slots, length)], slots)],
            axis=0,
        )
        value_cols = jnp.concatenate(
            [kv_ref[0, 0, HEAD_DIM:], extra_rows([ones_key] * 3, slots)], axis=0
        )
        scores = dot(qa_ref[0, 0], key_cols, TN) * EXP2_SCALE
        if diagonal:
            query_at = lax.broadcasted_iota(jnp.int32, (cols, slots), 0) % slots
            key_at = lax.broadcasted_iota(jnp.int32, (cols, slots), 1)
            scores = jnp.where(key_at <= query_at, scores, NEG)
        weights = jnp.exp2(scores)
        d_scores = (weights * dot(da_ref[0, 0], value_cols, TN)).astype(bf16)
        d_value = dot(da_ref[0, 0, 0:HEAD_DIM], weights.astype(bf16), NN)
        d_key = dot(qa_ref[0, 0, 0:HEAD_DIM], d_scores, NN) * (HEAD_DIM ** (-0.5))
        acc_ref[0, 0] += dot(keys, d_scores, NT)
        dkv_ref[0, 0, 0:HEAD_DIM] = d_key.astype(bf16)
        dkv_ref[0, 0, HEAD_DIM:] = d_value.astype(bf16)

    active = own_block * slots < length
    for kv_ref, dkv_ref, mask in zip(kv_refs, dkv_refs, masks):
        block = block_of(device ^ mask, seq, ring_size)
        turn = needed(device, mask, seq)

        @pl.when(turn & active)
        def _():
            step(kv_ref, dkv_ref, block, mask == 0)

        @pl.when(turn & jnp.logical_not(active))
        def _():
            dkv_ref[...] = jnp.zeros(dkv_ref.shape, bf16)

    if last:
        d_query = acc_ref[0, 0] * (HEAD_DIM ** (-0.5))
        for h in range(GROUP):
            dq_ref[0, h] = d_query[:, h * slots : (h + 1) * slots]


def head_spec(rows, lanes, heads=1):
    return pl.BlockSpec((1, heads, rows, lanes), lambda group, seq: (seq, group, 0, 0))


def kv_specs(masks, slots):
    half = pl.BlockSpec((1, 1, 2 * HEAD_DIM, slots), lambda group, seq: (seq // 2, group, 0, 0))
    return [half if mask else head_spec(2 * HEAD_DIM, slots) for mask in masks]


SMEM_SPEC = pl.BlockSpec(memory_space=pltpu.SMEM)
PARAMS = pltpu.CompilerParams(vmem_limit_bytes=60 * 2**20)


def call_cost(kv_shape, count, products):
    seqs, groups, _, slots = kv_shape
    pairs = seqs * groups * GROUP * slots * slots * count
    return pl.CostEstimate(
        flops=pairs * HEAD_DIM * products * 4,
        transcendentals=pairs,
        bytes_accessed=seqs * groups * count * 4 * HEAD_DIM * slots,
    )


def attend(ring_size, masks, info, queries, kvs, state, last):
    first = state is None
    groups, slots = kvs[0].shape[1], kvs[0].shape[3]
    seqs = queries.shape[0]
    cols = GROUP * slots
    wide_spec = head_spec(AUG, cols)
    row_spec = head_spec(1, cols)
    wide_shape = (seqs, groups, AUG, cols)
    row_shape = jax.ShapeDtypeStruct((seqs, groups, 1, cols), f32)
    state_specs = [row_spec, wide_spec]
    state_shapes = [row_shape, jax.ShapeDtypeStruct(wide_shape, f32)]
    query_spec = wide_spec
    scratch = []
    if first:
        query_spec = head_spec(HEAD_DIM, slots, GROUP)
        out_specs = [wide_spec] + state_specs
        out_shape = [jax.ShapeDtypeStruct(wide_shape, bf16)] + state_shapes
    elif last:
        out_specs = [head_spec(HEAD_DIM, slots, GROUP), row_spec]
        out_shape = [jax.ShapeDtypeStruct((seqs, groups * GROUP, HEAD_DIM, slots), bf16), row_shape]
        scratch = [pltpu.VMEM((1, 1, 1, cols), f32), pltpu.VMEM((1, 1, AUG, cols), f32)]
    else:
        out_specs = state_specs
        out_shape = state_shapes
    return pl.pallas_call(
        functools.partial(forward_kernel, ring_size, masks, first, last),
        grid=(groups, seqs),
        in_specs=[SMEM_SPEC, query_spec]
        + kv_specs(masks, slots)
        + ([] if first else state_specs),
        out_specs=out_specs,
        out_shape=out_shape,
        scratch_shapes=scratch,
        compiler_params=PARAMS,
        cost_estimate=call_cost(kvs[0].shape, len(masks), 4),
        name="attend",
    )(info, queries, *kvs, *([] if first else state))


def attend_back(ring_size, masks, info, kvs, operands, first, last):
    groups, slots = kvs[0].shape[1], kvs[0].shape[3]
    seqs = operands[0].shape[0]
    cols = GROUP * slots
    heads_spec = head_spec(HEAD_DIM, slots, GROUP)
    wide_spec = head_spec(AUG, cols)
    acc_spec = head_spec(HEAD_DIM, cols)
    kv_shapes = [jax.ShapeDtypeStruct(kv.shape, bf16) for kv in kvs]
    wide_shape = jax.ShapeDtypeStruct((seqs, groups, AUG, cols), bf16)
    acc_shape = jax.ShapeDtypeStruct((seqs, groups, HEAD_DIM, cols), f32)
    scratch = []
    if first:
        operand_specs = [heads_spec] * 3 + [head_spec(1, cols)]
        out_specs = [acc_spec, wide_spec, wide_spec]
        out_shape = [acc_shape, wide_shape, wide_shape]
    else:
        operand_specs = [wide_spec, wide_spec, acc_spec]
        if last:
            out_specs = [heads_spec]
            out_shape = [jax.ShapeDtypeStruct((seqs, groups * GROUP, HEAD_DIM, slots), f32)]
            scratch = [pltpu.VMEM((1, 1, HEAD_DIM, cols), f32)]
        else:
            out_specs = [acc_spec]
            out_shape = [acc_shape]
    outs = pl.pallas_call(
        functools.partial(backward_kernel, ring_size, masks, first, last),
        grid=(groups, seqs),
        in_specs=[SMEM_SPEC] + kv_specs(masks, slots) + operand_specs,
        out_specs=kv_specs(masks, slots) + out_specs,
        out_shape=kv_shapes + out_shape,
        scratch_shapes=scratch,
        compiler_params=PARAMS,
        cost_estimate=call_cost(kvs[0].shape, len(masks), 10),
        name="attend_back",
    )(info, *kvs, *operands)
    return (outs[: len(masks)], outs[len(masks) :])


RING = ("ctx", "tp")


def swap(value, mask):
    size = lax.axis_size(RING)
    return lax.ppermute(value, RING, [(i, i ^ mask) for i in range(size)])


def mirror(value):
    size = lax.axis_size(RING)
    return lax.ppermute(value, RING, [(i, size - 1 - i) for i in range(size)])


def mirror_odd(value):
    moved = mirror(value[1::2])
    seqs = value.shape[0]
    return jnp.concatenate(
        [moved[s // 2][None] if s % 2 else value[s][None] for s in range(seqs)], axis=0
    )


def move_back(value):
    moved = mirror(value[1::2].astype(bf16)).astype(f32)
    seqs = value.shape[0]
    return jnp.concatenate(
        [moved[s // 2][None] if s % 2 else value[s][None] for s in range(seqs)], axis=0
    )


def add_low(*parts):
    total = parts[0].astype(f32)
    for part in parts[1:]:
        total = total + part.astype(f32)
    return total.astype(bf16)


def gather_fsdp(value):
    if lax.axis_size("fsdp") != 2:
        return lax.all_gather(value, "fsdp", axis=0, tiled=False)
    other = lax.ppermute(value, "fsdp", [(0, 1), (1, 0)])
    at_zero = lax.axis_index("fsdp") == 0
    return jnp.stack([jnp.where(at_zero, value, other), jnp.where(at_zero, other, value)])


def pick_half(value, axis, index):
    half = value.shape[axis] // 2
    return lax.dynamic_slice_in_dim(value, index * half, half, axis)


def join_halves(mine, other, axis, index):
    return jnp.where(
        index == 0,
        jnp.concatenate([mine, other], axis=axis),
        jnp.concatenate([other, mine], axis=axis),
    )


def reduce_steps(value, own):
    fsdp_size, rows, columns = value.shape
    outer = lax.axis_size(RING) // 4
    core = own % 2
    column = (own // 2) % 2
    plane = own // 4
    value = value.astype(bf16)
    value = add_low(pick_half(value, 2, core), swap(pick_half(value, 2, 1 - core), 1))
    value = yield value
    if fsdp_size == 2:
        here = lax.axis_index("fsdp")
        away = lax.dynamic_index_in_dim(value, 1 - here, 0, False)
        mine = lax.dynamic_index_in_dim(value, here, 0, False)
        value = add_low(mine, lax.ppermute(away, "fsdp", [(0, 1), (1, 0)]))
    else:
        value = lax.psum_scatter(value, "fsdp", scatter_dimension=0, tiled=False)
    value = yield value
    value = add_low(pick_half(value, 1, column), swap(pick_half(value, 1, 1 - column), 2))
    value = yield value
    piece = rows // outer

    def rows_of(index):
        return lax.dynamic_slice_in_dim(value, index * piece, piece, 0)

    mine = add_low(
        rows_of(plane), *[swap(rows_of(plane ^ k), 4 * k) for k in range(1, outer)]
    )
    mine = yield mine
    whole = jnp.zeros((rows, columns // 4), bf16)
    whole = lax.dynamic_update_slice_in_dim(whole, mine, plane * piece, 0)
    for k in range(1, outer):
        whole = lax.dynamic_update_slice_in_dim(whole, swap(mine, 4 * k), (plane ^ k) * piece, 0)
    whole = yield whole
    whole = join_halves(whole, swap(whole, 2), 1, column)
    whole = yield whole
    yield join_halves(whole, swap(whole, 1), 1, core).astype(f32)


def sum_steps(value):
    value = jnp.full((1, 128), value, f32)
    mask = 1
    while mask < lax.axis_size(RING):
        value = yield value + swap(value, mask)
        mask *= 2
    if lax.axis_size("fsdp") == 2:
        value = value + lax.ppermute(value, "fsdp", [(0, 1), (1, 0)])
    else:
        value = lax.psum(value, "fsdp")
    yield value


def advance(steps, value):
    try:
        return steps.send(value)
    except StopIteration:
        return value


def run_steps(steps, value=None):
    while True:
        try:
            value = steps.send(value)
        except StopIteration:
            return value


def shards(
    tokens,
    teacher,
    lengths,
    gain_one,
    w_query,
    w_key,
    w_value,
    w_out,
    gain_two,
    w_gate,
    w_up,
    w_down,
):
    seqs, slots, width = tokens.shape
    rows = seqs * slots
    kv_width = KV_HEADS * HEAD_DIM
    qkv_width = width + 2 * kv_width
    out_at = -(-qkv_width // 128) * 128
    gain_at = out_at + width
    pack_width = -(-(gain_at + 4) // 128) * 128
    grad_width = -(-(qkv_width + 2) // 512) * 512
    half = w_query.shape[0]
    hidden_part = w_gate.shape[1]
    fsdp_size = lax.axis_size("fsdp")
    tp_size = lax.axis_size("tp")
    ring_size = lax.axis_size(RING)
    outer = ring_size // 4

    tokens_here = mirror_odd(tokens)
    valid_here = jnp.sum(lengths)
    length_cols = jnp.stack([valid_here // 128, valid_here % 128]).astype(bf16)
    packed = jnp.concatenate(
        [
            w_query,
            w_key,
            w_value,
            jnp.zeros((half, out_at - qkv_width), bf16),
            w_out,
            gain_one[:, None],
            gain_two[:, None],
            jnp.broadcast_to(length_cols[None], (half, 2)),
            jnp.zeros((half, pack_width - gain_at - 4), bf16),
        ],
        axis=1,
    )
    packed = gather_fsdp(packed)
    count_total = jnp.sum(
        packed[:, 0, gain_at + 2].astype(f32) * 128.0 + packed[:, 0, gain_at + 3].astype(f32)
    )
    packed = packed.reshape(width, pack_width)
    w_qkv = packed[:, :qkv_width]
    w_o = packed[:, out_at:gain_at]
    g_one = packed[:, gain_at].astype(f32)
    g_two = packed[:, gain_at + 1].astype(f32)
    ffn_pack = jnp.concatenate([w_gate, w_up, w_down.T], axis=1)

    own = lax.axis_index(RING).astype(jnp.int32)
    blocks = jnp.stack([block_of(own, s, ring_size) for s in range(seqs)])
    positions = blocks[:, None] * slots + jnp.arange(slots, dtype=jnp.int32)[None]
    cosine, sine = rope_tables(positions)
    info = jnp.concatenate([lengths.astype(jnp.int32), own[None]])
    valid_mask = (positions < lengths[:, None]).astype(f32)

    inputs = tokens_here.astype(f32)
    normed = norm_rows(inputs, g_one).astype(bf16)
    qkv = jnp.einsum("df,sld->sfl", w_qkv, normed, preferred_element_type=f32)
    qk = qkv[:, : width + kv_width].reshape(seqs, HEADS + KV_HEADS, HEAD_DIM, slots)
    qk = rotate_cols(qk, cosine, sine).astype(bf16)
    queries = qk[:, :HEADS]
    values = qkv[:, width + kv_width :].astype(bf16).reshape(seqs, KV_HEADS, HEAD_DIM, slots)

    kv = {0: jnp.concatenate([qk[:, HEADS:], values], axis=2)}

    def outgoing(mask):
        return jnp.where(own < (own ^ mask), kv[0][0::2], kv[0][1::2])

    coming = {mask: swap(outgoing(mask), mask) for mask in [1, 2] + [4 * k for k in range(1, outer)]}
    calls = [(0,), (1, 2, 4)]
    for k in range(1, outer - 1):
        calls.append((4 * k - 1, 4 * k + 1, 4 * k + 2, 4 * k + 4))
    calls.append((4 * outer - 5, 4 * outer - 3, 4 * outer - 2, 4 * outer - 1))
    query_rows, *state = attend(ring_size, calls[0], info, queries, [kv[0]], None, False)
    for number, masks in enumerate(calls[1:], 1):
        if masks[-1] not in coming:
            coming[masks[-1]] = swap(coming[masks[-1] - 1], 1)
        later = [ffn_pack] if number == 1 else [teacher] if number == 2 else []
        *arrived, first_state = lax.optimization_barrier(
            [coming[m] for m in masks] + later + [state[0]]
        )
        if number == 1:
            ffn_all = lax.all_gather(arrived.pop(), ("tp", "fsdp"), axis=0, tiled=False)
            ffn_all = ffn_all.reshape(tp_size, width, 3 * hidden_part)
        if number == 2:
            teacher_here = mirror_odd(arrived.pop())
        kv.update(zip(masks, arrived))
        state = [first_state, state[1]]
        for mask in masks:
            if mask % 4 == 0:
                coming[mask + 2] = swap(kv[mask], 2)
                coming[mask + 1] = swap(kv[mask], 1)
            elif mask % 4 == 2 and mask + 1 not in coming:
                coming[mask + 1] = swap(kv[mask], 1)
        state = attend(
            ring_size, masks, info, query_rows, arrived, state, number == len(calls) - 1
        )
    attended, lse = state
    attended_t = attended.reshape(seqs, width, slots)

    middle = inputs + jnp.einsum("sfl,fd->sld", attended_t, w_o, preferred_element_type=f32)
    normed_two = norm_rows(middle, g_two).astype(bf16)
    flat_two = normed_two.reshape(rows, width)
    gate_up_w = ffn_all[:, :, : 2 * hidden_part]
    down_wt = ffn_all[:, :, 2 * hidden_part :]
    gate_up = jnp.einsum("rd,tdf->trf", flat_two, gate_up_w, preferred_element_type=f32)
    gate_pre = gate_up[..., :hidden_part]
    up_pre = gate_up[..., hidden_part:]
    gate_sigmoid = jax.nn.sigmoid(gate_pre)
    hidden = (gate_pre * gate_sigmoid * up_pre).astype(bf16)
    branch = jnp.einsum("trf,tdf->rd", hidden, down_wt, preferred_element_type=f32)
    result = middle + branch.reshape(seqs, slots, width)
    mismatch = result - teacher_here.astype(f32)
    squared_part = jnp.sum(valid_mask[..., None] * mismatch * mismatch)
    slots_all = seqs * fsdp_size * slots * ring_size
    d_result = valid_mask[..., None] * mismatch * (slots_all / count_total)
    d_branch = d_result.astype(bf16).reshape(rows, width)
    d_hidden = jnp.einsum("rd,tdf->trf", d_branch, down_wt, preferred_element_type=f32)
    d_down_wt = jnp.einsum("rd,trf->tdf", d_branch, hidden, preferred_element_type=f32)
    d_gate = (d_hidden * up_pre * gate_sigmoid * (1.0 + gate_pre * (1.0 - gate_sigmoid))).astype(bf16)
    d_up = (d_hidden * gate_pre * gate_sigmoid).astype(bf16)
    d_gate_up = jnp.concatenate([d_gate, d_up], axis=-1)
    d_gate_up_w = jnp.einsum("rd,trf->tdf", flat_two, d_gate_up, preferred_element_type=f32)
    d_normed_two = jnp.einsum("trf,tdf->rd", d_gate_up, gate_up_w, preferred_element_type=f32)
    norm_two_pull = jax.vjp(norm_rows, middle, g_two)[1]
    d_middle_norm, d_gain_two = norm_two_pull(d_normed_two.reshape(seqs, slots, width))
    d_middle = d_result + d_middle_norm
    d_attn_branch = d_middle.astype(bf16)
    d_attended_t = jnp.einsum("fd,sld->sfl", w_o, d_attn_branch, preferred_element_type=f32)
    d_attended_t = d_attended_t.astype(bf16).reshape(seqs, HEADS, HEAD_DIM, slots)
    d_out_w = jnp.einsum("sfl,sld->fd", attended_t, d_attn_branch, preferred_element_type=f32)

    d_ffn = jnp.concatenate([d_gate_up_w, d_down_wt], axis=-1).astype(bf16)
    d_ffn = d_ffn.reshape(tp_size * fsdp_size, half, 3 * hidden_part)
    d_ffn = lax.psum_scatter(d_ffn, ("tp", "fsdp"), scatter_dimension=0, tiled=False)
    out_width = -(-width // 512) * 512
    d_out_w = jnp.pad(d_out_w, ((0, 0), (0, out_width - width))).reshape(fsdp_size, half, out_width)
    output = move_back(result)
    out_steps = reduce_steps(d_out_w, own)
    loss_steps = sum_steps(squared_part)
    d_out_w = next(out_steps)
    loss_sum = next(loss_steps)

    calls = [(4 * outer - 2, 4 * outer - 1)]
    for k in reversed(range(1, outer)):
        calls.append((4 * k, 4 * k + 1, 4 * k - 2, 4 * k - 1))
    calls.append((0, 1))
    operands = [queries, d_attended_t, attended, lse]
    core_sums = {}
    sums = {}
    d_kv_terms = []
    for number, masks in enumerate(calls):
        last = number == len(calls) - 1
        if number:
            if number >= 2:
                due = list(calls[number - 2][::2])
            else:
                due = []
            held = [core_sums[m] for m in due] + [d_out_w, loss_sum]
            if number == 2:
                held.append(output)
            if number == 3:
                held.append(d_ffn)
            held = list(lax.optimization_barrier([info] + held))
            info = held.pop(0)
            if number == 3:
                d_ffn = lax.psum(held.pop(), "ctx")
            if number == 2:
                output = held.pop()
            loss_sum = advance(loss_steps, held.pop())
            d_out_w = advance(out_steps, held.pop())
            for mask, value in zip(due, held):
                core_sums[mask] = value
                if mask % 4:
                    sums[mask - 2] = swap(value, 2)
                else:
                    d_kv_terms.append((mask, swap(add_low(value, sums[mask]), mask)))
        parts, outs = attend_back(
            ring_size, masks, info, [kv[m] for m in masks], operands, number == 0, last
        )
        parts = list(parts)
        for place in range(0, 0 if last else len(masks), 2):
            core_sums[masks[place]] = add_low(parts[place], swap(parts[place + 1], 1))
        if number == 0:
            operands = [outs[1], outs[2], outs[0]]
        else:
            operands = operands[:2] + [outs[0]]
    d_query = outs[0]
    for mask in calls[-2][::2]:
        if mask % 4:
            sums[mask - 2] = swap(core_sums[mask], 2)
        else:
            d_kv_terms.append((mask, swap(add_low(core_sums[mask], sums[mask]), mask)))
    d_kv_terms += [(2, sums[0]), (1, swap(parts[1], 1))]
    d_ffn, parts[0] = lax.optimization_barrier((d_ffn, parts[0]))
    d_kv_halves = []
    for parity in range(2):
        total = parts[0][parity::2].astype(f32)
        for mask, term in d_kv_terms:
            from_it = (own > (own ^ mask)) == (parity == 1)
            total = total + jnp.where(from_it, term.astype(f32), 0.0)
        d_kv_halves.append(total)
    d_kv = jnp.stack(d_kv_halves, axis=1).reshape((seqs,) + parts[0].shape[1:])
    loss_sum = run_steps(loss_steps, loss_sum)
    loss_value = loss_sum[0, 0] / (count_total * width)
    d_out_w = run_steps(out_steps, d_out_w)
    d_ffn = d_ffn.astype(f32)

    d_qk = jnp.concatenate([d_query, d_kv[:, :, :HEAD_DIM]], axis=1)
    d_qk = rotate_cols(d_qk, cosine, -sine).astype(bf16).reshape(seqs, width + kv_width, slots)
    d_values = d_kv[:, :, HEAD_DIM:].astype(bf16).reshape(seqs, kv_width, slots)
    d_qkv = jnp.concatenate([d_qk, d_values], axis=1)
    d_normed = jnp.einsum("sfl,df->sld", d_qkv, w_qkv, preferred_element_type=f32)
    d_qkv_w = jnp.einsum("sld,sfl->df", normed, d_qkv, preferred_element_type=f32)
    norm_one_pull = jax.vjp(norm_rows, inputs, g_one)[1]
    d_inputs_norm, d_gain_one = norm_one_pull(d_normed)
    tokens_grad = move_back(d_middle + d_inputs_norm)
    d_packed = jnp.concatenate(
        [
            d_qkv_w,
            d_gain_one[:, None],
            d_gain_two[:, None],
            jnp.zeros((width, grad_width - qkv_width - 2), f32),
        ],
        axis=1,
    )
    steps = reduce_steps(d_packed.reshape(fsdp_size, half, grad_width), own)
    d_packed = next(steps)
    d_packed = steps.send(d_packed)
    d_packed = steps.send(d_packed)
    tokens_grad, d_packed = lax.optimization_barrier((tokens_grad, d_packed))
    d_packed = run_steps(steps, d_packed)
    return (
        output,
        loss_value,
        tokens_grad,
        d_packed[:, qkv_width],
        d_packed[:, :width],
        d_packed[:, width : width + kv_width],
        d_packed[:, width + kv_width : qkv_width],
        d_out_w[:, :width],
        d_packed[:, qkv_width + 1],
        d_ffn[:, :hidden_part],
        d_ffn[:, hidden_part : 2 * hidden_part],
        d_ffn[:, 2 * hidden_part :].T,
    )


def solution(mesh):
    slots_spec = P("fsdp", ("ctx", "tp"), None)
    rows_spec = P("fsdp", None)
    return jax.shard_map(
        shards,
        mesh=mesh,
        in_specs=(
            slots_spec,
            slots_spec,
            P("fsdp"),
            P("fsdp"),
            rows_spec,
            rows_spec,
            rows_spec,
            rows_spec,
            P("fsdp"),
            P("fsdp", "tp"),
            P("fsdp", "tp"),
            P("tp", "fsdp"),
        ),
        out_specs=(
            slots_spec,
            P(),
            slots_spec,
            P("fsdp"),
            rows_spec,
            rows_spec,
            rows_spec,
            rows_spec,
            P("fsdp"),
            P("fsdp", "tp"),
            P("fsdp", "tp"),
            P("tp", "fsdp"),
        ),
        check_vma=False,
    )
```

```python
import functools

import jax
import jax.numpy as jnp
from jax import lax
from jax.experimental import pallas as pl
from jax.experimental.pallas import tpu as pltpu
from jax.sharding import PartitionSpec as P

HEADS = 9
KV_HEADS = 3
GROUP = HEADS // KV_HEADS
HEAD_DIM = 64
AUG = HEAD_DIM + 16

EPS = 1e-05
ROPE_BASE = 10000.0
NEG = -1e30
LOG2E = 1.4426950408889634
EXP2_SCALE = LOG2E * HEAD_DIM ** (-0.5)

f32 = jnp.float32
bf16 = jnp.bfloat16
NN = ((1,), (0,))
TN = ((0,), (0,))
NT = ((1,), (1,))


def dot(left, right, dims):
    return lax.dot_general(left, right, (dims, ((), ())), preferred_element_type=f32)


def norm_rows(values, gain):
    return values * lax.rsqrt(jnp.mean(values * values, axis=-1, keepdims=True) + EPS) * gain


def rope_tables(positions):
    half_width = HEAD_DIM // 2
    frequency = ROPE_BASE ** (-(jnp.arange(half_width, dtype=f32) * 2.0) / HEAD_DIM)
    angles = frequency[None, None, :, None] * positions.astype(f32)[:, None, None, :]
    return (jnp.cos(angles), jnp.sin(angles))


def rotate_cols(values, cosine, sine):
    half_width = HEAD_DIM // 2
    lower = values[..., :half_width, :]
    upper = values[..., half_width:, :]
    return jnp.concatenate([lower * cosine - upper * sine, upper * cosine + lower * sine], axis=-2)


def three_pieces(row):
    first = row.astype(bf16)
    rest = row - first.astype(f32)
    second = rest.astype(bf16)
    third = (rest - second.astype(f32)).astype(bf16)
    return (first, second, third)


def penalty_row(block_start, width, length):
    key_pos = block_start + lax.broadcasted_iota(jnp.int32, (1, width), 1)
    return jnp.where(key_pos < length, 0.0, NEG).astype(bf16)


def extra_rows(rows, width):
    wide = jnp.zeros((16, width), f32)
    index = lax.broadcasted_iota(jnp.int32, (16, width), 0)
    for place, row in enumerate(rows):
        wide = jnp.where(index == place, row.astype(f32), wide)
    return wide.astype(bf16)


def block_of(device, seq, ring_size):
    return jnp.where(seq % 2 == 1, ring_size - 1 - device, device)


def needed(device, mask, seq):
    if mask == 0:
        return seq >= 0
    return (device ^ mask > device) == (seq % 2 == 1)


def forward_kernel(ring_size, masks, first, last, *refs):
    count = len(masks)
    info, q_ref = refs[:2]
    kv_refs = refs[2 : 2 + count]
    rest = refs[2 + count :]
    slots = kv_refs[0].shape[-1]
    cols = GROUP * slots
    if first:
        qa_ref, max_ref, acc_ref = rest
    else:
        qa_ref = q_ref
        if last:
            max_in, acc_in, out_ref, lse_ref, max_ref, acc_ref = rest
        else:
            max_in, acc_in, max_ref, acc_ref = rest
        max_ref[...] = max_in[...]
        acc_ref[...] = acc_in[...]
    device = info[info.shape[0] - 1]

    def step(seq, keys, values, block, diagonal):
        key_cols = jnp.concatenate(
            [keys, extra_rows([penalty_row(block * slots, slots, info[seq])], slots)], axis=0
        )
        value_ones = extra_rows([jnp.ones((1, slots), f32)], slots)
        value_cols = jnp.concatenate([values, value_ones], axis=0)
        scores = dot(key_cols, qa_ref[seq, 0], TN) * EXP2_SCALE
        if diagonal:
            key_at = lax.broadcasted_iota(jnp.int32, (slots, cols), 0)
            query_at = lax.broadcasted_iota(jnp.int32, (slots, cols), 1) % slots
            scores = jnp.where(key_at <= query_at, scores, NEG)
        old_max = max_ref[seq, 0]
        new_max = jnp.maximum(old_max, jnp.max(scores, axis=0, keepdims=True))
        weights = jnp.exp2(scores - new_max).astype(bf16)
        max_ref[seq, 0] = new_max
        acc_ref[seq, 0] = acc_ref[seq, 0] * jnp.exp2(old_max - new_max) + dot(value_cols, weights, NN)

    def work(seq, carry):
        if first:
            heads = [q_ref[seq, h] for h in range(GROUP)]
            qa_ref[seq, 0, 0:HEAD_DIM] = jnp.concatenate(heads, axis=1)
            qa_ref[seq, 0, HEAD_DIM:AUG] = extra_rows([jnp.ones((1, cols), f32)], cols)
            max_ref[seq] = jnp.full(max_ref.shape[1:], NEG, f32)
            acc_ref[seq] = jnp.zeros(acc_ref.shape[1:], f32)
        for kv_ref, mask in zip(kv_refs, masks):
            block = block_of(device ^ mask, seq, ring_size)
            at = seq // 2 if mask else seq

            @pl.when(needed(device, mask, seq) & (block * slots < info[seq]))
            def _():
                keys = kv_ref[at, 0, 0:HEAD_DIM]
                step(seq, keys, kv_ref[at, 0, HEAD_DIM:], block, mask == 0)

        if last:
            total = acc_ref[seq, 0, HEAD_DIM : HEAD_DIM + 1]
            heads_out = acc_ref[seq, 0, 0:HEAD_DIM] / total
            lse_ref[seq, 0] = (max_ref[seq, 0] + jnp.log2(total)) * (1.0 / EXP2_SCALE)
            for h in range(GROUP):
                out_ref[seq, h] = heads_out[:, h * slots : (h + 1) * slots].astype(bf16)
        return carry

    lax.fori_loop(0, qa_ref.shape[0], work, 0)


def backward_kernel(ring_size, masks, first, last, *refs):
    count = len(masks)
    info = refs[0]
    kv_refs = refs[1 : 1 + count]
    rest = refs[1 + count :]
    slots = kv_refs[0].shape[-1]
    cols = GROUP * slots
    if first:
        q_ref, do_ref, o_ref, lse_ref = rest[:4]
        dkv_refs = rest[4 : 4 + count]
        acc_ref, qa_ref, da_ref = rest[4 + count :]
    else:
        qa_ref, da_ref, acc_in = rest[:3]
        dkv_refs = rest[3 : 3 + count]
        if last:
            dq_ref, acc_ref = rest[3 + count :]
        else:
            (acc_ref,) = rest[3 + count :]
        acc_ref[...] = acc_in[...]
    device = info[info.shape[0] - 1]

    def prepare(seq):
        grads = jnp.concatenate([do_ref[seq, h] for h in range(GROUP)], axis=1)
        heads_out = jnp.concatenate([o_ref[seq, h] for h in range(GROUP)], axis=1)
        delta = jnp.sum(grads.astype(f32) * heads_out.astype(f32), axis=0, keepdims=True)
        heads = [q_ref[seq, h] for h in range(GROUP)]
        qa_ref[seq, 0, 0:HEAD_DIM] = jnp.concatenate(heads, axis=1)
        qa_ref[seq, 0, HEAD_DIM:AUG] = extra_rows(
            three_pieces(-lse_ref[seq, 0]) + (jnp.ones((1, cols), f32),), cols
        )
        da_ref[seq, 0, 0:HEAD_DIM] = grads
        da_ref[seq, 0, HEAD_DIM:AUG] = extra_rows(three_pieces(-delta), cols)
        acc_ref[seq] = jnp.zeros(acc_ref.shape[1:], f32)

    def step(seq, keys, values, dkv_ref, at, block, diagonal):
        ones_key = jnp.ones((1, slots), f32)
        penalty = penalty_row(block * slots, slots, info[seq])
        key_cols = jnp.concatenate([keys, extra_rows([ones_key] * 3 + [penalty], slots)], axis=0)
        value_cols = jnp.concatenate([values, extra_rows([ones_key] * 3, slots)], axis=0)
        scores = dot(qa_ref[seq, 0], key_cols, TN) * EXP2_SCALE
        if diagonal:
            query_at = lax.broadcasted_iota(jnp.int32, (cols, slots), 0) % slots
            key_at = lax.broadcasted_iota(jnp.int32, (cols, slots), 1)
            scores = jnp.where(key_at <= query_at, scores, NEG)
        weights = jnp.exp2(scores)
        d_scores = (weights * dot(da_ref[seq, 0], value_cols, TN)).astype(bf16)
        d_value = dot(da_ref[seq, 0, 0:HEAD_DIM], weights.astype(bf16), NN)
        d_key = dot(qa_ref[seq, 0, 0:HEAD_DIM], d_scores, NN) * (HEAD_DIM ** (-0.5))
        acc_ref[seq, 0] += dot(keys, d_scores, NT)
        dkv_ref[at, 0, 0:HEAD_DIM] = d_key.astype(bf16)
        dkv_ref[at, 0, HEAD_DIM:] = d_value.astype(bf16)

    def work(seq, carry):
        if first:
            prepare(seq)
        active = block_of(device, seq, ring_size) * slots < info[seq]
        for kv_ref, dkv_ref, mask in zip(kv_refs, dkv_refs, masks):
            block = block_of(device ^ mask, seq, ring_size)
            turn = needed(device, mask, seq)
            at = seq // 2 if mask else seq

            @pl.when(turn & active)
            def _():
                keys = kv_ref[at, 0, 0:HEAD_DIM]
                step(seq, keys, kv_ref[at, 0, HEAD_DIM:], dkv_ref, at, block, mask == 0)

            @pl.when(turn & jnp.logical_not(active))
            def _():
                dkv_ref[at] = jnp.zeros(dkv_ref.shape[1:], bf16)

        if last:
            d_query = acc_ref[seq, 0] * (HEAD_DIM ** (-0.5))
            for h in range(GROUP):
                dq_ref[seq, h] = d_query[:, h * slots : (h + 1) * slots]
        return carry

    lax.fori_loop(0, qa_ref.shape[0], work, 0)


def head_spec(seqs, rows, lanes, heads=1):
    return pl.BlockSpec((seqs, heads, rows, lanes), lambda group: (0, group, 0, 0))


def kv_specs(kvs):
    return [head_spec(kv.shape[0], kv.shape[2], kv.shape[3]) for kv in kvs]


SMEM_SPEC = pl.BlockSpec(memory_space=pltpu.SMEM)
PARAMS = pltpu.CompilerParams(vmem_limit_bytes=60 * 2**20)


def call_cost(kv_shape, count, products):
    seqs, groups, _, slots = kv_shape
    pairs = seqs * groups * GROUP * slots * slots * count
    return pl.CostEstimate(
        flops=pairs * HEAD_DIM * products * 4,
        transcendentals=pairs,
        bytes_accessed=seqs * groups * count * 4 * HEAD_DIM * slots,
    )


def attend(ring_size, masks, info, queries, kvs, state, last):
    first = state is None
    groups, slots = kvs[0].shape[1], kvs[0].shape[3]
    seqs = queries.shape[0]
    cols = GROUP * slots
    wide_spec = head_spec(seqs, AUG, cols)
    row_spec = head_spec(seqs, 1, cols)
    wide_shape = (seqs, groups, AUG, cols)
    row_shape = jax.ShapeDtypeStruct((seqs, groups, 1, cols), f32)
    state_specs = [row_spec, wide_spec]
    state_shapes = [row_shape, jax.ShapeDtypeStruct(wide_shape, f32)]
    query_spec = wide_spec
    scratch = []
    if first:
        query_spec = head_spec(seqs, HEAD_DIM, slots, GROUP)
        out_specs = [wide_spec] + state_specs
        out_shape = [jax.ShapeDtypeStruct(wide_shape, bf16)] + state_shapes
    elif last:
        out_specs = [head_spec(seqs, HEAD_DIM, slots, GROUP), row_spec]
        out_shape = [jax.ShapeDtypeStruct((seqs, groups * GROUP, HEAD_DIM, slots), bf16), row_shape]
        scratch = [pltpu.VMEM((seqs, 1, 1, cols), f32), pltpu.VMEM((seqs, 1, AUG, cols), f32)]
    else:
        out_specs = state_specs
        out_shape = state_shapes
    return pl.pallas_call(
        functools.partial(forward_kernel, ring_size, masks, first, last),
        grid=(groups,),
        in_specs=[SMEM_SPEC, query_spec]
        + kv_specs(kvs)
        + ([] if first else state_specs),
        out_specs=out_specs,
        out_shape=out_shape,
        scratch_shapes=scratch,
        compiler_params=PARAMS,
        cost_estimate=call_cost(kvs[0].shape, len(masks), 4),
        name="attend",
    )(info, queries, *kvs, *([] if first else state))


def attend_back(ring_size, masks, info, kvs, operands, first, last):
    groups, slots = kvs[0].shape[1], kvs[0].shape[3]
    seqs = operands[0].shape[0]
    cols = GROUP * slots
    heads_spec = head_spec(seqs, HEAD_DIM, slots, GROUP)
    wide_spec = head_spec(seqs, AUG, cols)
    acc_spec = head_spec(seqs, HEAD_DIM, cols)
    kv_shapes = [jax.ShapeDtypeStruct(kv.shape, bf16) for kv in kvs]
    wide_shape = jax.ShapeDtypeStruct((seqs, groups, AUG, cols), bf16)
    acc_shape = jax.ShapeDtypeStruct((seqs, groups, HEAD_DIM, cols), f32)
    scratch = []
    if first:
        operand_specs = [heads_spec] * 3 + [head_spec(seqs, 1, cols)]
        out_specs = [acc_spec, wide_spec, wide_spec]
        out_shape = [acc_shape, wide_shape, wide_shape]
    else:
        operand_specs = [wide_spec, wide_spec, acc_spec]
        if last:
            out_specs = [heads_spec]
            out_shape = [jax.ShapeDtypeStruct((seqs, groups * GROUP, HEAD_DIM, slots), f32)]
            scratch = [pltpu.VMEM((seqs, 1, HEAD_DIM, cols), f32)]
        else:
            out_specs = [acc_spec]
            out_shape = [acc_shape]
    outs = pl.pallas_call(
        functools.partial(backward_kernel, ring_size, masks, first, last),
        grid=(groups,),
        in_specs=[SMEM_SPEC] + kv_specs(kvs) + operand_specs,
        out_specs=kv_specs(kvs) + out_specs,
        out_shape=kv_shapes + out_shape,
        scratch_shapes=scratch,
        compiler_params=PARAMS,
        cost_estimate=call_cost(kvs[0].shape, len(masks), 10),
        name="attend_back",
    )(info, *kvs, *operands)
    return (outs[: len(masks)], outs[len(masks) :])


RING = ("ctx", "tp")


def swap(value, mask):
    size = lax.axis_size(RING)
    return lax.ppermute(value, RING, [(i, i ^ mask) for i in range(size)])


def mirror(value):
    size = lax.axis_size(RING)
    return lax.ppermute(value, RING, [(i, size - 1 - i) for i in range(size)])


def mirror_odd(value):
    moved = mirror(value[1::2])
    seqs = value.shape[0]
    return jnp.concatenate(
        [moved[s // 2][None] if s % 2 else value[s][None] for s in range(seqs)], axis=0
    )


def move_back(value):
    moved = mirror(value[1::2].astype(bf16)).astype(f32)
    seqs = value.shape[0]
    return jnp.concatenate(
        [moved[s // 2][None] if s % 2 else value[s][None] for s in range(seqs)], axis=0
    )


def add_low(*parts):
    total = parts[0].astype(f32)
    for part in parts[1:]:
        total = total + part.astype(f32)
    return total.astype(bf16)


def gather_fsdp(value):
    if lax.axis_size("fsdp") != 2:
        return lax.all_gather(value, "fsdp", axis=0, tiled=False)
    other = lax.ppermute(value, "fsdp", [(0, 1), (1, 0)])
    at_zero = lax.axis_index("fsdp") == 0
    return jnp.stack([jnp.where(at_zero, value, other), jnp.where(at_zero, other, value)])


def pick_half(value, axis, index):
    half = value.shape[axis] // 2
    return lax.dynamic_slice_in_dim(value, index * half, half, axis)


def join_halves(mine, other, axis, index):
    return jnp.where(
        index == 0,
        jnp.concatenate([mine, other], axis=axis),
        jnp.concatenate([other, mine], axis=axis),
    )


def reduce_steps(value, own):
    fsdp_size, rows, columns = value.shape
    outer = lax.axis_size(RING) // 4
    core = own % 2
    column = (own // 2) % 2
    plane = own // 4
    value = value.astype(bf16)
    value = add_low(pick_half(value, 2, core), swap(pick_half(value, 2, 1 - core), 1))
    value = yield value
    if fsdp_size == 2:
        here = lax.axis_index("fsdp")
        away = lax.dynamic_index_in_dim(value, 1 - here, 0, False)
        mine = lax.dynamic_index_in_dim(value, here, 0, False)
        value = add_low(mine, lax.ppermute(away, "fsdp", [(0, 1), (1, 0)]))
    else:
        value = lax.psum_scatter(value, "fsdp", scatter_dimension=0, tiled=False)
    value = yield value
    value = add_low(pick_half(value, 1, column), swap(pick_half(value, 1, 1 - column), 2))
    value = yield value
    piece = rows // outer

    def rows_of(index):
        return lax.dynamic_slice_in_dim(value, index * piece, piece, 0)

    mine = add_low(
        rows_of(plane), *[swap(rows_of(plane ^ k), 4 * k) for k in range(1, outer)]
    )
    mine = yield mine
    whole = jnp.zeros((rows, columns // 4), bf16)
    whole = lax.dynamic_update_slice_in_dim(whole, mine, plane * piece, 0)
    for k in range(1, outer):
        whole = lax.dynamic_update_slice_in_dim(whole, swap(mine, 4 * k), (plane ^ k) * piece, 0)
    whole = yield whole
    whole = join_halves(whole, swap(whole, 2), 1, column)
    whole = yield whole
    yield join_halves(whole, swap(whole, 1), 1, core).astype(f32)


def sum_steps(value):
    value = jnp.full((1, 128), value, f32)
    mask = 1
    while mask < lax.axis_size(RING):
        value = yield value + swap(value, mask)
        mask *= 2
    if lax.axis_size("fsdp") == 2:
        value = value + lax.ppermute(value, "fsdp", [(0, 1), (1, 0)])
    else:
        value = lax.psum(value, "fsdp")
    yield value


def advance(steps, value):
    try:
        return steps.send(value)
    except StopIteration:
        return value


def run_steps(steps, value=None):
    while True:
        try:
            value = steps.send(value)
        except StopIteration:
            return value


def shards(
    tokens,
    teacher,
    lengths,
    gain_one,
    w_query,
    w_key,
    w_value,
    w_out,
    gain_two,
    w_gate,
    w_up,
    w_down,
):
    seqs, slots, width = tokens.shape
    rows = seqs * slots
    kv_width = KV_HEADS * HEAD_DIM
    qkv_width = width + 2 * kv_width
    gain_at = qkv_width
    pack_width = -(-(gain_at + 2) // 128) * 128
    grad_width = -(-(qkv_width + 2) // 512) * 512
    half = w_query.shape[0]
    hidden_part = w_gate.shape[1]
    fsdp_size = lax.axis_size("fsdp")
    tp_size = lax.axis_size("tp")
    ring_size = lax.axis_size(RING)
    outer = ring_size // 4

    tokens_here = mirror_odd(tokens)
    count_total = jnp.sum(gather_fsdp(lengths)).astype(f32)
    packed = jnp.concatenate(
        [
            w_query,
            w_key,
            w_value,
            gain_one[:, None],
            gain_two[:, None],
            jnp.zeros((half, pack_width - gain_at - 2), bf16),
        ],
        axis=1,
    )
    packed = gather_fsdp(packed)
    packed = packed.reshape(width, pack_width)
    w_qkv = packed[:, :qkv_width]
    g_one = packed[:, gain_at].astype(f32)
    g_two = packed[:, gain_at + 1].astype(f32)
    ffn_pack = jnp.concatenate([w_gate, w_up, w_down.T], axis=1)

    own = lax.axis_index(RING).astype(jnp.int32)
    blocks = jnp.stack([block_of(own, s, ring_size) for s in range(seqs)])
    positions = blocks[:, None] * slots + jnp.arange(slots, dtype=jnp.int32)[None]
    cosine, sine = rope_tables(positions)
    info = jnp.concatenate([lengths.astype(jnp.int32), own[None]])
    valid_mask = (positions < lengths[:, None]).astype(f32)

    inputs = tokens_here.astype(f32)
    normed = norm_rows(inputs, g_one).astype(bf16)
    qkv = jnp.einsum("df,sld->sfl", w_qkv, normed, preferred_element_type=f32)
    qk = qkv[:, : width + kv_width].reshape(seqs, HEADS + KV_HEADS, HEAD_DIM, slots)
    qk = rotate_cols(qk, cosine, sine).astype(bf16)
    queries = qk[:, :HEADS]
    values = qkv[:, width + kv_width :].astype(bf16).reshape(seqs, KV_HEADS, HEAD_DIM, slots)

    kv = {0: jnp.concatenate([qk[:, HEADS:], values], axis=2)}

    def outgoing(mask):
        return jnp.where(own < (own ^ mask), kv[0][0::2], kv[0][1::2])

    coming = {mask: swap(outgoing(mask), mask) for mask in [1, 2] + [4 * k for k in range(1, outer)]}
    calls = [(0,), (1, 2, 4)]
    for k in range(1, outer - 1):
        calls.append((4 * k - 1, 4 * k + 1, 4 * k + 2, 4 * k + 4))
    calls.append((4 * outer - 5, 4 * outer - 3, 4 * outer - 2, 4 * outer - 1))
    query_rows, *state = attend(ring_size, calls[0], info, queries, [kv[0]], None, False)
    for number, masks in enumerate(calls[1:], 1):
        if masks[-1] not in coming:
            coming[masks[-1]] = swap(coming[masks[-1] - 1], 1)
        later = [ffn_pack] if number == 1 else [w_out, teacher] if number == 2 else []
        *arrived, first_state = lax.optimization_barrier(
            [coming[m] for m in masks] + later + [state[0]]
        )
        if number == 1:
            ffn_all = lax.all_gather(arrived.pop(), ("tp", "fsdp"), axis=0, tiled=False)
            ffn_all = ffn_all.reshape(tp_size, width, 3 * hidden_part)
        if number == 2:
            teacher_here = mirror_odd(arrived.pop())
            w_o = gather_fsdp(arrived.pop()).reshape(width, width)
        kv.update(zip(masks, arrived))
        state = [first_state, state[1]]
        for mask in masks:
            if mask % 4 == 0:
                coming[mask + 2] = swap(kv[mask], 2)
                coming[mask + 1] = swap(kv[mask], 1)
            elif mask % 4 == 2 and mask + 1 not in coming:
                coming[mask + 1] = swap(kv[mask], 1)
        state = attend(
            ring_size, masks, info, query_rows, arrived, state, number == len(calls) - 1
        )
    attended, lse = state
    attended_t = attended.reshape(seqs, width, slots)

    middle = inputs + jnp.einsum("sfl,fd->sld", attended_t, w_o, preferred_element_type=f32)
    normed_two = norm_rows(middle, g_two).astype(bf16)
    flat_two = normed_two.reshape(rows, width)
    gate_up_w = ffn_all[:, :, : 2 * hidden_part]
    down_wt = ffn_all[:, :, 2 * hidden_part :]
    gate_up = jnp.einsum("rd,tdf->trf", flat_two, gate_up_w, preferred_element_type=f32)
    gate_pre = gate_up[..., :hidden_part]
    up_pre = gate_up[..., hidden_part:]
    gate_sigmoid = jax.nn.sigmoid(gate_pre)
    hidden = (gate_pre * gate_sigmoid * up_pre).astype(bf16)
    branch = jnp.einsum("trf,tdf->rd", hidden, down_wt, preferred_element_type=f32)
    result = middle + branch.reshape(seqs, slots, width)
    mismatch = result - teacher_here.astype(f32)
    squared_part = jnp.sum(valid_mask[..., None] * mismatch * mismatch)
    slots_all = seqs * fsdp_size * slots * ring_size
    d_result = valid_mask[..., None] * mismatch * (slots_all / count_total)
    d_branch = d_result.astype(bf16).reshape(rows, width)
    d_hidden = jnp.einsum("rd,tdf->trf", d_branch, down_wt, preferred_element_type=f32)
    d_down_wt = jnp.einsum("rd,trf->tdf", d_branch, hidden, preferred_element_type=f32)
    d_gate = (d_hidden * up_pre * gate_sigmoid * (1.0 + gate_pre * (1.0 - gate_sigmoid))).astype(bf16)
    d_up = (d_hidden * gate_pre * gate_sigmoid).astype(bf16)
    d_gate_up = jnp.concatenate([d_gate, d_up], axis=-1)
    d_gate_up_w = jnp.einsum("rd,trf->tdf", flat_two, d_gate_up, preferred_element_type=f32)
    d_normed_two = jnp.einsum("trf,tdf->rd", d_gate_up, gate_up_w, preferred_element_type=f32)
    norm_two_pull = jax.vjp(norm_rows, middle, g_two)[1]
    d_middle_norm, d_gain_two = norm_two_pull(d_normed_two.reshape(seqs, slots, width))
    d_middle = d_result + d_middle_norm
    d_attn_branch = d_middle.astype(bf16)
    d_attended_t = jnp.einsum("fd,sld->sfl", w_o, d_attn_branch, preferred_element_type=f32)
    d_attended_t = d_attended_t.astype(bf16).reshape(seqs, HEADS, HEAD_DIM, slots)
    d_out_w = jnp.einsum("sfl,sld->fd", attended_t, d_attn_branch, preferred_element_type=f32)

    d_ffn = jnp.concatenate([d_gate_up_w, d_down_wt], axis=-1).astype(bf16)
    d_ffn = d_ffn.reshape(tp_size * fsdp_size, half, 3 * hidden_part)
    d_ffn = lax.psum_scatter(d_ffn, ("tp", "fsdp"), scatter_dimension=0, tiled=False)
    out_width = -(-width // 512) * 512
    d_out_w = jnp.pad(d_out_w, ((0, 0), (0, out_width - width))).reshape(fsdp_size, half, out_width)
    output = move_back(result)
    out_steps = reduce_steps(d_out_w, own)
    loss_steps = sum_steps(squared_part)
    d_out_w = next(out_steps)
    loss_sum = next(loss_steps)

    calls = [(4 * outer - 2, 4 * outer - 1)]
    for k in reversed(range(1, outer)):
        calls.append((4 * k, 4 * k + 1, 4 * k - 2, 4 * k - 1))
    calls.append((0, 1))
    operands = [queries, d_attended_t, attended, lse]
    core_sums = {}
    sums = {}
    d_kv_terms = []
    for number, masks in enumerate(calls):
        last = number == len(calls) - 1
        if number:
            if number >= 2:
                due = list(calls[number - 2][::2])
            else:
                due = []
            held = [core_sums[m] for m in due] + [d_out_w, loss_sum]
            if number == 2:
                held.append(output)
            if number == 3:
                held.append(d_ffn)
            held = list(lax.optimization_barrier([info] + held))
            info = held.pop(0)
            if number == 3:
                d_ffn = lax.psum(held.pop(), "ctx")
            if number == 2:
                output = held.pop()
            loss_sum = advance(loss_steps, held.pop())
            d_out_w = advance(out_steps, held.pop())
            for mask, value in zip(due, held):
                core_sums[mask] = value
                if mask % 4:
                    sums[mask - 2] = swap(value, 2)
                else:
                    d_kv_terms.append((mask, swap(add_low(value, sums[mask]), mask)))
        parts, outs = attend_back(
            ring_size, masks, info, [kv[m] for m in masks], operands, number == 0, last
        )
        parts = list(parts)
        for place in range(0, 0 if last else len(masks), 2):
            core_sums[masks[place]] = add_low(parts[place], swap(parts[place + 1], 1))
        if number == 0:
            operands = [outs[1], outs[2], outs[0]]
        else:
            operands = operands[:2] + [outs[0]]
    d_query = outs[0]
    for mask in calls[-2][::2]:
        if mask % 4:
            sums[mask - 2] = swap(core_sums[mask], 2)
        else:
            d_kv_terms.append((mask, swap(add_low(core_sums[mask], sums[mask]), mask)))
    d_kv_terms += [(2, sums[0]), (1, swap(parts[1], 1))]
    d_ffn, parts[0] = lax.optimization_barrier((d_ffn, parts[0]))
    d_kv_halves = []
    for parity in range(2):
        total = parts[0][parity::2].astype(f32)
        for mask, term in d_kv_terms:
            from_it = (own > (own ^ mask)) == (parity == 1)
            total = total + jnp.where(from_it, term.astype(f32), 0.0)
        d_kv_halves.append(total)
    d_kv = jnp.stack(d_kv_halves, axis=1).reshape((seqs,) + parts[0].shape[1:])
    loss_sum = run_steps(loss_steps, loss_sum)
    loss_value = loss_sum[0, 0] / (count_total * width)
    d_out_w = run_steps(out_steps, d_out_w)
    d_ffn = d_ffn.astype(f32)

    d_qk = jnp.concatenate([d_query, d_kv[:, :, :HEAD_DIM]], axis=1)
    d_qk = rotate_cols(d_qk, cosine, -sine).astype(bf16).reshape(seqs, width + kv_width, slots)
    d_values = d_kv[:, :, HEAD_DIM:].astype(bf16).reshape(seqs, kv_width, slots)
    d_qkv = jnp.concatenate([d_qk, d_values], axis=1)
    d_normed = jnp.einsum("sfl,df->sld", d_qkv, w_qkv, preferred_element_type=f32)
    d_qkv_w = jnp.einsum("sld,sfl->df", normed, d_qkv, preferred_element_type=f32)
    norm_one_pull = jax.vjp(norm_rows, inputs, g_one)[1]
    d_inputs_norm, d_gain_one = norm_one_pull(d_normed)
    tokens_grad = d_middle + d_inputs_norm
    back = tokens_grad[1::2].astype(bf16)
    cut = 2 * width // 3 // 128 * 128
    back_parts = [mirror(back[..., :cut]), back[..., cut:]]
    d_packed = jnp.concatenate(
        [
            d_qkv_w,
            d_gain_one[:, None],
            d_gain_two[:, None],
            jnp.zeros((width, grad_width - qkv_width - 2), f32),
        ],
        axis=1,
    )
    steps = reduce_steps(d_packed.reshape(fsdp_size, half, grad_width), own)
    d_packed = next(steps)
    d_packed = steps.send(d_packed)
    d_packed = steps.send(d_packed)
    back_parts[0], d_packed = lax.optimization_barrier((back_parts[0], d_packed))
    d_packed = steps.send(d_packed)
    d_packed = steps.send(d_packed)
    back_parts[1], d_packed = lax.optimization_barrier((back_parts[1], d_packed))
    back = jnp.concatenate([back_parts[0], mirror(back_parts[1])], axis=2).astype(f32)
    tokens_grad = jnp.stack([tokens_grad[0::2], back], axis=1).reshape(tokens_grad.shape)
    d_packed = run_steps(steps, d_packed)
    return (
        output,
        loss_value,
        tokens_grad,
        d_packed[:, qkv_width],
        d_packed[:, :width],
        d_packed[:, width : width + kv_width],
        d_packed[:, width + kv_width : qkv_width],
        d_out_w[:, :width],
        d_packed[:, qkv_width + 1],
        d_ffn[:, :hidden_part],
        d_ffn[:, hidden_part : 2 * hidden_part],
        d_ffn[:, 2 * hidden_part :].T,
    )


def solution(mesh):
    slots_spec = P("fsdp", ("ctx", "tp"), None)
    rows_spec = P("fsdp", None)
    return jax.shard_map(
        shards,
        mesh=mesh,
        in_specs=(
            slots_spec,
            slots_spec,
            P("fsdp"),
            P("fsdp"),
            rows_spec,
            rows_spec,
            rows_spec,
            rows_spec,
            P("fsdp"),
            P("fsdp", "tp"),
            P("fsdp", "tp"),
            P("tp", "fsdp"),
        ),
        out_specs=(
            slots_spec,
            P(),
            slots_spec,
            P("fsdp"),
            rows_spec,
            rows_spec,
            rows_spec,
            rows_spec,
            P("fsdp"),
            P("fsdp", "tp"),
            P("fsdp", "tp"),
            P("tp", "fsdp"),
        ),
        check_vma=False,
    )
```

```python
import functools

import jax
import jax.numpy as jnp
from jax import lax
from jax.experimental import pallas as pl
from jax.experimental.pallas import tpu as pltpu
from jax.sharding import PartitionSpec as P

HEADS = 9
KV_HEADS = 3
GROUP = HEADS // KV_HEADS
HEAD_DIM = 64
AUG = HEAD_DIM + 16

EPS = 1e-05
ROPE_BASE = 10000.0
NEG = -1e30
LOG2E = 1.4426950408889634
EXP2_SCALE = LOG2E * HEAD_DIM ** (-0.5)

f32 = jnp.float32
bf16 = jnp.bfloat16
NN = ((1,), (0,))
TN = ((0,), (0,))
NT = ((1,), (1,))


def dot(left, right, dims):
    return lax.dot_general(left, right, (dims, ((), ())), preferred_element_type=f32)


def norm_rows(values, gain):
    return values * lax.rsqrt(jnp.mean(values * values, axis=-1, keepdims=True) + EPS) * gain


def rope_tables(positions):
    half_width = HEAD_DIM // 2
    frequency = ROPE_BASE ** (-(jnp.arange(half_width, dtype=f32) * 2.0) / HEAD_DIM)
    angles = frequency[None, None, :, None] * positions.astype(f32)[:, None, None, :]
    return (jnp.cos(angles), jnp.sin(angles))


def rotate_cols(values, cosine, sine):
    half_width = HEAD_DIM // 2
    lower = values[..., :half_width, :]
    upper = values[..., half_width:, :]
    return jnp.concatenate([lower * cosine - upper * sine, upper * cosine + lower * sine], axis=-2)


def three_pieces(row):
    first = row.astype(bf16)
    rest = row - first.astype(f32)
    second = rest.astype(bf16)
    third = (rest - second.astype(f32)).astype(bf16)
    return (first, second, third)


def penalty_row(block_start, width, length):
    key_pos = block_start + lax.broadcasted_iota(jnp.int32, (1, width), 1)
    return jnp.where(key_pos < length, 0.0, NEG).astype(bf16)


def extra_rows(rows, width):
    wide = jnp.zeros((16, width), f32)
    index = lax.broadcasted_iota(jnp.int32, (16, width), 0)
    for place, row in enumerate(rows):
        wide = jnp.where(index == place, row.astype(f32), wide)
    return wide.astype(bf16)


def block_of(device, seq, ring_size):
    return jnp.where(seq % 2 == 1, ring_size - 1 - device, device)


def needed(device, mask, seq):
    if mask == 0:
        return seq >= 0
    return (device ^ mask > device) == (seq % 2 == 1)


def forward_kernel(ring_size, masks, first, last, *refs):
    count = len(masks)
    info, q_ref = refs[:2]
    kv_refs = refs[2 : 2 + count]
    rest = refs[2 + count :]
    slots = kv_refs[0].shape[-1]
    cols = GROUP * slots
    if first:
        qa_ref, max_ref, acc_ref = rest
    else:
        qa_ref = q_ref
        if last:
            max_in, acc_in, out_ref, lse_ref, max_ref, acc_ref = rest
        else:
            max_in, acc_in, max_ref, acc_ref = rest
        max_ref[...] = max_in[...]
        acc_ref[...] = acc_in[...]
    device = info[info.shape[0] - 1]

    def step(seq, keys, values, block, diagonal):
        key_cols = jnp.concatenate(
            [keys, extra_rows([penalty_row(block * slots, slots, info[seq])], slots)], axis=0
        )
        value_ones = extra_rows([jnp.ones((1, slots), f32)], slots)
        value_cols = jnp.concatenate([values, value_ones], axis=0)
        scores = dot(key_cols, qa_ref[seq, 0], TN) * EXP2_SCALE
        if diagonal:
            key_at = lax.broadcasted_iota(jnp.int32, (slots, cols), 0)
            query_at = lax.broadcasted_iota(jnp.int32, (slots, cols), 1) % slots
            scores = jnp.where(key_at <= query_at, scores, NEG)
        old_max = max_ref[seq, 0]
        new_max = jnp.maximum(old_max, jnp.max(scores, axis=0, keepdims=True))
        weights = jnp.exp2(scores - new_max).astype(bf16)
        max_ref[seq, 0] = new_max
        acc_ref[seq, 0] = acc_ref[seq, 0] * jnp.exp2(old_max - new_max) + dot(value_cols, weights, NN)

    def work(seq, carry):
        if first:
            heads = [q_ref[seq, h] for h in range(GROUP)]
            qa_ref[seq, 0, 0:HEAD_DIM] = jnp.concatenate(heads, axis=1)
            qa_ref[seq, 0, HEAD_DIM:AUG] = extra_rows([jnp.ones((1, cols), f32)], cols)
            max_ref[seq] = jnp.full(max_ref.shape[1:], NEG, f32)
            acc_ref[seq] = jnp.zeros(acc_ref.shape[1:], f32)
        for kv_ref, mask in zip(kv_refs, masks):
            block = block_of(device ^ mask, seq, ring_size)
            at = seq // 2 if mask else seq

            @pl.when(needed(device, mask, seq) & (block * slots < info[seq]))
            def _():
                keys = kv_ref[at, 0, 0:HEAD_DIM]
                step(seq, keys, kv_ref[at, 0, HEAD_DIM:], block, mask == 0)

        if last:
            total = acc_ref[seq, 0, HEAD_DIM : HEAD_DIM + 1]
            heads_out = acc_ref[seq, 0, 0:HEAD_DIM] / total
            lse_ref[seq, 0] = (max_ref[seq, 0] + jnp.log2(total)) * (1.0 / EXP2_SCALE)
            for h in range(GROUP):
                out_ref[seq, h] = heads_out[:, h * slots : (h + 1) * slots].astype(bf16)
        return carry

    lax.fori_loop(0, qa_ref.shape[0], work, 0)


def backward_kernel(ring_size, masks, first, last, *refs):
    count = len(masks)
    info = refs[0]
    kv_refs = refs[1 : 1 + count]
    rest = refs[1 + count :]
    slots = kv_refs[0].shape[-1]
    cols = GROUP * slots
    if first:
        q_ref, do_ref, o_ref, lse_ref = rest[:4]
        dkv_refs = rest[4 : 4 + count]
        acc_ref, qa_ref, da_ref = rest[4 + count :]
    else:
        qa_ref, da_ref, acc_in = rest[:3]
        dkv_refs = rest[3 : 3 + count]
        if last:
            dq_ref, acc_ref = rest[3 + count :]
        else:
            (acc_ref,) = rest[3 + count :]
        acc_ref[...] = acc_in[...]
    device = info[info.shape[0] - 1]

    def prepare(seq):
        grads = jnp.concatenate([do_ref[seq, h] for h in range(GROUP)], axis=1)
        heads_out = jnp.concatenate([o_ref[seq, h] for h in range(GROUP)], axis=1)
        delta = jnp.sum(grads.astype(f32) * heads_out.astype(f32), axis=0, keepdims=True)
        heads = [q_ref[seq, h] for h in range(GROUP)]
        qa_ref[seq, 0, 0:HEAD_DIM] = jnp.concatenate(heads, axis=1)
        qa_ref[seq, 0, HEAD_DIM:AUG] = extra_rows(
            three_pieces(-lse_ref[seq, 0]) + (jnp.ones((1, cols), f32),), cols
        )
        da_ref[seq, 0, 0:HEAD_DIM] = grads
        da_ref[seq, 0, HEAD_DIM:AUG] = extra_rows(three_pieces(-delta), cols)
        acc_ref[seq] = jnp.zeros(acc_ref.shape[1:], f32)

    def step(seq, keys, values, dkv_ref, at, block, diagonal):
        ones_key = jnp.ones((1, slots), f32)
        penalty = penalty_row(block * slots, slots, info[seq])
        key_cols = jnp.concatenate([keys, extra_rows([ones_key] * 3 + [penalty], slots)], axis=0)
        value_cols = jnp.concatenate([values, extra_rows([ones_key] * 3, slots)], axis=0)
        scores = dot(qa_ref[seq, 0], key_cols, TN) * EXP2_SCALE
        if diagonal:
            query_at = lax.broadcasted_iota(jnp.int32, (cols, slots), 0) % slots
            key_at = lax.broadcasted_iota(jnp.int32, (cols, slots), 1)
            scores = jnp.where(key_at <= query_at, scores, NEG)
        weights = jnp.exp2(scores)
        d_scores = (weights * dot(da_ref[seq, 0], value_cols, TN)).astype(bf16)
        d_value = dot(da_ref[seq, 0, 0:HEAD_DIM], weights.astype(bf16), NN)
        d_key = dot(qa_ref[seq, 0, 0:HEAD_DIM], d_scores, NN) * (HEAD_DIM ** (-0.5))
        acc_ref[seq, 0] += dot(keys, d_scores, NT)
        dkv_ref[at, 0, 0:HEAD_DIM] = d_key.astype(bf16)
        dkv_ref[at, 0, HEAD_DIM:] = d_value.astype(bf16)

    def work(seq, carry):
        if first:
            prepare(seq)
        active = block_of(device, seq, ring_size) * slots < info[seq]
        for kv_ref, dkv_ref, mask in zip(kv_refs, dkv_refs, masks):
            block = block_of(device ^ mask, seq, ring_size)
            turn = needed(device, mask, seq)
            at = seq // 2 if mask else seq

            @pl.when(turn & active)
            def _():
                keys = kv_ref[at, 0, 0:HEAD_DIM]
                step(seq, keys, kv_ref[at, 0, HEAD_DIM:], dkv_ref, at, block, mask == 0)

            @pl.when(turn & jnp.logical_not(active))
            def _():
                dkv_ref[at] = jnp.zeros(dkv_ref.shape[1:], bf16)

        if last:
            d_query = acc_ref[seq, 0] * (HEAD_DIM ** (-0.5))
            for h in range(GROUP):
                dq_ref[seq, h] = d_query[:, h * slots : (h + 1) * slots]
        return carry

    lax.fori_loop(0, qa_ref.shape[0], work, 0)


def head_spec(seqs, rows, lanes, heads=1):
    return pl.BlockSpec((seqs, heads, rows, lanes), lambda group: (0, group, 0, 0))


def kv_specs(kvs):
    return [head_spec(kv.shape[0], kv.shape[2], kv.shape[3]) for kv in kvs]


SMEM_SPEC = pl.BlockSpec(memory_space=pltpu.SMEM)
PARAMS = pltpu.CompilerParams(vmem_limit_bytes=60 * 2**20)


def call_cost(kv_shape, count, products):
    seqs, groups, _, slots = kv_shape
    pairs = seqs * groups * GROUP * slots * slots * count
    return pl.CostEstimate(
        flops=pairs * HEAD_DIM * products * 4,
        transcendentals=pairs,
        bytes_accessed=seqs * groups * count * 4 * HEAD_DIM * slots,
    )


def attend(ring_size, masks, info, queries, kvs, state, last):
    first = state is None
    groups, slots = kvs[0].shape[1], kvs[0].shape[3]
    seqs = queries.shape[0]
    cols = GROUP * slots
    wide_spec = head_spec(seqs, AUG, cols)
    row_spec = head_spec(seqs, 1, cols)
    wide_shape = (seqs, groups, AUG, cols)
    row_shape = jax.ShapeDtypeStruct((seqs, groups, 1, cols), f32)
    state_specs = [row_spec, wide_spec]
    state_shapes = [row_shape, jax.ShapeDtypeStruct(wide_shape, f32)]
    query_spec = wide_spec
    scratch = []
    if first:
        query_spec = head_spec(seqs, HEAD_DIM, slots, GROUP)
        out_specs = [wide_spec] + state_specs
        out_shape = [jax.ShapeDtypeStruct(wide_shape, bf16)] + state_shapes
    elif last:
        out_specs = [head_spec(seqs, HEAD_DIM, slots, GROUP), row_spec]
        out_shape = [jax.ShapeDtypeStruct((seqs, groups * GROUP, HEAD_DIM, slots), bf16), row_shape]
        scratch = [pltpu.VMEM((seqs, 1, 1, cols), f32), pltpu.VMEM((seqs, 1, AUG, cols), f32)]
    else:
        out_specs = state_specs
        out_shape = state_shapes
    return pl.pallas_call(
        functools.partial(forward_kernel, ring_size, masks, first, last),
        grid=(groups,),
        in_specs=[SMEM_SPEC, query_spec]
        + kv_specs(kvs)
        + ([] if first else state_specs),
        out_specs=out_specs,
        out_shape=out_shape,
        scratch_shapes=scratch,
        compiler_params=PARAMS,
        cost_estimate=call_cost(kvs[0].shape, len(masks), 4),
        name="attend",
    )(info, queries, *kvs, *([] if first else state))


def attend_back(ring_size, masks, info, kvs, operands, first, last):
    groups, slots = kvs[0].shape[1], kvs[0].shape[3]
    seqs = operands[0].shape[0]
    cols = GROUP * slots
    heads_spec = head_spec(seqs, HEAD_DIM, slots, GROUP)
    wide_spec = head_spec(seqs, AUG, cols)
    acc_spec = head_spec(seqs, HEAD_DIM, cols)
    kv_shapes = [jax.ShapeDtypeStruct(kv.shape, bf16) for kv in kvs]
    wide_shape = jax.ShapeDtypeStruct((seqs, groups, AUG, cols), bf16)
    acc_shape = jax.ShapeDtypeStruct((seqs, groups, HEAD_DIM, cols), f32)
    scratch = []
    if first:
        operand_specs = [heads_spec] * 3 + [head_spec(seqs, 1, cols)]
        out_specs = [acc_spec, wide_spec, wide_spec]
        out_shape = [acc_shape, wide_shape, wide_shape]
    else:
        operand_specs = [wide_spec, wide_spec, acc_spec]
        if last:
            out_specs = [heads_spec]
            out_shape = [jax.ShapeDtypeStruct((seqs, groups * GROUP, HEAD_DIM, slots), f32)]
            scratch = [pltpu.VMEM((seqs, 1, HEAD_DIM, cols), f32)]
        else:
            out_specs = [acc_spec]
            out_shape = [acc_shape]
    outs = pl.pallas_call(
        functools.partial(backward_kernel, ring_size, masks, first, last),
        grid=(groups,),
        in_specs=[SMEM_SPEC] + kv_specs(kvs) + operand_specs,
        out_specs=kv_specs(kvs) + out_specs,
        out_shape=kv_shapes + out_shape,
        scratch_shapes=scratch,
        compiler_params=PARAMS,
        cost_estimate=call_cost(kvs[0].shape, len(masks), 10),
        name="attend_back",
    )(info, *kvs, *operands)
    return (outs[: len(masks)], outs[len(masks) :])


def feed_forward_kernel(
    ring_size, info, scale, att_ref, tok_ref, teach_ref, wo_ref, gain_ref, w_ref,
    out_ref, dmid_ref, datt_ref, dw_ref, dwo_ref, dgain_ref, loss_ref,
    slope_ref, silu_ref, hidden_ref, dw_acc, dwo_acc,
):
    tile = pl.program_id(0)
    parts, width, hidden3 = w_ref.shape
    part = hidden3 // 3
    tile_rows = tok_ref.shape[1]
    slots = info[info.shape[0] - 2]
    device = info[info.shape[0] - 1]
    seq = tile * tile_rows // slots
    first_pos = block_of(device, seq, ring_size) * slots + tile * tile_rows % slots

    @pl.when(tile == 0)
    def _():
        dw_acc[...] = jnp.zeros(dw_acc.shape, f32)
        dwo_acc[...] = jnp.zeros(dwo_acc.shape, f32)
        dgain_ref[...] = jnp.zeros(dgain_ref.shape, f32)
        loss_ref[...] = jnp.zeros(loss_ref.shape, f32)

    gain = gain_ref[...]
    att = att_ref[0]
    middle = tok_ref[0].astype(f32) + dot(att, wo_ref[...], TN)
    inverse = lax.rsqrt(jnp.mean(middle * middle, axis=-1, keepdims=True) + EPS)
    unit = middle * inverse
    normed = (unit * gain).astype(bf16)
    branch = jnp.zeros((tile_rows, width), f32)
    for t in range(parts):
        both = dot(normed, w_ref[t, :, : 2 * part], NN)
        gate = both[:, :part]
        up = both[:, part:]
        sigmoid = jax.nn.sigmoid(gate)
        silu = gate * sigmoid
        hidden = (silu * up).astype(bf16)
        slope_ref[t] = up * sigmoid * (1.0 + gate * (1.0 - sigmoid))
        silu_ref[t] = silu
        hidden_ref[t] = hidden
        branch = branch + dot(hidden, w_ref[t, :, 2 * part :], NT)
    result = middle + branch
    out_ref[0] = result
    row_pos = first_pos + lax.broadcasted_iota(jnp.int32, (tile_rows, 1), 0)
    valid = (row_pos < info[seq]).astype(f32)
    mismatch = valid * (result - teach_ref[0].astype(f32))
    loss_ref[...] += jnp.sum(mismatch * mismatch)
    d_result = mismatch * scale[0]
    d_branch = d_result.astype(bf16)
    d_normed = jnp.zeros((tile_rows, width), f32)
    for t in range(parts):
        d_hidden = dot(d_branch, w_ref[t, :, 2 * part :], NN)
        d_both = jnp.concatenate([d_hidden * slope_ref[t], d_hidden * silu_ref[t]], axis=1)
        d_both = d_both.astype(bf16)
        dw_acc[t, :, : 2 * part] += dot(normed, d_both, TN)
        dw_acc[t, :, 2 * part :] += dot(d_branch, hidden_ref[t], TN)
        d_normed = d_normed + dot(d_both, w_ref[t, :, : 2 * part], NT)
    dgain_ref[...] += jnp.sum(d_normed * unit, axis=0, keepdims=True)
    d_unit = d_normed * gain
    d_middle = d_result + inverse * (d_unit - unit * jnp.mean(d_unit * unit, axis=-1, keepdims=True))
    dmid_ref[0] = d_middle
    d_attn = d_middle.astype(bf16)
    datt_ref[0] = dot(wo_ref[...], d_attn, NT).astype(bf16)
    dwo_acc[...] += dot(att, d_attn, NN)

    @pl.when(tile == pl.num_programs(0) - 1)
    def _():
        dw_ref[...] = dw_acc[...].astype(bf16)
        dwo_ref[...] = jnp.zeros(dwo_ref.shape, bf16)
        dwo_ref[:, :width] = dwo_acc[...].astype(bf16)


def feed_forward(ring_size, info, scale, attended_t, tokens, teacher, w_o, gain, weights, out_width):
    seqs, slots, width = tokens.shape
    parts, _, hidden3 = weights.shape
    part = hidden3 // 3
    tile_rows = min(512, slots)
    per_seq = slots // tile_rows
    row_spec = pl.BlockSpec((1, tile_rows, width), lambda i: (i // per_seq, i % per_seq, 0))
    col_spec = pl.BlockSpec((1, width, tile_rows), lambda i: (i // per_seq, 0, i % per_seq))

    def whole(*shape):
        return pl.BlockSpec(shape, lambda i: (0,) * len(shape), pipeline_mode=pl.Buffered(1))

    def kept(*shape):
        return pl.BlockSpec(shape, lambda i: (0,) * len(shape))

    rows = seqs * slots
    return pl.pallas_call(
        functools.partial(feed_forward_kernel, ring_size),
        grid=(seqs * per_seq,),
        in_specs=[SMEM_SPEC, SMEM_SPEC, col_spec, row_spec, row_spec]
        + [whole(width, width), whole(1, width), whole(parts, width, hidden3)],
        out_specs=[row_spec, row_spec, col_spec]
        + [kept(parts, width, hidden3), kept(width, out_width), kept(1, width), kept(1, 128)],
        out_shape=[
            jax.ShapeDtypeStruct((seqs, slots, width), f32),
            jax.ShapeDtypeStruct((seqs, slots, width), f32),
            jax.ShapeDtypeStruct((seqs, width, slots), bf16),
            jax.ShapeDtypeStruct((parts, width, hidden3), bf16),
            jax.ShapeDtypeStruct((width, out_width), bf16),
            jax.ShapeDtypeStruct((1, width), f32),
            jax.ShapeDtypeStruct((1, 128), f32),
        ],
        scratch_shapes=[
            pltpu.VMEM((parts, tile_rows, part), f32),
            pltpu.VMEM((parts, tile_rows, part), f32),
            pltpu.VMEM((parts, tile_rows, part), bf16),
            pltpu.VMEM((parts, width, hidden3), f32),
            pltpu.VMEM((width, width), f32),
        ],
        compiler_params=PARAMS,
        cost_estimate=pl.CostEstimate(
            flops=6 * rows * width * (parts * hidden3 + width),
            transcendentals=rows * parts * part,
            bytes_accessed=rows * width * 20 + parts * width * hidden3 * 4,
        ),
        name="feed_forward",
    )(info, scale, attended_t, tokens, teacher, w_o, gain, weights)


RING = ("ctx", "tp")


def swap(value, mask):
    size = lax.axis_size(RING)
    return lax.ppermute(value, RING, [(i, i ^ mask) for i in range(size)])


def mirror(value):
    size = lax.axis_size(RING)
    return lax.ppermute(value, RING, [(i, size - 1 - i) for i in range(size)])


def mirror_odd(value):
    moved = mirror(value[1::2])
    seqs = value.shape[0]
    return jnp.concatenate(
        [moved[s // 2][None] if s % 2 else value[s][None] for s in range(seqs)], axis=0
    )


def move_back(value):
    moved = mirror(value[1::2].astype(bf16)).astype(f32)
    seqs = value.shape[0]
    return jnp.concatenate(
        [moved[s // 2][None] if s % 2 else value[s][None] for s in range(seqs)], axis=0
    )


def add_low(*parts):
    total = parts[0].astype(f32)
    for part in parts[1:]:
        total = total + part.astype(f32)
    return total.astype(bf16)


def gather_fsdp(value):
    if lax.axis_size("fsdp") != 2:
        return lax.all_gather(value, "fsdp", axis=0, tiled=False)
    other = lax.ppermute(value, "fsdp", [(0, 1), (1, 0)])
    at_zero = lax.axis_index("fsdp") == 0
    return jnp.stack([jnp.where(at_zero, value, other), jnp.where(at_zero, other, value)])


def pick_half(value, axis, index):
    half = value.shape[axis] // 2
    return lax.dynamic_slice_in_dim(value, index * half, half, axis)


def join_halves(mine, other, axis, index):
    return jnp.where(
        index == 0,
        jnp.concatenate([mine, other], axis=axis),
        jnp.concatenate([other, mine], axis=axis),
    )


def reduce_steps(value, own):
    fsdp_size, rows, columns = value.shape
    outer = lax.axis_size(RING) // 4
    core = own % 2
    column = (own // 2) % 2
    plane = own // 4
    value = value.astype(bf16)
    value = add_low(pick_half(value, 2, core), swap(pick_half(value, 2, 1 - core), 1))
    value = yield value
    if fsdp_size == 2:
        here = lax.axis_index("fsdp")
        away = lax.dynamic_index_in_dim(value, 1 - here, 0, False)
        mine = lax.dynamic_index_in_dim(value, here, 0, False)
        value = add_low(mine, lax.ppermute(away, "fsdp", [(0, 1), (1, 0)]))
    else:
        value = lax.psum_scatter(value, "fsdp", scatter_dimension=0, tiled=False)
    value = yield value
    value = add_low(pick_half(value, 1, column), swap(pick_half(value, 1, 1 - column), 2))
    value = yield value
    piece = rows // outer

    def rows_of(index):
        return lax.dynamic_slice_in_dim(value, index * piece, piece, 0)

    mine = add_low(
        rows_of(plane), *[swap(rows_of(plane ^ k), 4 * k) for k in range(1, outer)]
    )
    mine = yield mine
    whole = jnp.zeros((rows, columns // 4), bf16)
    whole = lax.dynamic_update_slice_in_dim(whole, mine, plane * piece, 0)
    for k in range(1, outer):
        whole = lax.dynamic_update_slice_in_dim(whole, swap(mine, 4 * k), (plane ^ k) * piece, 0)
    whole = yield whole
    whole = join_halves(whole, swap(whole, 2), 1, column)
    whole = yield whole
    yield join_halves(whole, swap(whole, 1), 1, core).astype(f32)


def sum_steps(value):
    mask = 1
    while mask < lax.axis_size(RING):
        value = yield value + swap(value, mask)
        mask *= 2
    if lax.axis_size("fsdp") == 2:
        value = value + lax.ppermute(value, "fsdp", [(0, 1), (1, 0)])
    else:
        value = lax.psum(value, "fsdp")
    yield value


def advance(steps, value):
    try:
        return steps.send(value)
    except StopIteration:
        return value


def run_steps(steps, value=None):
    while True:
        try:
            value = steps.send(value)
        except StopIteration:
            return value


def shards(
    tokens,
    teacher,
    lengths,
    gain_one,
    w_query,
    w_key,
    w_value,
    w_out,
    gain_two,
    w_gate,
    w_up,
    w_down,
):
    seqs, slots, width = tokens.shape
    kv_width = KV_HEADS * HEAD_DIM
    qkv_width = width + 2 * kv_width
    gain_at = qkv_width
    pack_width = -(-(gain_at + 2) // 128) * 128
    grad_width = -(-(qkv_width + 2) // 512) * 512
    half = w_query.shape[0]
    hidden_part = w_gate.shape[1]
    fsdp_size = lax.axis_size("fsdp")
    tp_size = lax.axis_size("tp")
    ring_size = lax.axis_size(RING)
    outer = ring_size // 4

    tokens_here = mirror_odd(tokens)
    count_total = jnp.sum(gather_fsdp(lengths)).astype(f32)
    packed = jnp.concatenate(
        [
            w_query,
            w_key,
            w_value,
            gain_one[:, None],
            gain_two[:, None],
            jnp.zeros((half, pack_width - gain_at - 2), bf16),
        ],
        axis=1,
    )
    packed = gather_fsdp(packed)
    packed = packed.reshape(width, pack_width)
    w_qkv = packed[:, :qkv_width]
    g_one = packed[:, gain_at].astype(f32)
    g_two = packed[:, gain_at + 1].astype(f32)
    ffn_pack = jnp.concatenate([w_gate, w_up, w_down.T], axis=1)

    own = lax.axis_index(RING).astype(jnp.int32)
    blocks = jnp.stack([block_of(own, s, ring_size) for s in range(seqs)])
    positions = blocks[:, None] * slots + jnp.arange(slots, dtype=jnp.int32)[None]
    cosine, sine = rope_tables(positions)
    info = jnp.concatenate([lengths.astype(jnp.int32), own[None]])

    inputs = tokens_here.astype(f32)
    normed = norm_rows(inputs, g_one).astype(bf16)
    qkv = jnp.einsum("df,sld->sfl", w_qkv, normed, preferred_element_type=f32)
    qk = qkv[:, : width + kv_width].reshape(seqs, HEADS + KV_HEADS, HEAD_DIM, slots)
    qk = rotate_cols(qk, cosine, sine).astype(bf16)
    queries = qk[:, :HEADS]
    values = qkv[:, width + kv_width :].astype(bf16).reshape(seqs, KV_HEADS, HEAD_DIM, slots)

    kv = {0: jnp.concatenate([qk[:, HEADS:], values], axis=2)}

    def outgoing(mask):
        return jnp.where(own < (own ^ mask), kv[0][0::2], kv[0][1::2])

    coming = {mask: swap(outgoing(mask), mask) for mask in [1, 2] + [4 * k for k in range(1, outer)]}
    calls = [(0,), (1, 2, 4)]
    for k in range(1, outer - 1):
        calls.append((4 * k - 1, 4 * k + 1, 4 * k + 2, 4 * k + 4))
    calls.append((4 * outer - 5, 4 * outer - 3, 4 * outer - 2, 4 * outer - 1))
    query_rows, *state = attend(ring_size, calls[0], info, queries, [kv[0]], None, False)
    for number, masks in enumerate(calls[1:], 1):
        if masks[-1] not in coming:
            coming[masks[-1]] = swap(coming[masks[-1] - 1], 1)
        later = [ffn_pack] if number == 1 else [w_out, teacher] if number == 2 else []
        *arrived, first_state = lax.optimization_barrier(
            [coming[m] for m in masks] + later + [state[0]]
        )
        if number == 1:
            ffn_all = lax.all_gather(arrived.pop(), ("tp", "fsdp"), axis=0, tiled=False)
            ffn_all = ffn_all.reshape(tp_size, width, 3 * hidden_part)
        if number == 2:
            teacher_here = mirror_odd(arrived.pop())
            w_o = gather_fsdp(arrived.pop()).reshape(width, width)
        kv.update(zip(masks, arrived))
        state = [first_state, state[1]]
        for mask in masks:
            if mask % 4 == 0:
                coming[mask + 2] = swap(kv[mask], 2)
                coming[mask + 1] = swap(kv[mask], 1)
            elif mask % 4 == 2 and mask + 1 not in coming:
                coming[mask + 1] = swap(kv[mask], 1)
        state = attend(
            ring_size, masks, info, query_rows, arrived, state, number == len(calls) - 1
        )
    attended, lse = state
    attended_t = attended.reshape(seqs, width, slots)

    slots_all = seqs * fsdp_size * slots * ring_size
    scale = (slots_all / count_total)[None]
    out_width = -(-width // 512) * 512
    tile_info = jnp.concatenate([lengths.astype(jnp.int32), jnp.full((1,), slots, jnp.int32), own[None]])
    result, d_middle, d_attended_t, d_ffn, d_out_w, d_gain_two, squared_part = feed_forward(
        ring_size, tile_info, scale, attended_t, tokens_here, teacher_here, w_o, g_two[None],
        ffn_all, out_width
    )
    d_attended_t = d_attended_t.reshape(seqs, HEADS, HEAD_DIM, slots)
    d_ffn = d_ffn.reshape(tp_size * fsdp_size, half, 3 * hidden_part)
    d_ffn = lax.psum_scatter(d_ffn, ("tp", "fsdp"), scatter_dimension=0, tiled=False)
    d_out_w = d_out_w.reshape(fsdp_size, half, out_width)
    output = move_back(result)
    out_steps = reduce_steps(d_out_w, own)
    loss_steps = sum_steps(squared_part)
    d_out_w = next(out_steps)
    loss_sum = next(loss_steps)

    calls = [(4 * outer - 2, 4 * outer - 1)]
    for k in reversed(range(1, outer)):
        calls.append((4 * k, 4 * k + 1, 4 * k - 2, 4 * k - 1))
    calls.append((0, 1))
    operands = [queries, d_attended_t, attended, lse]
    core_sums = {}
    sums = {}
    d_kv_terms = []
    for number, masks in enumerate(calls):
        last = number == len(calls) - 1
        if number:
            if number >= 2:
                due = list(calls[number - 2][::2])
            else:
                due = []
            held = [core_sums[m] for m in due] + [d_out_w, loss_sum]
            if number == 2:
                held.append(output)
            if number == 3:
                held.append(d_ffn)
            held = list(lax.optimization_barrier([info] + held))
            info = held.pop(0)
            if number == 3:
                d_ffn = lax.psum(held.pop(), "ctx")
            if number == 2:
                output = held.pop()
            loss_sum = advance(loss_steps, held.pop())
            d_out_w = advance(out_steps, held.pop())
            for mask, value in zip(due, held):
                core_sums[mask] = value
                if mask % 4:
                    sums[mask - 2] = swap(value, 2)
                else:
                    d_kv_terms.append((mask, swap(add_low(value, sums[mask]), mask)))
        parts, outs = attend_back(
            ring_size, masks, info, [kv[m] for m in masks], operands, number == 0, last
        )
        parts = list(parts)
        for place in range(0, 0 if last else len(masks), 2):
            core_sums[masks[place]] = add_low(parts[place], swap(parts[place + 1], 1))
        if number == 0:
            operands = [outs[1], outs[2], outs[0]]
        else:
            operands = operands[:2] + [outs[0]]
    d_query = outs[0]
    for mask in calls[-2][::2]:
        if mask % 4:
            sums[mask - 2] = swap(core_sums[mask], 2)
        else:
            d_kv_terms.append((mask, swap(add_low(core_sums[mask], sums[mask]), mask)))
    d_kv_terms += [(2, sums[0]), (1, swap(parts[1], 1))]
    d_ffn, parts[0] = lax.optimization_barrier((d_ffn, parts[0]))
    d_kv_halves = []
    for parity in range(2):
        total = parts[0][parity::2].astype(f32)
        for mask, term in d_kv_terms:
            from_it = (own > (own ^ mask)) == (parity == 1)
            total = total + jnp.where(from_it, term.astype(f32), 0.0)
        d_kv_halves.append(total)
    d_kv = jnp.stack(d_kv_halves, axis=1).reshape((seqs,) + parts[0].shape[1:])
    loss_sum = run_steps(loss_steps, loss_sum)
    loss_value = loss_sum[0, 0] / (count_total * width)
    d_out_w = run_steps(out_steps, d_out_w)
    d_ffn = d_ffn.astype(f32)

    d_qk = jnp.concatenate([d_query, d_kv[:, :, :HEAD_DIM]], axis=1)
    d_qk = rotate_cols(d_qk, cosine, -sine).astype(bf16).reshape(seqs, width + kv_width, slots)
    d_values = d_kv[:, :, HEAD_DIM:].astype(bf16).reshape(seqs, kv_width, slots)
    d_qkv = jnp.concatenate([d_qk, d_values], axis=1)
    d_normed = jnp.einsum("sfl,df->sld", d_qkv, w_qkv, preferred_element_type=f32)
    d_qkv_w = jnp.einsum("sld,sfl->df", normed, d_qkv, preferred_element_type=f32)
    norm_one_pull = jax.vjp(norm_rows, inputs, g_one)[1]
    d_inputs_norm, d_gain_one = norm_one_pull(d_normed)
    tokens_grad = d_middle + d_inputs_norm
    back = tokens_grad[1::2].astype(bf16)
    cut = 2 * width // 3 // 128 * 128
    back_parts = [mirror(back[..., :cut]), back[..., cut:]]
    d_packed = jnp.concatenate(
        [
            d_qkv_w,
            d_gain_one[:, None],
            d_gain_two.T,
            jnp.zeros((width, grad_width - qkv_width - 2), f32),
        ],
        axis=1,
    )
    steps = reduce_steps(d_packed.reshape(fsdp_size, half, grad_width), own)
    d_packed = next(steps)
    d_packed = steps.send(d_packed)
    d_packed = steps.send(d_packed)
    back_parts[0], d_packed = lax.optimization_barrier((back_parts[0], d_packed))
    d_packed = steps.send(d_packed)
    d_packed = steps.send(d_packed)
    back_parts[1], d_packed = lax.optimization_barrier((back_parts[1], d_packed))
    back = jnp.concatenate([back_parts[0], mirror(back_parts[1])], axis=2).astype(f32)
    tokens_grad = jnp.stack([tokens_grad[0::2], back], axis=1).reshape(tokens_grad.shape)
    d_packed = run_steps(steps, d_packed)
    return (
        output,
        loss_value,
        tokens_grad,
        d_packed[:, qkv_width],
        d_packed[:, :width],
        d_packed[:, width : width + kv_width],
        d_packed[:, width + kv_width : qkv_width],
        d_out_w[:, :width],
        d_packed[:, qkv_width + 1],
        d_ffn[:, :hidden_part],
        d_ffn[:, hidden_part : 2 * hidden_part],
        d_ffn[:, 2 * hidden_part :].T,
    )


def solution(mesh):
    slots_spec = P("fsdp", ("ctx", "tp"), None)
    rows_spec = P("fsdp", None)
    return jax.shard_map(
        shards,
        mesh=mesh,
        in_specs=(
            slots_spec,
            slots_spec,
            P("fsdp"),
            P("fsdp"),
            rows_spec,
            rows_spec,
            rows_spec,
            rows_spec,
            P("fsdp"),
            P("fsdp", "tp"),
            P("fsdp", "tp"),
            P("tp", "fsdp"),
        ),
        out_specs=(
            slots_spec,
            P(),
            slots_spec,
            P("fsdp"),
            rows_spec,
            rows_spec,
            rows_spec,
            rows_spec,
            P("fsdp"),
            P("fsdp", "tp"),
            P("fsdp", "tp"),
            P("tp", "fsdp"),
        ),
        check_vma=False,
    )
```

```python
import functools

import jax
import jax.numpy as jnp
from jax import lax
from jax.experimental import pallas as pl
from jax.experimental.pallas import tpu as pltpu
from jax.sharding import PartitionSpec as P

HEADS = 9
KV_HEADS = 3
GROUP = HEADS // KV_HEADS
HEAD_DIM = 64
AUG = HEAD_DIM + 16

EPS = 1e-05
ROPE_BASE = 10000.0
NEG = -1e30
LOG2E = 1.4426950408889634
EXP2_SCALE = LOG2E * HEAD_DIM ** (-0.5)

f32 = jnp.float32
bf16 = jnp.bfloat16
NN = ((1,), (0,))
TN = ((0,), (0,))
NT = ((1,), (1,))


def dot(left, right, dims):
    return lax.dot_general(left, right, (dims, ((), ())), preferred_element_type=f32)


def norm_rows(values, gain):
    return values * lax.rsqrt(jnp.mean(values * values, axis=-1, keepdims=True) + EPS) * gain


def rope_tables(positions):
    half_width = HEAD_DIM // 2
    frequency = ROPE_BASE ** (-(jnp.arange(half_width, dtype=f32) * 2.0) / HEAD_DIM)
    angles = frequency[None, None, :, None] * positions.astype(f32)[:, None, None, :]
    return (jnp.cos(angles), jnp.sin(angles))


def rotate_cols(values, cosine, sine):
    half_width = HEAD_DIM // 2
    lower = values[..., :half_width, :]
    upper = values[..., half_width:, :]
    return jnp.concatenate([lower * cosine - upper * sine, upper * cosine + lower * sine], axis=-2)


def three_pieces(row):
    first = row.astype(bf16)
    rest = row - first.astype(f32)
    second = rest.astype(bf16)
    third = (rest - second.astype(f32)).astype(bf16)
    return (first, second, third)


def penalty_row(block_start, width, length):
    key_pos = block_start + lax.broadcasted_iota(jnp.int32, (1, width), 1)
    return jnp.where(key_pos < length, 0.0, NEG).astype(bf16)


def extra_rows(rows, width):
    wide = jnp.zeros((16, width), f32)
    index = lax.broadcasted_iota(jnp.int32, (16, width), 0)
    for place, row in enumerate(rows):
        wide = jnp.where(index == place, row.astype(f32), wide)
    return wide.astype(bf16)


def block_of(device, seq, ring_size):
    return jnp.where(seq % 2 == 1, ring_size - 1 - device, device)


def needed(device, mask, seq):
    if mask == 0:
        return seq >= 0
    return (device ^ mask > device) == (seq % 2 == 1)


def forward_kernel(ring_size, masks, first, last, *refs):
    count = len(masks)
    info, q_ref = refs[:2]
    kv_refs = refs[2 : 2 + count]
    rest = refs[2 + count :]
    slots = kv_refs[0].shape[-1]
    cols = GROUP * slots
    if first:
        qa_ref, max_ref, acc_ref = rest
    else:
        qa_ref = q_ref
        if last:
            max_in, acc_in, out_ref, lse_ref, max_ref, acc_ref = rest
        else:
            max_in, acc_in, max_ref, acc_ref = rest
        max_ref[...] = max_in[...]
        acc_ref[...] = acc_in[...]
    device = info[info.shape[0] - 1]

    def step(seq, keys, values, block, diagonal):
        key_cols = jnp.concatenate(
            [keys, extra_rows([penalty_row(block * slots, slots, info[seq])], slots)], axis=0
        )
        value_ones = extra_rows([jnp.ones((1, slots), f32)], slots)
        value_cols = jnp.concatenate([values, value_ones], axis=0)
        scores = dot(key_cols, qa_ref[seq, 0], TN) * EXP2_SCALE
        if diagonal:
            key_at = lax.broadcasted_iota(jnp.int32, (slots, cols), 0)
            query_at = lax.broadcasted_iota(jnp.int32, (slots, cols), 1) % slots
            scores = jnp.where(key_at <= query_at, scores, NEG)
        old_max = max_ref[seq, 0]
        new_max = jnp.maximum(old_max, jnp.max(scores, axis=0, keepdims=True))
        weights = jnp.exp2(scores - new_max).astype(bf16)
        max_ref[seq, 0] = new_max
        acc_ref[seq, 0] = acc_ref[seq, 0] * jnp.exp2(old_max - new_max) + dot(value_cols, weights, NN)

    def work(seq, carry):
        if first:
            heads = [q_ref[seq, h] for h in range(GROUP)]
            qa_ref[seq, 0, 0:HEAD_DIM] = jnp.concatenate(heads, axis=1)
            qa_ref[seq, 0, HEAD_DIM:AUG] = extra_rows([jnp.ones((1, cols), f32)], cols)
            max_ref[seq] = jnp.full(max_ref.shape[1:], NEG, f32)
            acc_ref[seq] = jnp.zeros(acc_ref.shape[1:], f32)
        for kv_ref, mask in zip(kv_refs, masks):
            block = block_of(device ^ mask, seq, ring_size)
            at = seq // 2 if mask else seq

            @pl.when(needed(device, mask, seq) & (block * slots < info[seq]))
            def _():
                keys = kv_ref[at, 0, 0:HEAD_DIM]
                step(seq, keys, kv_ref[at, 0, HEAD_DIM:], block, mask == 0)

        if last:
            total = acc_ref[seq, 0, HEAD_DIM : HEAD_DIM + 1]
            heads_out = acc_ref[seq, 0, 0:HEAD_DIM] / total
            lse_ref[seq, 0] = (max_ref[seq, 0] + jnp.log2(total)) * (1.0 / EXP2_SCALE)
            for h in range(GROUP):
                out_ref[seq, h] = heads_out[:, h * slots : (h + 1) * slots].astype(bf16)
        return carry

    lax.fori_loop(0, qa_ref.shape[0], work, 0)


def backward_kernel(ring_size, masks, first, last, *refs):
    count = len(masks)
    info = refs[0]
    kv_refs = refs[1 : 1 + count]
    rest = refs[1 + count :]
    slots = kv_refs[0].shape[-1]
    cols = GROUP * slots
    if first:
        q_ref, do_ref, o_ref, lse_ref = rest[:4]
        dkv_refs = rest[4 : 4 + count]
        acc_ref, qa_ref, da_ref = rest[4 + count :]
    else:
        qa_ref, da_ref, acc_in = rest[:3]
        dkv_refs = rest[3 : 3 + count]
        if last:
            dq_ref, acc_ref = rest[3 + count :]
        else:
            (acc_ref,) = rest[3 + count :]
        acc_ref[...] = acc_in[...]
    device = info[info.shape[0] - 1]

    def prepare(seq):
        grads = jnp.concatenate([do_ref[seq, h] for h in range(GROUP)], axis=1)
        heads_out = jnp.concatenate([o_ref[seq, h] for h in range(GROUP)], axis=1)
        delta = jnp.sum(grads.astype(f32) * heads_out.astype(f32), axis=0, keepdims=True)
        heads = [q_ref[seq, h] for h in range(GROUP)]
        qa_ref[seq, 0, 0:HEAD_DIM] = jnp.concatenate(heads, axis=1)
        qa_ref[seq, 0, HEAD_DIM:AUG] = extra_rows(
            three_pieces(-lse_ref[seq, 0]) + (jnp.ones((1, cols), f32),), cols
        )
        da_ref[seq, 0, 0:HEAD_DIM] = grads
        da_ref[seq, 0, HEAD_DIM:AUG] = extra_rows(three_pieces(-delta), cols)
        acc_ref[seq] = jnp.zeros(acc_ref.shape[1:], f32)

    def step(seq, keys, values, dkv_ref, at, block, diagonal):
        ones_key = jnp.ones((1, slots), f32)
        penalty = penalty_row(block * slots, slots, info[seq])
        key_cols = jnp.concatenate([keys, extra_rows([ones_key] * 3 + [penalty], slots)], axis=0)
        value_cols = jnp.concatenate([values, extra_rows([ones_key] * 3, slots)], axis=0)
        scores = dot(qa_ref[seq, 0], key_cols, TN) * EXP2_SCALE
        if diagonal:
            query_at = lax.broadcasted_iota(jnp.int32, (cols, slots), 0) % slots
            key_at = lax.broadcasted_iota(jnp.int32, (cols, slots), 1)
            scores = jnp.where(key_at <= query_at, scores, NEG)
        weights = jnp.exp2(scores)
        d_scores = (weights * dot(da_ref[seq, 0], value_cols, TN)).astype(bf16)
        d_value = dot(da_ref[seq, 0, 0:HEAD_DIM], weights.astype(bf16), NN)
        d_key = dot(qa_ref[seq, 0, 0:HEAD_DIM], d_scores, NN) * (HEAD_DIM ** (-0.5))
        acc_ref[seq, 0] += dot(keys, d_scores, NT)
        dkv_ref[at, 0, 0:HEAD_DIM] = d_key.astype(bf16)
        dkv_ref[at, 0, HEAD_DIM:] = d_value.astype(bf16)

    def work(seq, carry):
        if first:
            prepare(seq)
        active = block_of(device, seq, ring_size) * slots < info[seq]
        for kv_ref, dkv_ref, mask in zip(kv_refs, dkv_refs, masks):
            block = block_of(device ^ mask, seq, ring_size)
            turn = needed(device, mask, seq)
            at = seq // 2 if mask else seq

            @pl.when(turn & active)
            def _():
                keys = kv_ref[at, 0, 0:HEAD_DIM]
                step(seq, keys, kv_ref[at, 0, HEAD_DIM:], dkv_ref, at, block, mask == 0)

            @pl.when(turn & jnp.logical_not(active))
            def _():
                dkv_ref[at] = jnp.zeros(dkv_ref.shape[1:], bf16)

        if last:
            d_query = acc_ref[seq, 0] * (HEAD_DIM ** (-0.5))
            for h in range(GROUP):
                dq_ref[seq, h] = d_query[:, h * slots : (h + 1) * slots]
        return carry

    lax.fori_loop(0, qa_ref.shape[0], work, 0)


def head_spec(seqs, rows, lanes, heads=1):
    return pl.BlockSpec((seqs, heads, rows, lanes), lambda group: (0, group, 0, 0))


def kv_specs(kvs):
    return [head_spec(kv.shape[0], kv.shape[2], kv.shape[3]) for kv in kvs]


SMEM_SPEC = pl.BlockSpec(memory_space=pltpu.SMEM)
PARAMS = pltpu.CompilerParams(vmem_limit_bytes=60 * 2**20)


def call_cost(kv_shape, count, products):
    seqs, groups, _, slots = kv_shape
    pairs = seqs * groups * GROUP * slots * slots * count
    return pl.CostEstimate(
        flops=pairs * HEAD_DIM * products * 4,
        transcendentals=pairs,
        bytes_accessed=seqs * groups * count * 4 * HEAD_DIM * slots,
    )


def attend(ring_size, masks, info, queries, kvs, state, last):
    first = state is None
    groups, slots = kvs[0].shape[1], kvs[0].shape[3]
    seqs = queries.shape[0]
    cols = GROUP * slots
    wide_spec = head_spec(seqs, AUG, cols)
    row_spec = head_spec(seqs, 1, cols)
    wide_shape = (seqs, groups, AUG, cols)
    row_shape = jax.ShapeDtypeStruct((seqs, groups, 1, cols), f32)
    state_specs = [row_spec, wide_spec]
    state_shapes = [row_shape, jax.ShapeDtypeStruct(wide_shape, f32)]
    query_spec = wide_spec
    scratch = []
    if first:
        query_spec = head_spec(seqs, HEAD_DIM, slots, GROUP)
        out_specs = [wide_spec] + state_specs
        out_shape = [jax.ShapeDtypeStruct(wide_shape, bf16)] + state_shapes
    elif last:
        out_specs = [head_spec(seqs, HEAD_DIM, slots, GROUP), row_spec]
        out_shape = [jax.ShapeDtypeStruct((seqs, groups * GROUP, HEAD_DIM, slots), bf16), row_shape]
        scratch = [pltpu.VMEM((seqs, 1, 1, cols), f32), pltpu.VMEM((seqs, 1, AUG, cols), f32)]
    else:
        out_specs = state_specs
        out_shape = state_shapes
    return pl.pallas_call(
        functools.partial(forward_kernel, ring_size, masks, first, last),
        grid=(groups,),
        in_specs=[SMEM_SPEC, query_spec]
        + kv_specs(kvs)
        + ([] if first else state_specs),
        out_specs=out_specs,
        out_shape=out_shape,
        scratch_shapes=scratch,
        compiler_params=PARAMS,
        cost_estimate=call_cost(kvs[0].shape, len(masks), 4),
        name="attend",
    )(info, queries, *kvs, *([] if first else state))


def attend_back(ring_size, masks, info, kvs, operands, first, last):
    groups, slots = kvs[0].shape[1], kvs[0].shape[3]
    seqs = operands[0].shape[0]
    cols = GROUP * slots
    heads_spec = head_spec(seqs, HEAD_DIM, slots, GROUP)
    wide_spec = head_spec(seqs, AUG, cols)
    acc_spec = head_spec(seqs, HEAD_DIM, cols)
    kv_shapes = [jax.ShapeDtypeStruct(kv.shape, bf16) for kv in kvs]
    wide_shape = jax.ShapeDtypeStruct((seqs, groups, AUG, cols), bf16)
    acc_shape = jax.ShapeDtypeStruct((seqs, groups, HEAD_DIM, cols), f32)
    scratch = []
    if first:
        operand_specs = [heads_spec] * 3 + [head_spec(seqs, 1, cols)]
        out_specs = [acc_spec, wide_spec, wide_spec]
        out_shape = [acc_shape, wide_shape, wide_shape]
    else:
        operand_specs = [wide_spec, wide_spec, acc_spec]
        if last:
            out_specs = [heads_spec]
            out_shape = [jax.ShapeDtypeStruct((seqs, groups * GROUP, HEAD_DIM, slots), f32)]
            scratch = [pltpu.VMEM((seqs, 1, HEAD_DIM, cols), f32)]
        else:
            out_specs = [acc_spec]
            out_shape = [acc_shape]
    outs = pl.pallas_call(
        functools.partial(backward_kernel, ring_size, masks, first, last),
        grid=(groups,),
        in_specs=[SMEM_SPEC] + kv_specs(kvs) + operand_specs,
        out_specs=kv_specs(kvs) + out_specs,
        out_shape=kv_shapes + out_shape,
        scratch_shapes=scratch,
        compiler_params=PARAMS,
        cost_estimate=call_cost(kvs[0].shape, len(masks), 10),
        name="attend_back",
    )(info, *kvs, *operands)
    return (outs[: len(masks)], outs[len(masks) :])


def feed_forward_kernel(
    ring_size, info, scale, att_ref, tok_ref, teach_ref, wo_ref, gain_ref, w_ref,
    out_ref, dmid_ref, datt_ref, dw_ref, dgain_ref, loss_ref,
    slope_ref, silu_ref, hidden_ref, dw_acc, dwo_acc,
):
    tile = pl.program_id(0)
    parts, width, hidden3 = w_ref.shape
    part = hidden3 // 3
    tile_rows = tok_ref.shape[1]
    slots = info[info.shape[0] - 2]
    device = info[info.shape[0] - 1]
    seq = tile * tile_rows // slots
    first_pos = block_of(device, seq, ring_size) * slots + tile * tile_rows % slots

    @pl.when(tile == 0)
    def _():
        dw_acc[...] = jnp.zeros(dw_acc.shape, f32)
        dwo_acc[...] = jnp.zeros(dwo_acc.shape, f32)
        dgain_ref[...] = jnp.zeros(dgain_ref.shape, f32)
        loss_ref[...] = jnp.zeros(loss_ref.shape, f32)

    gain = gain_ref[...]
    att = att_ref[0]
    middle = tok_ref[0].astype(f32) + dot(att, wo_ref[...], TN)
    inverse = lax.rsqrt(jnp.mean(middle * middle, axis=-1, keepdims=True) + EPS)
    unit = middle * inverse
    normed = (unit * gain).astype(bf16)
    branch = jnp.zeros((tile_rows, width), f32)
    for t in range(parts):
        both = dot(normed, w_ref[t, :, : 2 * part], NN)
        gate = both[:, :part]
        up = both[:, part:]
        sigmoid = jax.nn.sigmoid(gate)
        silu = gate * sigmoid
        hidden = (silu * up).astype(bf16)
        slope_ref[t] = up * sigmoid * (1.0 + gate * (1.0 - sigmoid))
        silu_ref[t] = silu
        hidden_ref[t] = hidden
        branch = branch + dot(hidden, w_ref[t, :, 2 * part :], NT)
    result = middle + branch
    out_ref[0] = result
    row_pos = first_pos + lax.broadcasted_iota(jnp.int32, (tile_rows, 1), 0)
    valid = (row_pos < info[seq]).astype(f32)
    mismatch = valid * (result - teach_ref[0].astype(f32))
    loss_ref[...] += jnp.sum(mismatch * mismatch)
    d_result = mismatch * scale[0]
    d_branch = d_result.astype(bf16)
    d_normed = jnp.zeros((tile_rows, width), f32)
    for t in range(parts):
        d_hidden = dot(d_branch, w_ref[t, :, 2 * part :], NN)
        d_both = jnp.concatenate([d_hidden * slope_ref[t], d_hidden * silu_ref[t]], axis=1)
        d_both = d_both.astype(bf16)
        dw_acc[t, :, : 2 * part] += dot(normed, d_both, TN)
        dw_acc[t, :, 2 * part :] += dot(d_branch, hidden_ref[t], TN)
        d_normed = d_normed + dot(d_both, w_ref[t, :, : 2 * part], NT)
    dgain_ref[...] += jnp.sum(d_normed * unit, axis=0, keepdims=True)
    d_unit = d_normed * gain
    d_middle = d_result + inverse * (d_unit - unit * jnp.mean(d_unit * unit, axis=-1, keepdims=True))
    dmid_ref[0] = d_middle
    d_attn = d_middle.astype(bf16)
    datt_ref[0] = dot(wo_ref[...], d_attn, NT).astype(bf16)
    dwo_acc[...] += dot(att, d_attn, NN)

    @pl.when(tile == pl.num_programs(0) - 1)
    def _():
        dw_ref[:, :, :hidden3] = dw_acc[...].astype(bf16)
        quarter = width // parts
        spare = jnp.zeros((width, dw_ref.shape[2] - hidden3 - quarter), f32)
        for t in range(parts):
            columns = [dwo_acc[:, t * quarter : (t + 1) * quarter], spare]
            dw_ref[t, :, hidden3:] = jnp.concatenate(columns, axis=1).astype(bf16)


def feed_forward(ring_size, info, scale, attended_t, tokens, teacher, w_o, gain, weights, pack_width):
    seqs, slots, width = tokens.shape
    parts, _, hidden3 = weights.shape
    part = hidden3 // 3
    tile_rows = min(512, slots)
    per_seq = slots // tile_rows
    row_spec = pl.BlockSpec((1, tile_rows, width), lambda i: (i // per_seq, i % per_seq, 0))
    col_spec = pl.BlockSpec((1, width, tile_rows), lambda i: (i // per_seq, 0, i % per_seq))

    def whole(*shape):
        return pl.BlockSpec(shape, lambda i: (0,) * len(shape), pipeline_mode=pl.Buffered(1))

    def kept(*shape):
        return pl.BlockSpec(shape, lambda i: (0,) * len(shape))

    rows = seqs * slots
    return pl.pallas_call(
        functools.partial(feed_forward_kernel, ring_size),
        grid=(seqs * per_seq,),
        in_specs=[SMEM_SPEC, SMEM_SPEC, col_spec, row_spec, row_spec]
        + [whole(width, width), whole(1, width), whole(parts, width, hidden3)],
        out_specs=[row_spec, row_spec, col_spec]
        + [kept(parts, width, pack_width), kept(1, width), kept(1, 128)],
        out_shape=[
            jax.ShapeDtypeStruct((seqs, slots, width), f32),
            jax.ShapeDtypeStruct((seqs, slots, width), f32),
            jax.ShapeDtypeStruct((seqs, width, slots), bf16),
            jax.ShapeDtypeStruct((parts, width, pack_width), bf16),
            jax.ShapeDtypeStruct((1, width), f32),
            jax.ShapeDtypeStruct((1, 128), f32),
        ],
        scratch_shapes=[
            pltpu.VMEM((parts, tile_rows, part), f32),
            pltpu.VMEM((parts, tile_rows, part), f32),
            pltpu.VMEM((parts, tile_rows, part), bf16),
            pltpu.VMEM((parts, width, hidden3), f32),
            pltpu.VMEM((width, width), f32),
        ],
        compiler_params=PARAMS,
        cost_estimate=pl.CostEstimate(
            flops=6 * rows * width * (parts * hidden3 + width),
            transcendentals=rows * parts * part,
            bytes_accessed=rows * width * 20 + parts * width * hidden3 * 4,
        ),
        name="feed_forward",
    )(info, scale, attended_t, tokens, teacher, w_o, gain, weights)


RING = ("ctx", "tp")


def swap(value, mask):
    size = lax.axis_size(RING)
    return lax.ppermute(value, RING, [(i, i ^ mask) for i in range(size)])


def mirror(value):
    size = lax.axis_size(RING)
    return lax.ppermute(value, RING, [(i, size - 1 - i) for i in range(size)])


def mirror_odd(value):
    moved = mirror(value[1::2])
    seqs = value.shape[0]
    return jnp.concatenate(
        [moved[s // 2][None] if s % 2 else value[s][None] for s in range(seqs)], axis=0
    )


def move_back(value):
    moved = mirror(value[1::2].astype(bf16)).astype(f32)
    seqs = value.shape[0]
    return jnp.concatenate(
        [moved[s // 2][None] if s % 2 else value[s][None] for s in range(seqs)], axis=0
    )


def add_low(*parts):
    total = parts[0].astype(f32)
    for part in parts[1:]:
        total = total + part.astype(f32)
    return total.astype(bf16)


def gather_fsdp(value):
    if lax.axis_size("fsdp") != 2:
        return lax.all_gather(value, "fsdp", axis=0, tiled=False)
    other = lax.ppermute(value, "fsdp", [(0, 1), (1, 0)])
    at_zero = lax.axis_index("fsdp") == 0
    return jnp.stack([jnp.where(at_zero, value, other), jnp.where(at_zero, other, value)])


def pick_half(value, axis, index):
    half = value.shape[axis] // 2
    return lax.dynamic_slice_in_dim(value, index * half, half, axis)


def join_halves(mine, other, axis, index):
    return jnp.where(
        index == 0,
        jnp.concatenate([mine, other], axis=axis),
        jnp.concatenate([other, mine], axis=axis),
    )


def reduce_steps(value, own):
    fsdp_size, rows, columns = value.shape
    outer = lax.axis_size(RING) // 4
    core = own % 2
    column = (own // 2) % 2
    plane = own // 4
    value = value.astype(bf16)
    value = add_low(pick_half(value, 2, core), swap(pick_half(value, 2, 1 - core), 1))
    value = yield value
    if fsdp_size == 2:
        here = lax.axis_index("fsdp")
        away = lax.dynamic_index_in_dim(value, 1 - here, 0, False)
        mine = lax.dynamic_index_in_dim(value, here, 0, False)
        value = add_low(mine, lax.ppermute(away, "fsdp", [(0, 1), (1, 0)]))
    else:
        value = lax.psum_scatter(value, "fsdp", scatter_dimension=0, tiled=False)
    value = yield value
    value = add_low(pick_half(value, 1, column), swap(pick_half(value, 1, 1 - column), 2))
    value = yield value
    piece = rows // outer

    def rows_of(index):
        return lax.dynamic_slice_in_dim(value, index * piece, piece, 0)

    mine = add_low(
        rows_of(plane), *[swap(rows_of(plane ^ k), 4 * k) for k in range(1, outer)]
    )
    mine = yield mine
    whole = jnp.zeros((rows, columns // 4), bf16)
    whole = lax.dynamic_update_slice_in_dim(whole, mine, plane * piece, 0)
    for k in range(1, outer):
        whole = lax.dynamic_update_slice_in_dim(whole, swap(mine, 4 * k), (plane ^ k) * piece, 0)
    whole = yield whole
    whole = join_halves(whole, swap(whole, 2), 1, column)
    whole = yield whole
    yield join_halves(whole, swap(whole, 1), 1, core)


def advance(steps, value):
    try:
        return steps.send(value)
    except StopIteration:
        return value


def sum_steps(value):
    mask = 1
    while mask < lax.axis_size(RING):
        value = yield value + swap(value, mask)
        mask *= 2
    if lax.axis_size("fsdp") == 2:
        value = value + lax.ppermute(value, "fsdp", [(0, 1), (1, 0)])
    else:
        value = lax.psum(value, "fsdp")
    yield value


def run_steps(steps, value=None):
    while True:
        try:
            value = steps.send(value)
        except StopIteration:
            return value


def shards(
    tokens,
    teacher,
    lengths,
    gain_one,
    w_query,
    w_key,
    w_value,
    w_out,
    gain_two,
    w_gate,
    w_up,
    w_down,
):
    seqs, slots, width = tokens.shape
    kv_width = KV_HEADS * HEAD_DIM
    qkv_width = width + 2 * kv_width
    gain_at = qkv_width
    pack_width = -(-(gain_at + 2) // 128) * 128
    grad_width = -(-(qkv_width + 2) // 512) * 512
    half = w_query.shape[0]
    hidden_part = w_gate.shape[1]
    fsdp_size = lax.axis_size("fsdp")
    tp_size = lax.axis_size("tp")
    ring_size = lax.axis_size(RING)
    outer = ring_size // 4

    tokens_here = mirror_odd(tokens)
    count_total = jnp.sum(gather_fsdp(lengths)).astype(f32)
    packed = jnp.concatenate(
        [
            w_query,
            w_key,
            w_value,
            gain_one[:, None],
            gain_two[:, None],
            jnp.zeros((half, pack_width - gain_at - 2), bf16),
        ],
        axis=1,
    )
    packed = gather_fsdp(packed)
    packed = packed.reshape(width, pack_width)
    w_qkv = packed[:, :qkv_width]
    g_one = packed[:, gain_at].astype(f32)
    g_two = packed[:, gain_at + 1].astype(f32)
    ffn_pack = jnp.concatenate([w_gate, w_up, w_down.T], axis=1)

    own = lax.axis_index(RING).astype(jnp.int32)
    blocks = jnp.stack([block_of(own, s, ring_size) for s in range(seqs)])
    positions = blocks[:, None] * slots + jnp.arange(slots, dtype=jnp.int32)[None]
    cosine, sine = rope_tables(positions)
    info = jnp.concatenate([lengths.astype(jnp.int32), own[None]])

    inputs = tokens_here.astype(f32)
    normed = norm_rows(inputs, g_one).astype(bf16)
    qkv = jnp.einsum("df,sld->sfl", w_qkv, normed, preferred_element_type=f32)
    qk = qkv[:, : width + kv_width].reshape(seqs, HEADS + KV_HEADS, HEAD_DIM, slots)
    qk = rotate_cols(qk, cosine, sine).astype(bf16)
    queries = qk[:, :HEADS]
    values = qkv[:, width + kv_width :].astype(bf16).reshape(seqs, KV_HEADS, HEAD_DIM, slots)

    kv = {0: jnp.concatenate([qk[:, HEADS:], values], axis=2)}

    def outgoing(mask):
        return jnp.where(own < (own ^ mask), kv[0][0::2], kv[0][1::2])

    coming = {mask: swap(outgoing(mask), mask) for mask in [1, 2] + [4 * k for k in range(1, outer)]}
    calls = [(0,), (1, 2, 4)]
    for k in range(1, outer - 1):
        calls.append((4 * k - 1, 4 * k + 1, 4 * k + 2, 4 * k + 4))
    calls.append((4 * outer - 5, 4 * outer - 3, 4 * outer - 2, 4 * outer - 1))
    query_rows, *state = attend(ring_size, calls[0], info, queries, [kv[0]], None, False)
    for number, masks in enumerate(calls[1:], 1):
        if masks[-1] not in coming:
            coming[masks[-1]] = swap(coming[masks[-1] - 1], 1)
        later = [ffn_pack] if number == 1 else [w_out, teacher] if number == 2 else []
        *arrived, first_state = lax.optimization_barrier(
            [coming[m] for m in masks] + later + [state[0]]
        )
        if number == 1:
            ffn_all = lax.all_gather(arrived.pop(), ("tp", "fsdp"), axis=0, tiled=False)
            ffn_all = ffn_all.reshape(tp_size, width, 3 * hidden_part)
        if number == 2:
            teacher_here = mirror_odd(arrived.pop())
            w_o = gather_fsdp(arrived.pop()).reshape(width, width)
        kv.update(zip(masks, arrived))
        state = [first_state, state[1]]
        for mask in masks:
            if mask % 4 == 0:
                coming[mask + 2] = swap(kv[mask], 2)
                coming[mask + 1] = swap(kv[mask], 1)
            elif mask % 4 == 2 and mask + 1 not in coming:
                coming[mask + 1] = swap(kv[mask], 1)
        state = attend(
            ring_size, masks, info, query_rows, arrived, state, number == len(calls) - 1
        )
    attended, lse = state
    attended_t = attended.reshape(seqs, width, slots)

    slots_all = seqs * fsdp_size * slots * ring_size
    scale = (slots_all / count_total)[None]
    quarter = width // tp_size
    ffn_width = -(-(3 * hidden_part + quarter) // 128) * 128
    tile_info = jnp.concatenate([lengths.astype(jnp.int32), jnp.full((1,), slots, jnp.int32), own[None]])
    result, d_middle, d_attended_t, d_ffn, d_gain_two, squared_part = feed_forward(
        ring_size, tile_info, scale, attended_t, tokens_here, teacher_here, w_o, g_two[None],
        ffn_all, ffn_width
    )
    d_attended_t = d_attended_t.reshape(seqs, HEADS, HEAD_DIM, slots)
    d_ffn = d_ffn.reshape(tp_size * fsdp_size, half, ffn_width)
    d_ffn = lax.psum_scatter(d_ffn, ("tp", "fsdp"), scatter_dimension=0, tiled=False)
    loss_steps = sum_steps(squared_part)
    loss_sum = next(loss_steps)
    output = move_back(result)

    calls = [(4 * outer - 2, 4 * outer - 1)]
    for k in reversed(range(1, outer)):
        calls.append((4 * k, 4 * k + 1, 4 * k - 2, 4 * k - 1))
    calls += [(1,), (0,)]
    operands = [queries, d_attended_t, attended, lse]
    core_sums = {}
    own_parts = {}
    x_sums = {}
    plane_sums = {}
    for number, masks in enumerate(calls):
        last = number == len(calls) - 1
        if number:
            held = {("loss", 0): loss_sum}
            if number == 2:
                held[("output", 0)] = output
            if number == 3 or last:
                held[("ffn", 0)] = d_ffn
            if number >= 2:
                for mask in calls[number - 2][::2]:
                    held[("core", mask)] = core_sums[mask]
            for mask, (made, value) in x_sums.items():
                if made == number - 1:
                    held[("x", mask)] = value
            for mask, (made, value) in plane_sums.items():
                if made == number - 1 and not last:
                    held[("plane", mask)] = value
            names = list(held)
            info, *tied = lax.optimization_barrier([info] + [held[name] for name in names])
            tied = dict(zip(names, tied))
            loss_sum = advance(loss_steps, tied[("loss", 0)])
            output = tied.get(("output", 0), output)
            d_ffn = tied.get(("ffn", 0), d_ffn)
            if number == 3:
                d_ffn = lax.psum(d_ffn, "ctx")
            for (kind, mask), value in tied.items():
                if kind == "x":
                    x_sums[mask] = (-1, value)
                elif kind == "plane":
                    plane_sums[mask] = (-1, value)
                elif kind == "core":
                    core_sums[mask] = value
            for kind, mask in names:
                if kind == "core" and mask % 4:
                    x_sums[mask - 2] = (number, swap(core_sums[mask], 2))
                elif kind == "core":
                    total = add_low(core_sums[mask], x_sums[mask][1])
                    plane_sums[mask] = (number, swap(total, mask))
        parts, outs = attend_back(
            ring_size, masks, info, [kv[m] for m in masks], operands, number == 0, last
        )
        if len(masks) == 1:
            own_parts[masks[0]] = parts[0]
        for place in range(0, len(masks) - 1, 2):
            core_sums[masks[place]] = add_low(parts[place], swap(parts[place + 1], 1))
        if number == 0:
            operands = [outs[1], outs[2], outs[0]]
        else:
            operands = operands[:2] + [outs[0]]
    d_query = outs[0]
    d_kv_terms = [(mask, value) for mask, (_, value) in plane_sums.items()]
    d_kv_terms += [(2, x_sums[0][1]), (1, swap(own_parts[1], 1))]
    own_part = own_parts[0]
    d_kv_halves = []
    for parity in range(2):
        total = own_part[parity::2].astype(f32)
        for mask, term in d_kv_terms:
            from_it = (own > (own ^ mask)) == (parity == 1)
            total = total + jnp.where(from_it, term.astype(f32), 0.0)
        d_kv_halves.append(total)
    d_kv = jnp.stack(d_kv_halves, axis=1).reshape(own_part.shape)

    d_query = rotate_cols(d_query, cosine, -sine).astype(bf16).reshape(seqs, width, slots)
    d_normed = jnp.einsum("sfl,df->sld", d_query, w_qkv[:, :width], preferred_element_type=f32)
    d_query_w = jnp.einsum("sld,sfl->df", normed, d_query, preferred_element_type=f32)
    d_keys = rotate_cols(d_kv[:, :, :HEAD_DIM], cosine, -sine).astype(bf16)
    d_values = d_kv[:, :, HEAD_DIM:].astype(bf16)
    d_kv_rows = jnp.concatenate(
        [d_keys.reshape(seqs, kv_width, slots), d_values.reshape(seqs, kv_width, slots)], axis=1
    )
    d_normed += jnp.einsum("sfl,df->sld", d_kv_rows, w_qkv[:, width:], preferred_element_type=f32)
    d_kv_w = jnp.einsum("sld,sfl->df", normed, d_kv_rows, preferred_element_type=f32)
    loss_sum = run_steps(loss_steps, loss_sum)
    loss_value = loss_sum[0, 0] / (count_total * width)
    norm_one_pull = jax.vjp(norm_rows, inputs, g_one)[1]
    d_inputs_norm, d_gain_one = norm_one_pull(d_normed)
    tokens_grad = d_middle + d_inputs_norm
    back = tokens_grad[1::2].astype(bf16)
    cut = width // 2 // 128 * 128
    back_parts = [mirror(back[..., :cut]), mirror(back[..., cut:])]
    d_packed = jnp.concatenate(
        [
            d_query_w,
            d_kv_w,
            d_gain_one[:, None],
            d_gain_two.T,
            jnp.zeros((width, grad_width - qkv_width - 2), f32),
        ],
        axis=1,
    )
    steps = reduce_steps(d_packed.reshape(fsdp_size, half, grad_width), own)
    d_packed = next(steps)
    d_packed = steps.send(d_packed)
    back_parts[0], d_packed = lax.optimization_barrier((back_parts[0], d_packed))
    d_packed = steps.send(d_packed)
    back_parts[1], d_packed = lax.optimization_barrier((back_parts[1], d_packed))
    d_packed = steps.send(d_packed)
    d_packed = steps.send(d_packed)
    piece = d_packed.shape[1]
    out_piece = d_ffn[:, 3 * hidden_part : 3 * hidden_part + quarter]
    out_piece = jnp.pad(out_piece, ((0, 0), (0, piece - quarter)))
    d_packed = run_steps(steps, jnp.concatenate([d_packed, out_piece], axis=1))
    pieces = d_packed.astype(f32).reshape(half, 2, 2, 2, piece)
    d_packed = pieces[:, :, :, 0].reshape(half, grad_width)
    d_out_w = pieces[:, :, :, 1, :quarter].swapaxes(1, 2).reshape(half, width)
    d_ffn = d_ffn.astype(f32)
    back = jnp.concatenate(back_parts, axis=2).astype(f32)
    tokens_grad = jnp.stack([tokens_grad[0::2], back], axis=1).reshape(tokens_grad.shape)
    return (
        output,
        loss_value,
        tokens_grad,
        d_packed[:, qkv_width],
        d_packed[:, :width],
        d_packed[:, width : width + kv_width],
        d_packed[:, width + kv_width : qkv_width],
        d_out_w,
        d_packed[:, qkv_width + 1],
        d_ffn[:, :hidden_part],
        d_ffn[:, hidden_part : 2 * hidden_part],
        d_ffn[:, 2 * hidden_part : 3 * hidden_part].T,
    )


def solution(mesh):
    slots_spec = P("fsdp", ("ctx", "tp"), None)
    rows_spec = P("fsdp", None)
    return jax.shard_map(
        shards,
        mesh=mesh,
        in_specs=(
            slots_spec,
            slots_spec,
            P("fsdp"),
            P("fsdp"),
            rows_spec,
            rows_spec,
            rows_spec,
            rows_spec,
            P("fsdp"),
            P("fsdp", "tp"),
            P("fsdp", "tp"),
            P("tp", "fsdp"),
        ),
        out_specs=(
            slots_spec,
            P(),
            slots_spec,
            P("fsdp"),
            rows_spec,
            rows_spec,
            rows_spec,
            rows_spec,
            P("fsdp"),
            P("fsdp", "tp"),
            P("fsdp", "tp"),
            P("tp", "fsdp"),
        ),
        check_vma=False,
    )
```

```python
import functools

import jax
import jax.numpy as jnp
from jax import lax
from jax.experimental import pallas as pl
from jax.experimental.pallas import tpu as pltpu
from jax.sharding import PartitionSpec as P

HEADS = 9
KV_HEADS = 3
GROUP = HEADS // KV_HEADS
HEAD_DIM = 64
AUG = HEAD_DIM + 16

EPS = 1e-05
ROPE_BASE = 10000.0
NEG = -1e30
LOG2E = 1.4426950408889634
EXP2_SCALE = LOG2E * HEAD_DIM ** (-0.5)

f32 = jnp.float32
bf16 = jnp.bfloat16
NN = ((1,), (0,))
TN = ((0,), (0,))
NT = ((1,), (1,))


def dot(left, right, dims):
    return lax.dot_general(left, right, (dims, ((), ())), preferred_element_type=f32)


def norm_rows(values, gain):
    return values * lax.rsqrt(jnp.mean(values * values, axis=-1, keepdims=True) + EPS) * gain


def rope_tables(positions):
    half_width = HEAD_DIM // 2
    frequency = ROPE_BASE ** (-(jnp.arange(half_width, dtype=f32) * 2.0) / HEAD_DIM)
    angles = frequency[None, None, :, None] * positions.astype(f32)[:, None, None, :]
    return (jnp.cos(angles), jnp.sin(angles))


def rotate_cols(values, cosine, sine):
    half_width = HEAD_DIM // 2
    lower = values[..., :half_width, :]
    upper = values[..., half_width:, :]
    return jnp.concatenate([lower * cosine - upper * sine, upper * cosine + lower * sine], axis=-2)


def three_pieces(row):
    first = row.astype(bf16)
    rest = row - first.astype(f32)
    second = rest.astype(bf16)
    third = (rest - second.astype(f32)).astype(bf16)
    return (first, second, third)


def penalty_row(block_start, width, length):
    key_pos = block_start + lax.broadcasted_iota(jnp.int32, (1, width), 1)
    return jnp.where(key_pos < length, 0.0, NEG).astype(bf16)


def extra_rows(rows, width):
    wide = jnp.zeros((16, width), f32)
    index = lax.broadcasted_iota(jnp.int32, (16, width), 0)
    for place, row in enumerate(rows):
        wide = jnp.where(index == place, row.astype(f32), wide)
    return wide.astype(bf16)


def block_of(device, seq, ring_size):
    return jnp.where(seq % 2 == 1, ring_size - 1 - device, device)


def needed(device, mask, seq):
    if mask == 0:
        return seq >= 0
    return (device ^ mask > device) == (seq % 2 == 1)


def pair_up(masks):
    groups = []
    for mask in masks:
        for group in groups:
            if len(group) == 1 and mask and masks[group[0]].bit_length() == mask.bit_length():
                group.append(masks.index(mask))
                break
        else:
            groups.append([masks.index(mask)])
    return groups


def forward_kernel(ring_size, masks, first, last, *refs):
    count = len(masks)
    info, q_ref = refs[:2]
    kv_refs = refs[2 : 2 + count]
    rest = refs[2 + count :]
    slots = kv_refs[0].shape[-1]
    cols = GROUP * slots
    if first:
        qa_ref, max_ref, acc_ref = rest
    else:
        qa_ref = q_ref
        if last:
            max_in, acc_in, out_ref, lse_ref, max_ref, acc_ref = rest
        else:
            max_in, acc_in, max_ref, acc_ref = rest
        max_ref[...] = max_in[...]
        acc_ref[...] = acc_in[...]
    device = info[info.shape[0] - 1]

    def step(seq, keys, values, penalty, diagonal):
        wide = keys.shape[1]
        key_cols = jnp.concatenate([keys, extra_rows([penalty], wide)], axis=0)
        value_ones = extra_rows([jnp.ones((1, wide), f32)], wide)
        value_cols = jnp.concatenate([values, value_ones], axis=0)
        scores = dot(key_cols, qa_ref[seq, 0], TN) * EXP2_SCALE
        if diagonal:
            key_at = lax.broadcasted_iota(jnp.int32, (slots, cols), 0)
            query_at = lax.broadcasted_iota(jnp.int32, (slots, cols), 1) % slots
            scores = jnp.where(key_at <= query_at, scores, NEG)
        old_max = max_ref[seq, 0]
        new_max = jnp.maximum(old_max, jnp.max(scores, axis=0, keepdims=True))
        weights = jnp.exp2(scores - new_max).astype(bf16)
        max_ref[seq, 0] = new_max
        acc_ref[seq, 0] = acc_ref[seq, 0] * jnp.exp2(old_max - new_max) + dot(value_cols, weights, NN)

    def work(seq, carry):
        if first:
            heads = [q_ref[seq, h] for h in range(GROUP)]
            qa_ref[seq, 0, 0:HEAD_DIM] = jnp.concatenate(heads, axis=1)
            qa_ref[seq, 0, HEAD_DIM:AUG] = extra_rows([jnp.ones((1, cols), f32)], cols)
            max_ref[seq] = jnp.full(max_ref.shape[1:], NEG, f32)
            acc_ref[seq] = jnp.zeros(acc_ref.shape[1:], f32)
        for group in pair_up(masks):
            mask = masks[group[0]]
            blocks = [block_of(device ^ masks[place], seq, ring_size) for place in group]
            at = seq // 2 if mask else seq
            start = functools.reduce(jnp.minimum, blocks) * slots

            @pl.when(needed(device, mask, seq) & (start < info[seq]))
            def _():
                penalty = [penalty_row(block * slots, slots, info[seq]) for block in blocks]
                keys = [kv_refs[place][at, 0, 0:HEAD_DIM] for place in group]
                values = [kv_refs[place][at, 0, HEAD_DIM:] for place in group]
                step(
                    seq,
                    jnp.concatenate(keys, axis=1),
                    jnp.concatenate(values, axis=1),
                    jnp.concatenate(penalty, axis=1),
                    mask == 0,
                )

        if last:
            total = acc_ref[seq, 0, HEAD_DIM : HEAD_DIM + 1]
            heads_out = acc_ref[seq, 0, 0:HEAD_DIM] / total
            lse_ref[seq, 0] = (max_ref[seq, 0] + jnp.log2(total)) * (1.0 / EXP2_SCALE)
            for h in range(GROUP):
                out_ref[seq, h] = heads_out[:, h * slots : (h + 1) * slots].astype(bf16)
        return carry

    lax.fori_loop(0, qa_ref.shape[0], work, 0)


def backward_kernel(ring_size, masks, first, last, *refs):
    count = len(masks)
    info = refs[0]
    kv_refs = refs[1 : 1 + count]
    rest = refs[1 + count :]
    slots = kv_refs[0].shape[-1]
    cols = GROUP * slots
    if first:
        q_ref, do_ref, o_ref, lse_ref = rest[:4]
        dkv_refs = rest[4 : 4 + count]
        acc_ref, qa_ref, da_ref = rest[4 + count :]
    else:
        qa_ref, da_ref, acc_in = rest[:3]
        dkv_refs = rest[3 : 3 + count]
        if last:
            dq_ref, acc_ref = rest[3 + count :]
        else:
            (acc_ref,) = rest[3 + count :]
        acc_ref[...] = acc_in[...]
    device = info[info.shape[0] - 1]

    def prepare(seq):
        grads = jnp.concatenate([do_ref[seq, h] for h in range(GROUP)], axis=1)
        heads_out = jnp.concatenate([o_ref[seq, h] for h in range(GROUP)], axis=1)
        delta = jnp.sum(grads.astype(f32) * heads_out.astype(f32), axis=0, keepdims=True)
        heads = [q_ref[seq, h] for h in range(GROUP)]
        qa_ref[seq, 0, 0:HEAD_DIM] = jnp.concatenate(heads, axis=1)
        qa_ref[seq, 0, HEAD_DIM:AUG] = extra_rows(
            three_pieces(-lse_ref[seq, 0]) + (jnp.ones((1, cols), f32),), cols
        )
        da_ref[seq, 0, 0:HEAD_DIM] = grads
        da_ref[seq, 0, HEAD_DIM:AUG] = extra_rows(three_pieces(-delta), cols)
        acc_ref[seq] = jnp.zeros(acc_ref.shape[1:], f32)

    def step(seq, keys, values, penalty, diagonal):
        wide = keys.shape[1]
        ones_key = jnp.ones((1, wide), f32)
        key_cols = jnp.concatenate([keys, extra_rows([ones_key] * 3 + [penalty], wide)], axis=0)
        value_cols = jnp.concatenate([values, extra_rows([ones_key] * 3, wide)], axis=0)
        scores = dot(qa_ref[seq, 0], key_cols, TN) * EXP2_SCALE
        if diagonal:
            query_at = lax.broadcasted_iota(jnp.int32, (cols, slots), 0) % slots
            key_at = lax.broadcasted_iota(jnp.int32, (cols, slots), 1)
            scores = jnp.where(key_at <= query_at, scores, NEG)
        weights = jnp.exp2(scores)
        d_scores = (weights * dot(da_ref[seq, 0], value_cols, TN)).astype(bf16)
        d_value = dot(da_ref[seq, 0, 0:HEAD_DIM], weights.astype(bf16), NN)
        d_key = dot(qa_ref[seq, 0, 0:HEAD_DIM], d_scores, NN) * (HEAD_DIM ** (-0.5))
        acc_ref[seq, 0] += dot(keys, d_scores, NT)
        return (d_key.astype(bf16), d_value.astype(bf16))

    def work(seq, carry):
        if first:
            prepare(seq)
        active = block_of(device, seq, ring_size) * slots < info[seq]
        for group in pair_up(masks):
            mask = masks[group[0]]
            blocks = [block_of(device ^ masks[place], seq, ring_size) for place in group]
            turn = needed(device, mask, seq)
            at = seq // 2 if mask else seq

            @pl.when(turn & active)
            def _():
                penalty = [penalty_row(block * slots, slots, info[seq]) for block in blocks]
                keys = [kv_refs[place][at, 0, 0:HEAD_DIM] for place in group]
                values = [kv_refs[place][at, 0, HEAD_DIM:] for place in group]
                d_key, d_value = step(
                    seq,
                    jnp.concatenate(keys, axis=1),
                    jnp.concatenate(values, axis=1),
                    jnp.concatenate(penalty, axis=1),
                    mask == 0,
                )
                for number, place in enumerate(group):
                    part = slice(number * slots, (number + 1) * slots)
                    dkv_refs[place][at, 0, 0:HEAD_DIM] = d_key[:, part]
                    dkv_refs[place][at, 0, HEAD_DIM:] = d_value[:, part]

            @pl.when(turn & jnp.logical_not(active))
            def _():
                for place in group:
                    dkv_refs[place][at] = jnp.zeros(dkv_refs[place].shape[1:], bf16)

        if last:
            d_query = acc_ref[seq, 0] * (HEAD_DIM ** (-0.5))
            for h in range(GROUP):
                dq_ref[seq, h] = d_query[:, h * slots : (h + 1) * slots]
        return carry

    lax.fori_loop(0, qa_ref.shape[0], work, 0)


def head_spec(seqs, rows, lanes, heads=1):
    return pl.BlockSpec((seqs, heads, rows, lanes), lambda group: (0, group, 0, 0))


def kv_specs(kvs):
    return [head_spec(kv.shape[0], kv.shape[2], kv.shape[3]) for kv in kvs]


SMEM_SPEC = pl.BlockSpec(memory_space=pltpu.SMEM)
PARAMS = pltpu.CompilerParams(vmem_limit_bytes=60 * 2**20)


def call_cost(kv_shape, count, products):
    seqs, groups, _, slots = kv_shape
    pairs = seqs * groups * GROUP * slots * slots * count
    return pl.CostEstimate(
        flops=pairs * HEAD_DIM * products * 4,
        transcendentals=pairs,
        bytes_accessed=seqs * groups * count * 4 * HEAD_DIM * slots,
    )


def attend(ring_size, masks, info, queries, kvs, state, last):
    first = state is None
    groups, slots = kvs[0].shape[1], kvs[0].shape[3]
    seqs = queries.shape[0]
    cols = GROUP * slots
    wide_spec = head_spec(seqs, AUG, cols)
    row_spec = head_spec(seqs, 1, cols)
    wide_shape = (seqs, groups, AUG, cols)
    row_shape = jax.ShapeDtypeStruct((seqs, groups, 1, cols), f32)
    state_specs = [row_spec, wide_spec]
    state_shapes = [row_shape, jax.ShapeDtypeStruct(wide_shape, f32)]
    query_spec = wide_spec
    scratch = []
    if first:
        query_spec = head_spec(seqs, HEAD_DIM, slots, GROUP)
        out_specs = [wide_spec] + state_specs
        out_shape = [jax.ShapeDtypeStruct(wide_shape, bf16)] + state_shapes
    elif last:
        out_specs = [head_spec(seqs, HEAD_DIM, slots, GROUP), row_spec]
        out_shape = [jax.ShapeDtypeStruct((seqs, groups * GROUP, HEAD_DIM, slots), bf16), row_shape]
        scratch = [pltpu.VMEM((seqs, 1, 1, cols), f32), pltpu.VMEM((seqs, 1, AUG, cols), f32)]
    else:
        out_specs = state_specs
        out_shape = state_shapes
    return pl.pallas_call(
        functools.partial(forward_kernel, ring_size, masks, first, last),
        grid=(groups,),
        in_specs=[SMEM_SPEC, query_spec]
        + kv_specs(kvs)
        + ([] if first else state_specs),
        out_specs=out_specs,
        out_shape=out_shape,
        scratch_shapes=scratch,
        compiler_params=PARAMS,
        cost_estimate=call_cost(kvs[0].shape, len(masks), 4),
        name="attend",
    )(info, queries, *kvs, *([] if first else state))


def attend_back(ring_size, masks, info, kvs, operands, first, last):
    groups, slots = kvs[0].shape[1], kvs[0].shape[3]
    seqs = operands[0].shape[0]
    cols = GROUP * slots
    heads_spec = head_spec(seqs, HEAD_DIM, slots, GROUP)
    wide_spec = head_spec(seqs, AUG, cols)
    acc_spec = head_spec(seqs, HEAD_DIM, cols)
    kv_shapes = [jax.ShapeDtypeStruct(kv.shape, bf16) for kv in kvs]
    wide_shape = jax.ShapeDtypeStruct((seqs, groups, AUG, cols), bf16)
    acc_shape = jax.ShapeDtypeStruct((seqs, groups, HEAD_DIM, cols), f32)
    scratch = []
    if first:
        operand_specs = [heads_spec] * 3 + [head_spec(seqs, 1, cols)]
        out_specs = [acc_spec, wide_spec, wide_spec]
        out_shape = [acc_shape, wide_shape, wide_shape]
    else:
        operand_specs = [wide_spec, wide_spec, acc_spec]
        if last:
            out_specs = [heads_spec]
            out_shape = [jax.ShapeDtypeStruct((seqs, groups * GROUP, HEAD_DIM, slots), f32)]
            scratch = [pltpu.VMEM((seqs, 1, HEAD_DIM, cols), f32)]
        else:
            out_specs = [acc_spec]
            out_shape = [acc_shape]
    outs = pl.pallas_call(
        functools.partial(backward_kernel, ring_size, masks, first, last),
        grid=(groups,),
        in_specs=[SMEM_SPEC] + kv_specs(kvs) + operand_specs,
        out_specs=kv_specs(kvs) + out_specs,
        out_shape=kv_shapes + out_shape,
        scratch_shapes=scratch,
        compiler_params=PARAMS,
        cost_estimate=call_cost(kvs[0].shape, len(masks), 10),
        name="attend_back",
    )(info, *kvs, *operands)
    return (outs[: len(masks)], outs[len(masks) :])


def feed_forward_kernel(
    ring_size, info, scale, att_ref, tok_ref, teach_ref, wo_ref, gain_ref, w_ref,
    out_ref, dmid_ref, datt_ref, dw_ref, dwo_ref, dgain_ref, loss_ref,
    slope_ref, silu_ref, hidden_ref, dw_acc, dwo_acc,
):
    tile = pl.program_id(0)
    parts, width, hidden3 = w_ref.shape
    part = hidden3 // 3
    tile_rows = tok_ref.shape[1]
    slots = info[info.shape[0] - 2]
    device = info[info.shape[0] - 1]
    seq = tile * tile_rows // slots
    first_pos = block_of(device, seq, ring_size) * slots + tile * tile_rows % slots

    @pl.when(tile == 0)
    def _():
        dw_acc[...] = jnp.zeros(dw_acc.shape, f32)
        dwo_acc[...] = jnp.zeros(dwo_acc.shape, f32)
        dgain_ref[...] = jnp.zeros(dgain_ref.shape, f32)
        loss_ref[...] = jnp.zeros(loss_ref.shape, f32)

    gain = gain_ref[...]
    att = att_ref[0]
    middle = tok_ref[0].astype(f32) + dot(att, wo_ref[...], TN)
    inverse = lax.rsqrt(jnp.mean(middle * middle, axis=-1, keepdims=True) + EPS)
    unit = middle * inverse
    normed = (unit * gain).astype(bf16)
    branch = jnp.zeros((tile_rows, width), f32)
    for t in range(parts):
        both = dot(normed, w_ref[t, :, : 2 * part], NN)
        gate = both[:, :part]
        up = both[:, part:]
        sigmoid = jax.nn.sigmoid(gate)
        silu = gate * sigmoid
        hidden = (silu * up).astype(bf16)
        slope_ref[t] = up * sigmoid * (1.0 + gate * (1.0 - sigmoid))
        silu_ref[t] = silu
        hidden_ref[t] = hidden
        branch = branch + dot(hidden, w_ref[t, :, 2 * part :], NT)
    result = middle + branch
    out_ref[0] = result
    row_pos = first_pos + lax.broadcasted_iota(jnp.int32, (tile_rows, 1), 0)
    valid = (row_pos < info[seq]).astype(f32)
    mismatch = valid * (result - teach_ref[0].astype(f32))
    loss_ref[...] += jnp.sum(mismatch * mismatch)
    d_result = mismatch * scale[0]
    d_branch = d_result.astype(bf16)
    d_normed = jnp.zeros((tile_rows, width), f32)
    for t in range(parts):
        d_hidden = dot(d_branch, w_ref[t, :, 2 * part :], NN)
        d_both = jnp.concatenate([d_hidden * slope_ref[t], d_hidden * silu_ref[t]], axis=1)
        d_both = d_both.astype(bf16)
        dw_acc[t, :, : 2 * part] += dot(normed, d_both, TN)
        dw_acc[t, :, 2 * part :] += dot(d_branch, hidden_ref[t], TN)
        d_normed = d_normed + dot(d_both, w_ref[t, :, : 2 * part], NT)
    dgain_ref[...] += jnp.sum(d_normed * unit, axis=0, keepdims=True)
    d_unit = d_normed * gain
    d_middle = d_result + inverse * (d_unit - unit * jnp.mean(d_unit * unit, axis=-1, keepdims=True))
    dmid_ref[0] = d_middle
    d_attn = d_middle.astype(bf16)
    datt_ref[0] = dot(wo_ref[...], d_attn, NT).astype(bf16)
    dwo_acc[...] += dot(att, d_attn, NN)

    @pl.when(tile == pl.num_programs(0) - 1)
    def _():
        dw_ref[...] = dw_acc[...].astype(bf16)
        dwo_ref[...] = jnp.zeros(dwo_ref.shape, bf16)
        dwo_ref[:, :width] = dwo_acc[...].astype(bf16)


def feed_forward(ring_size, info, scale, attended_t, tokens, teacher, w_o, gain, weights, out_width):
    seqs, slots, width = tokens.shape
    parts, _, hidden3 = weights.shape
    part = hidden3 // 3
    tile_rows = min(512, slots)
    per_seq = slots // tile_rows
    row_spec = pl.BlockSpec((1, tile_rows, width), lambda i: (i // per_seq, i % per_seq, 0))
    col_spec = pl.BlockSpec((1, width, tile_rows), lambda i: (i // per_seq, 0, i % per_seq))

    def whole(*shape):
        return pl.BlockSpec(shape, lambda i: (0,) * len(shape), pipeline_mode=pl.Buffered(1))

    def kept(*shape):
        return pl.BlockSpec(shape, lambda i: (0,) * len(shape))

    rows = seqs * slots
    return pl.pallas_call(
        functools.partial(feed_forward_kernel, ring_size),
        grid=(seqs * per_seq,),
        in_specs=[SMEM_SPEC, SMEM_SPEC, col_spec, row_spec, row_spec]
        + [whole(width, width), whole(1, width), whole(parts, width, hidden3)],
        out_specs=[row_spec, row_spec, col_spec]
        + [kept(parts, width, hidden3), kept(width, out_width), kept(1, width), kept(1, 128)],
        out_shape=[
            jax.ShapeDtypeStruct((seqs, slots, width), f32),
            jax.ShapeDtypeStruct((seqs, slots, width), f32),
            jax.ShapeDtypeStruct((seqs, width, slots), bf16),
            jax.ShapeDtypeStruct((parts, width, hidden3), bf16),
            jax.ShapeDtypeStruct((width, out_width), bf16),
            jax.ShapeDtypeStruct((1, width), f32),
            jax.ShapeDtypeStruct((1, 128), f32),
        ],
        scratch_shapes=[
            pltpu.VMEM((parts, tile_rows, part), f32),
            pltpu.VMEM((parts, tile_rows, part), f32),
            pltpu.VMEM((parts, tile_rows, part), bf16),
            pltpu.VMEM((parts, width, hidden3), f32),
            pltpu.VMEM((width, width), f32),
        ],
        compiler_params=PARAMS,
        cost_estimate=pl.CostEstimate(
            flops=6 * rows * width * (parts * hidden3 + width),
            transcendentals=rows * parts * part,
            bytes_accessed=rows * width * 20 + parts * width * hidden3 * 4,
        ),
        name="feed_forward",
    )(info, scale, attended_t, tokens, teacher, w_o, gain, weights)


RING = ("ctx", "tp")


def swap(value, mask):
    size = lax.axis_size(RING)
    return lax.ppermute(value, RING, [(i, i ^ mask) for i in range(size)])


def mirror(value):
    size = lax.axis_size(RING)
    return lax.ppermute(value, RING, [(i, size - 1 - i) for i in range(size)])


def mirror_odd(value):
    moved = mirror(value[1::2])
    seqs = value.shape[0]
    return jnp.concatenate(
        [moved[s // 2][None] if s % 2 else value[s][None] for s in range(seqs)], axis=0
    )


def move_back(value):
    moved = mirror(value[1::2].astype(bf16)).astype(f32)
    seqs = value.shape[0]
    return jnp.concatenate(
        [moved[s // 2][None] if s % 2 else value[s][None] for s in range(seqs)], axis=0
    )


def add_low(*parts):
    total = parts[0].astype(f32)
    for part in parts[1:]:
        total = total + part.astype(f32)
    return total.astype(bf16)


def gather_fsdp(value):
    if lax.axis_size("fsdp") != 2:
        return lax.all_gather(value, "fsdp", axis=0, tiled=False)
    other = lax.ppermute(value, "fsdp", [(0, 1), (1, 0)])
    at_zero = lax.axis_index("fsdp") == 0
    return jnp.stack([jnp.where(at_zero, value, other), jnp.where(at_zero, other, value)])


def pick_half(value, axis, index):
    half = value.shape[axis] // 2
    return lax.dynamic_slice_in_dim(value, index * half, half, axis)


def join_halves(mine, other, axis, index):
    return jnp.where(
        index == 0,
        jnp.concatenate([mine, other], axis=axis),
        jnp.concatenate([other, mine], axis=axis),
    )


def reduce_steps(value, own):
    fsdp_size, rows, columns = value.shape
    outer = lax.axis_size(RING) // 4
    core = own % 2
    column = (own // 2) % 2
    plane = own // 4
    value = value.astype(bf16)
    value = add_low(pick_half(value, 2, core), swap(pick_half(value, 2, 1 - core), 1))
    value = yield value
    if fsdp_size == 2:
        here = lax.axis_index("fsdp")
        away = lax.dynamic_index_in_dim(value, 1 - here, 0, False)
        mine = lax.dynamic_index_in_dim(value, here, 0, False)
        value = add_low(mine, lax.ppermute(away, "fsdp", [(0, 1), (1, 0)]))
    else:
        value = lax.psum_scatter(value, "fsdp", scatter_dimension=0, tiled=False)
    value = yield value
    value = add_low(pick_half(value, 1, column), swap(pick_half(value, 1, 1 - column), 2))
    value = yield value
    piece = rows // outer

    def rows_of(index):
        return lax.dynamic_slice_in_dim(value, index * piece, piece, 0)

    mine = add_low(
        rows_of(plane), *[swap(rows_of(plane ^ k), 4 * k) for k in range(1, outer)]
    )
    mine = yield mine
    whole = jnp.zeros((rows, columns // 4), bf16)
    whole = lax.dynamic_update_slice_in_dim(whole, mine, plane * piece, 0)
    for k in range(1, outer):
        whole = lax.dynamic_update_slice_in_dim(whole, swap(mine, 4 * k), (plane ^ k) * piece, 0)
    whole = yield whole
    whole = join_halves(whole, swap(whole, 2), 1, column)
    whole = yield whole
    yield join_halves(whole, swap(whole, 1), 1, core).astype(f32)


def sum_steps(value):
    mask = 1
    while mask < lax.axis_size(RING):
        value = yield value + swap(value, mask)
        mask *= 2
    if lax.axis_size("fsdp") == 2:
        value = value + lax.ppermute(value, "fsdp", [(0, 1), (1, 0)])
    else:
        value = lax.psum(value, "fsdp")
    yield value


def advance(steps, value):
    try:
        return steps.send(value)
    except StopIteration:
        return value


def run_steps(steps, value=None):
    while True:
        try:
            value = steps.send(value)
        except StopIteration:
            return value


def shards(
    tokens,
    teacher,
    lengths,
    gain_one,
    w_query,
    w_key,
    w_value,
    w_out,
    gain_two,
    w_gate,
    w_up,
    w_down,
):
    seqs, slots, width = tokens.shape
    kv_width = KV_HEADS * HEAD_DIM
    qkv_width = width + 2 * kv_width
    gain_at = qkv_width
    pack_width = -(-(gain_at + 2) // 128) * 128
    grad_width = -(-(qkv_width + 2) // 512) * 512
    half = w_query.shape[0]
    hidden_part = w_gate.shape[1]
    fsdp_size = lax.axis_size("fsdp")
    tp_size = lax.axis_size("tp")
    ring_size = lax.axis_size(RING)
    outer = ring_size // 4

    tokens_here = mirror_odd(tokens)
    count_total = jnp.sum(gather_fsdp(lengths)).astype(f32)
    packed = jnp.concatenate(
        [
            w_query,
            w_key,
            w_value,
            gain_one[:, None],
            gain_two[:, None],
            jnp.zeros((half, pack_width - gain_at - 2), bf16),
        ],
        axis=1,
    )
    packed = gather_fsdp(packed)
    packed = packed.reshape(width, pack_width)
    w_qkv = packed[:, :qkv_width]
    g_one = packed[:, gain_at].astype(f32)
    g_two = packed[:, gain_at + 1].astype(f32)
    ffn_pack = jnp.concatenate([w_gate, w_up, w_down.T], axis=1)

    own = lax.axis_index(RING).astype(jnp.int32)
    blocks = jnp.stack([block_of(own, s, ring_size) for s in range(seqs)])
    positions = blocks[:, None] * slots + jnp.arange(slots, dtype=jnp.int32)[None]
    cosine, sine = rope_tables(positions)
    info = jnp.concatenate([lengths.astype(jnp.int32), own[None]])

    inputs = tokens_here.astype(f32)
    normed = norm_rows(inputs, g_one).astype(bf16)
    qkv = jnp.einsum("df,sld->sfl", w_qkv, normed, preferred_element_type=f32)
    qk = qkv[:, : width + kv_width].reshape(seqs, HEADS + KV_HEADS, HEAD_DIM, slots)
    qk = rotate_cols(qk, cosine, sine).astype(bf16)
    queries = qk[:, :HEADS]
    values = qkv[:, width + kv_width :].astype(bf16).reshape(seqs, KV_HEADS, HEAD_DIM, slots)

    kv = {0: jnp.concatenate([qk[:, HEADS:], values], axis=2)}

    def outgoing(mask):
        return jnp.where(own < (own ^ mask), kv[0][0::2], kv[0][1::2])

    coming = {mask: swap(outgoing(mask), mask) for mask in [1, 2] + [4 * k for k in range(1, outer)]}
    calls = [(0,), (1, 2, 4)]
    for k in range(1, outer - 1):
        calls.append((4 * k - 1, 4 * k + 1, 4 * k + 2, 4 * k + 4))
    calls.append((4 * outer - 5, 4 * outer - 3, 4 * outer - 2, 4 * outer - 1))
    query_rows, *state = attend(ring_size, calls[0], info, queries, [kv[0]], None, False)
    for number, masks in enumerate(calls[1:], 1):
        if masks[-1] not in coming:
            coming[masks[-1]] = swap(coming[masks[-1] - 1], 1)
        later = [ffn_pack] if number == 1 else [w_out, teacher] if number == 2 else []
        *arrived, first_state = lax.optimization_barrier(
            [coming[m] for m in masks] + later + [state[0]]
        )
        if number == 1:
            ffn_all = lax.all_gather(arrived.pop(), ("tp", "fsdp"), axis=0, tiled=False)
            ffn_all = ffn_all.reshape(tp_size, width, 3 * hidden_part)
        if number == 2:
            teacher_here = mirror_odd(arrived.pop())
            w_o = gather_fsdp(arrived.pop()).reshape(width, width)
        kv.update(zip(masks, arrived))
        state = [first_state, state[1]]
        for mask in masks:
            if mask % 4 == 0:
                coming[mask + 2] = swap(kv[mask], 2)
                coming[mask + 1] = swap(kv[mask], 1)
            elif mask % 4 == 2 and mask + 1 not in coming:
                coming[mask + 1] = swap(kv[mask], 1)
        state = attend(
            ring_size, masks, info, query_rows, arrived, state, number == len(calls) - 1
        )
    attended, lse = state
    attended_t = attended.reshape(seqs, width, slots)

    slots_all = seqs * fsdp_size * slots * ring_size
    scale = (slots_all / count_total)[None]
    out_width = -(-width // 512) * 512
    tile_info = jnp.concatenate([lengths.astype(jnp.int32), jnp.full((1,), slots, jnp.int32), own[None]])
    result, d_middle, d_attended_t, d_ffn, d_out_w, d_gain_two, squared_part = feed_forward(
        ring_size, tile_info, scale, attended_t, tokens_here, teacher_here, w_o, g_two[None],
        ffn_all, out_width
    )
    d_attended_t = d_attended_t.reshape(seqs, HEADS, HEAD_DIM, slots)
    d_ffn = d_ffn.reshape(tp_size * fsdp_size, half, 3 * hidden_part)
    d_ffn = lax.psum_scatter(d_ffn, ("tp", "fsdp"), scatter_dimension=0, tiled=False)
    d_out_w = d_out_w.reshape(fsdp_size, half, out_width)
    output = move_back(result)
    out_steps = reduce_steps(d_out_w, own)
    loss_steps = sum_steps(squared_part)
    d_out_w = next(out_steps)
    loss_sum = next(loss_steps)

    calls = [(4 * outer - 2, 4 * outer - 1)]
    for k in reversed(range(1, outer)):
        calls.append((4 * k, 4 * k + 1, 4 * k - 2, 4 * k - 1))
    calls.append((0, 1))
    operands = [queries, d_attended_t, attended, lse]
    core_sums = {}
    sums = {}
    d_kv_terms = []
    for number, masks in enumerate(calls):
        last = number == len(calls) - 1
        if number:
            if number >= 2:
                due = list(calls[number - 2][::2])
            else:
                due = []
            held = [core_sums[m] for m in due] + [d_out_w, loss_sum]
            if number == 2:
                held.append(output)
            if number == 3:
                held.append(d_ffn)
            held = list(lax.optimization_barrier([info] + held))
            info = held.pop(0)
            if number == 3:
                d_ffn = lax.psum(held.pop(), "ctx")
            if number == 2:
                output = held.pop()
            loss_sum = advance(loss_steps, held.pop())
            d_out_w = advance(out_steps, held.pop())
            for mask, value in zip(due, held):
                core_sums[mask] = value
                if mask % 4:
                    sums[mask - 2] = swap(value, 2)
                else:
                    d_kv_terms.append((mask, swap(add_low(value, sums[mask]), mask)))
        parts, outs = attend_back(
            ring_size, masks, info, [kv[m] for m in masks], operands, number == 0, last
        )
        parts = list(parts)
        for place in range(0, 0 if last else len(masks), 2):
            core_sums[masks[place]] = add_low(parts[place], swap(parts[place + 1], 1))
        if number == 0:
            operands = [outs[1], outs[2], outs[0]]
        else:
            operands = operands[:2] + [outs[0]]
    d_query = outs[0]
    for mask in calls[-2][::2]:
        if mask % 4:
            sums[mask - 2] = swap(core_sums[mask], 2)
        else:
            d_kv_terms.append((mask, swap(add_low(core_sums[mask], sums[mask]), mask)))
    d_kv_terms += [(2, sums[0]), (1, swap(parts[1], 1))]
    d_ffn, parts[0] = lax.optimization_barrier((d_ffn, parts[0]))
    d_kv_halves = []
    for parity in range(2):
        total = parts[0][parity::2].astype(f32)
        for mask, term in d_kv_terms:
            from_it = (own > (own ^ mask)) == (parity == 1)
            total = total + jnp.where(from_it, term.astype(f32), 0.0)
        d_kv_halves.append(total)
    d_kv = jnp.stack(d_kv_halves, axis=1).reshape((seqs,) + parts[0].shape[1:])
    loss_sum = run_steps(loss_steps, loss_sum)
    loss_value = loss_sum[0, 0] / (count_total * width)
    d_out_w = run_steps(out_steps, d_out_w)
    d_ffn = d_ffn.astype(f32)

    d_qk = jnp.concatenate([d_query, d_kv[:, :, :HEAD_DIM]], axis=1)
    d_qk = rotate_cols(d_qk, cosine, -sine).astype(bf16).reshape(seqs, width + kv_width, slots)
    d_values = d_kv[:, :, HEAD_DIM:].astype(bf16).reshape(seqs, kv_width, slots)
    d_qkv = jnp.concatenate([d_qk, d_values], axis=1)
    d_normed = jnp.einsum("sfl,df->sld", d_qkv, w_qkv, preferred_element_type=f32)
    d_qkv_w = jnp.einsum("sld,sfl->df", normed, d_qkv, preferred_element_type=f32)
    norm_one_pull = jax.vjp(norm_rows, inputs, g_one)[1]
    d_inputs_norm, d_gain_one = norm_one_pull(d_normed)
    tokens_grad = d_middle + d_inputs_norm
    back = tokens_grad[1::2].astype(bf16)
    cut = 2 * width // 3 // 128 * 128
    back_parts = [mirror(back[..., :cut]), back[..., cut:]]
    d_packed = jnp.concatenate(
        [
            d_qkv_w,
            d_gain_one[:, None],
            d_gain_two.T,
            jnp.zeros((width, grad_width - qkv_width - 2), f32),
        ],
        axis=1,
    )
    steps = reduce_steps(d_packed.reshape(fsdp_size, half, grad_width), own)
    d_packed = next(steps)
    d_packed = steps.send(d_packed)
    d_packed = steps.send(d_packed)
    back_parts[0], d_packed = lax.optimization_barrier((back_parts[0], d_packed))
    d_packed = steps.send(d_packed)
    d_packed = steps.send(d_packed)
    back_parts[1], d_packed = lax.optimization_barrier((back_parts[1], d_packed))
    back = jnp.concatenate([back_parts[0], mirror(back_parts[1])], axis=2).astype(f32)
    tokens_grad = jnp.stack([tokens_grad[0::2], back], axis=1).reshape(tokens_grad.shape)
    d_packed = run_steps(steps, d_packed)
    return (
        output,
        loss_value,
        tokens_grad,
        d_packed[:, qkv_width],
        d_packed[:, :width],
        d_packed[:, width : width + kv_width],
        d_packed[:, width + kv_width : qkv_width],
        d_out_w[:, :width],
        d_packed[:, qkv_width + 1],
        d_ffn[:, :hidden_part],
        d_ffn[:, hidden_part : 2 * hidden_part],
        d_ffn[:, 2 * hidden_part :].T,
    )


def solution(mesh):
    slots_spec = P("fsdp", ("ctx", "tp"), None)
    rows_spec = P("fsdp", None)
    return jax.shard_map(
        shards,
        mesh=mesh,
        in_specs=(
            slots_spec,
            slots_spec,
            P("fsdp"),
            P("fsdp"),
            rows_spec,
            rows_spec,
            rows_spec,
            rows_spec,
            P("fsdp"),
            P("fsdp", "tp"),
            P("fsdp", "tp"),
            P("tp", "fsdp"),
        ),
        out_specs=(
            slots_spec,
            P(),
            slots_spec,
            P("fsdp"),
            rows_spec,
            rows_spec,
            rows_spec,
            rows_spec,
            P("fsdp"),
            P("fsdp", "tp"),
            P("fsdp", "tp"),
            P("tp", "fsdp"),
        ),
        check_vma=False,
    )
```

```python
import functools

import jax
import jax.numpy as jnp
from jax import lax
from jax.experimental import pallas as pl
from jax.experimental.pallas import tpu as pltpu
from jax.sharding import PartitionSpec as P

HEADS = 9
KV_HEADS = 3
GROUP = HEADS // KV_HEADS
HEAD_DIM = 64
AUG = HEAD_DIM + 16

EPS = 1e-05
ROPE_BASE = 10000.0
NEG = -1e30
LOG2E = 1.4426950408889634
EXP2_SCALE = LOG2E * HEAD_DIM ** (-0.5)

f32 = jnp.float32
bf16 = jnp.bfloat16
NN = ((1,), (0,))
TN = ((0,), (0,))
NT = ((1,), (1,))


def dot(left, right, dims):
    return lax.dot_general(left, right, (dims, ((), ())), preferred_element_type=f32)


def norm_rows(values, gain):
    return values * lax.rsqrt(jnp.mean(values * values, axis=-1, keepdims=True) + EPS) * gain


def rope_tables(positions):
    half_width = HEAD_DIM // 2
    frequency = ROPE_BASE ** (-(jnp.arange(half_width, dtype=f32) * 2.0) / HEAD_DIM)
    angles = frequency[None, None, :, None] * positions.astype(f32)[:, None, None, :]
    return (jnp.cos(angles), jnp.sin(angles))


def rotate_cols(values, cosine, sine):
    half_width = HEAD_DIM // 2
    lower = values[..., :half_width, :]
    upper = values[..., half_width:, :]
    return jnp.concatenate([lower * cosine - upper * sine, upper * cosine + lower * sine], axis=-2)


def three_pieces(row):
    first = row.astype(bf16)
    rest = row - first.astype(f32)
    second = rest.astype(bf16)
    third = (rest - second.astype(f32)).astype(bf16)
    return (first, second, third)


def penalty_row(block_start, width, length):
    key_pos = block_start + lax.broadcasted_iota(jnp.int32, (1, width), 1)
    return jnp.where(key_pos < length, 0.0, NEG).astype(bf16)


def extra_rows(rows, width):
    wide = jnp.zeros((16, width), f32)
    index = lax.broadcasted_iota(jnp.int32, (16, width), 0)
    for place, row in enumerate(rows):
        wide = jnp.where(index == place, row.astype(f32), wide)
    return wide.astype(bf16)


def block_of(device, seq, ring_size):
    return jnp.where(seq % 2 == 1, ring_size - 1 - device, device)


def needed(device, mask, seq):
    if mask == 0:
        return seq >= 0
    return (device ^ mask > device) == (seq % 2 == 1)


def pair_up(masks):
    groups = []
    for mask in masks:
        for group in groups:
            if len(group) == 1 and mask and masks[group[0]].bit_length() == mask.bit_length():
                group.append(masks.index(mask))
                break
        else:
            groups.append([masks.index(mask)])
    return groups


def forward_kernel(ring_size, masks, first, last, *refs):
    count = len(masks)
    info, q_ref = refs[:2]
    kv_refs = refs[2 : 2 + count]
    rest = refs[2 + count :]
    slots = kv_refs[0].shape[-1]
    cols = GROUP * slots
    if first:
        qa_ref, max_ref, acc_ref = rest
    else:
        qa_ref = q_ref
        if last:
            max_in, acc_in, out_ref, lse_ref, max_ref, acc_ref = rest
        else:
            max_in, acc_in, max_ref, acc_ref = rest
        max_ref[...] = max_in[...]
        acc_ref[...] = acc_in[...]
    device = info[info.shape[0] - 1]

    def step(seq, keys, values, penalty, diagonal):
        wide = keys.shape[1]
        key_cols = jnp.concatenate([keys, extra_rows([penalty], wide)], axis=0)
        value_ones = extra_rows([jnp.ones((1, wide), f32)], wide)
        value_cols = jnp.concatenate([values, value_ones], axis=0)
        scores = dot(key_cols, qa_ref[seq, 0], TN) * EXP2_SCALE
        if diagonal:
            key_at = lax.broadcasted_iota(jnp.int32, (slots, cols), 0)
            query_at = lax.broadcasted_iota(jnp.int32, (slots, cols), 1) % slots
            scores = jnp.where(key_at <= query_at, scores, NEG)
        old_max = max_ref[seq, 0]
        new_max = jnp.maximum(old_max, jnp.max(scores, axis=0, keepdims=True))
        weights = jnp.exp2(scores - new_max).astype(bf16)
        max_ref[seq, 0] = new_max
        acc_ref[seq, 0] = acc_ref[seq, 0] * jnp.exp2(old_max - new_max) + dot(value_cols, weights, NN)

    def work(seq, carry):
        if first:
            heads = [q_ref[seq, h] for h in range(GROUP)]
            qa_ref[seq, 0, 0:HEAD_DIM] = jnp.concatenate(heads, axis=1)
            qa_ref[seq, 0, HEAD_DIM:AUG] = extra_rows([jnp.ones((1, cols), f32)], cols)
            max_ref[seq] = jnp.full(max_ref.shape[1:], NEG, f32)
            acc_ref[seq] = jnp.zeros(acc_ref.shape[1:], f32)
        for group in pair_up(masks):
            mask = masks[group[0]]
            blocks = [block_of(device ^ masks[place], seq, ring_size) for place in group]
            at = seq // 2 if mask else seq
            start = functools.reduce(jnp.minimum, blocks) * slots

            @pl.when(needed(device, mask, seq) & (start < info[seq]))
            def _():
                penalty = [penalty_row(block * slots, slots, info[seq]) for block in blocks]
                keys = [kv_refs[place][at, 0, 0:HEAD_DIM] for place in group]
                values = [kv_refs[place][at, 0, HEAD_DIM:] for place in group]
                step(
                    seq,
                    jnp.concatenate(keys, axis=1),
                    jnp.concatenate(values, axis=1),
                    jnp.concatenate(penalty, axis=1),
                    mask == 0,
                )

        if last:
            total = acc_ref[seq, 0, HEAD_DIM : HEAD_DIM + 1]
            heads_out = acc_ref[seq, 0, 0:HEAD_DIM] / total
            lse_ref[seq, 0] = (max_ref[seq, 0] + jnp.log2(total)) * (1.0 / EXP2_SCALE)
            for h in range(GROUP):
                out_ref[seq, h] = heads_out[:, h * slots : (h + 1) * slots].astype(bf16)
        return carry

    lax.fori_loop(0, qa_ref.shape[0], work, 0)


def backward_kernel(ring_size, masks, first, last, *refs):
    count = len(masks)
    info = refs[0]
    kv_refs = refs[1 : 1 + count]
    rest = refs[1 + count :]
    slots = kv_refs[0].shape[-1]
    cols = GROUP * slots
    if first:
        q_ref, do_ref, o_ref, lse_ref = rest[:4]
        dkv_refs = rest[4 : 4 + count]
        acc_ref, qa_ref, da_ref = rest[4 + count :]
    else:
        qa_ref, da_ref, acc_in = rest[:3]
        dkv_refs = rest[3 : 3 + count]
        if last:
            dq_ref, acc_ref = rest[3 + count :]
        else:
            (acc_ref,) = rest[3 + count :]
        acc_ref[...] = acc_in[...]
    device = info[info.shape[0] - 1]

    def prepare(seq):
        grads = jnp.concatenate([do_ref[seq, h] for h in range(GROUP)], axis=1)
        heads_out = jnp.concatenate([o_ref[seq, h] for h in range(GROUP)], axis=1)
        delta = jnp.sum(grads.astype(f32) * heads_out.astype(f32), axis=0, keepdims=True)
        heads = [q_ref[seq, h] for h in range(GROUP)]
        qa_ref[seq, 0, 0:HEAD_DIM] = jnp.concatenate(heads, axis=1)
        qa_ref[seq, 0, HEAD_DIM:AUG] = extra_rows(
            three_pieces(-lse_ref[seq, 0]) + (jnp.ones((1, cols), f32),), cols
        )
        da_ref[seq, 0, 0:HEAD_DIM] = grads
        da_ref[seq, 0, HEAD_DIM:AUG] = extra_rows(three_pieces(-delta), cols)
        acc_ref[seq] = jnp.zeros(acc_ref.shape[1:], f32)

    def step(seq, keys, values, penalty, diagonal):
        wide = keys.shape[1]
        ones_key = jnp.ones((1, wide), f32)
        key_cols = jnp.concatenate([keys, extra_rows([ones_key] * 3 + [penalty], wide)], axis=0)
        value_cols = jnp.concatenate([values, extra_rows([ones_key] * 3, wide)], axis=0)
        scores = dot(qa_ref[seq, 0], key_cols, TN) * EXP2_SCALE
        if diagonal:
            query_at = lax.broadcasted_iota(jnp.int32, (cols, slots), 0) % slots
            key_at = lax.broadcasted_iota(jnp.int32, (cols, slots), 1)
            scores = jnp.where(key_at <= query_at, scores, NEG)
        weights = jnp.exp2(scores)
        d_scores = (weights * dot(da_ref[seq, 0], value_cols, TN)).astype(bf16)
        d_value = dot(da_ref[seq, 0, 0:HEAD_DIM], weights.astype(bf16), NN)
        d_key = dot(qa_ref[seq, 0, 0:HEAD_DIM], d_scores, NN) * (HEAD_DIM ** (-0.5))
        acc_ref[seq, 0] += dot(keys, d_scores, NT)
        return (d_key.astype(bf16), d_value.astype(bf16))

    def work(seq, carry):
        if first:
            prepare(seq)
        active = block_of(device, seq, ring_size) * slots < info[seq]
        for group in pair_up(masks):
            mask = masks[group[0]]
            blocks = [block_of(device ^ masks[place], seq, ring_size) for place in group]
            turn = needed(device, mask, seq)
            at = seq // 2 if mask else seq

            @pl.when(turn & active)
            def _():
                penalty = [penalty_row(block * slots, slots, info[seq]) for block in blocks]
                keys = [kv_refs[place][at, 0, 0:HEAD_DIM] for place in group]
                values = [kv_refs[place][at, 0, HEAD_DIM:] for place in group]
                d_key, d_value = step(
                    seq,
                    jnp.concatenate(keys, axis=1),
                    jnp.concatenate(values, axis=1),
                    jnp.concatenate(penalty, axis=1),
                    mask == 0,
                )
                for number, place in enumerate(group):
                    part = slice(number * slots, (number + 1) * slots)
                    dkv_refs[place][at, 0, 0:HEAD_DIM] = d_key[:, part]
                    dkv_refs[place][at, 0, HEAD_DIM:] = d_value[:, part]

            @pl.when(turn & jnp.logical_not(active))
            def _():
                for place in group:
                    dkv_refs[place][at] = jnp.zeros(dkv_refs[place].shape[1:], bf16)

        if last:
            d_query = acc_ref[seq, 0] * (HEAD_DIM ** (-0.5))
            for h in range(GROUP):
                dq_ref[seq, h] = d_query[:, h * slots : (h + 1) * slots]
        return carry

    lax.fori_loop(0, qa_ref.shape[0], work, 0)


def head_spec(seqs, rows, lanes, heads=1):
    return pl.BlockSpec((seqs, heads, rows, lanes), lambda group: (0, group, 0, 0))


def kv_specs(kvs):
    return [head_spec(kv.shape[0], kv.shape[2], kv.shape[3]) for kv in kvs]


SMEM_SPEC = pl.BlockSpec(memory_space=pltpu.SMEM)
PARAMS = pltpu.CompilerParams(vmem_limit_bytes=60 * 2**20)


def call_cost(kv_shape, count, products):
    seqs, groups, _, slots = kv_shape
    pairs = seqs * groups * GROUP * slots * slots * count
    return pl.CostEstimate(
        flops=pairs * HEAD_DIM * products * 4,
        transcendentals=pairs,
        bytes_accessed=seqs * groups * count * 4 * HEAD_DIM * slots,
    )


def attend(ring_size, masks, info, queries, kvs, state, last):
    first = state is None
    groups, slots = kvs[0].shape[1], kvs[0].shape[3]
    seqs = queries.shape[0]
    cols = GROUP * slots
    wide_spec = head_spec(seqs, AUG, cols)
    row_spec = head_spec(seqs, 1, cols)
    wide_shape = (seqs, groups, AUG, cols)
    row_shape = jax.ShapeDtypeStruct((seqs, groups, 1, cols), f32)
    state_specs = [row_spec, wide_spec]
    state_shapes = [row_shape, jax.ShapeDtypeStruct(wide_shape, f32)]
    query_spec = wide_spec
    scratch = []
    if first:
        query_spec = head_spec(seqs, HEAD_DIM, slots, GROUP)
        out_specs = [wide_spec] + state_specs
        out_shape = [jax.ShapeDtypeStruct(wide_shape, bf16)] + state_shapes
    elif last:
        out_specs = [head_spec(seqs, HEAD_DIM, slots, GROUP), row_spec]
        out_shape = [jax.ShapeDtypeStruct((seqs, groups * GROUP, HEAD_DIM, slots), bf16), row_shape]
        scratch = [pltpu.VMEM((seqs, 1, 1, cols), f32), pltpu.VMEM((seqs, 1, AUG, cols), f32)]
    else:
        out_specs = state_specs
        out_shape = state_shapes
    return pl.pallas_call(
        functools.partial(forward_kernel, ring_size, masks, first, last),
        grid=(groups,),
        in_specs=[SMEM_SPEC, query_spec]
        + kv_specs(kvs)
        + ([] if first else state_specs),
        out_specs=out_specs,
        out_shape=out_shape,
        scratch_shapes=scratch,
        compiler_params=PARAMS,
        cost_estimate=call_cost(kvs[0].shape, len(masks), 4),
        name="attend",
    )(info, queries, *kvs, *([] if first else state))


def attend_back(ring_size, masks, info, kvs, operands, first, last):
    groups, slots = kvs[0].shape[1], kvs[0].shape[3]
    seqs = operands[0].shape[0]
    cols = GROUP * slots
    heads_spec = head_spec(seqs, HEAD_DIM, slots, GROUP)
    wide_spec = head_spec(seqs, AUG, cols)
    acc_spec = head_spec(seqs, HEAD_DIM, cols)
    kv_shapes = [jax.ShapeDtypeStruct(kv.shape, bf16) for kv in kvs]
    wide_shape = jax.ShapeDtypeStruct((seqs, groups, AUG, cols), bf16)
    acc_shape = jax.ShapeDtypeStruct((seqs, groups, HEAD_DIM, cols), f32)
    scratch = []
    if first:
        operand_specs = [heads_spec] * 3 + [head_spec(seqs, 1, cols)]
        out_specs = [acc_spec, wide_spec, wide_spec]
        out_shape = [acc_shape, wide_shape, wide_shape]
    else:
        operand_specs = [wide_spec, wide_spec, acc_spec]
        if last:
            out_specs = [heads_spec]
            out_shape = [jax.ShapeDtypeStruct((seqs, groups * GROUP, HEAD_DIM, slots), f32)]
            scratch = [pltpu.VMEM((seqs, 1, HEAD_DIM, cols), f32)]
        else:
            out_specs = [acc_spec]
            out_shape = [acc_shape]
    outs = pl.pallas_call(
        functools.partial(backward_kernel, ring_size, masks, first, last),
        grid=(groups,),
        in_specs=[SMEM_SPEC] + kv_specs(kvs) + operand_specs,
        out_specs=kv_specs(kvs) + out_specs,
        out_shape=kv_shapes + out_shape,
        scratch_shapes=scratch,
        compiler_params=PARAMS,
        cost_estimate=call_cost(kvs[0].shape, len(masks), 10),
        name="attend_back",
    )(info, *kvs, *operands)
    return (outs[: len(masks)], outs[len(masks) :])


def feed_forward_kernel(
    ring_size, info, scale, att_ref, tok_ref, teach_ref, wo_ref, gain_ref, w_ref,
    out_ref, dmid_ref, datt_ref, dw_ref, dwo_ref, dgain_ref, loss_ref,
    slope_ref, silu_ref, hidden_ref, dw_acc, dwo_acc,
):
    tile = pl.program_id(0)
    parts, width, hidden3 = w_ref.shape
    part = hidden3 // 3
    tile_rows = tok_ref.shape[1]
    slots = info[info.shape[0] - 2]
    device = info[info.shape[0] - 1]
    seq = tile * tile_rows // slots
    first_pos = block_of(device, seq, ring_size) * slots + tile * tile_rows % slots

    @pl.when(tile == 0)
    def _():
        dw_acc[...] = jnp.zeros(dw_acc.shape, f32)
        dwo_acc[...] = jnp.zeros(dwo_acc.shape, f32)
        dgain_ref[...] = jnp.zeros(dgain_ref.shape, f32)
        loss_ref[...] = jnp.zeros(loss_ref.shape, f32)

    gain = gain_ref[...]
    att = att_ref[0]
    middle = tok_ref[0].astype(f32) + dot(att, wo_ref[...], TN)
    inverse = lax.rsqrt(jnp.mean(middle * middle, axis=-1, keepdims=True) + EPS)
    unit = middle * inverse
    normed = (unit * gain).astype(bf16)
    branch = jnp.zeros((tile_rows, width), f32)
    for t in range(parts):
        both = dot(normed, w_ref[t, :, : 2 * part], NN)
        gate = both[:, :part]
        up = both[:, part:]
        sigmoid = jax.nn.sigmoid(gate)
        silu = gate * sigmoid
        hidden = (silu * up).astype(bf16)
        slope_ref[t] = up * sigmoid * (1.0 + gate * (1.0 - sigmoid))
        silu_ref[t] = silu
        hidden_ref[t] = hidden
        branch = branch + dot(hidden, w_ref[t, :, 2 * part :], NT)
    result = middle + branch
    out_ref[0] = result
    row_pos = first_pos + lax.broadcasted_iota(jnp.int32, (tile_rows, 1), 0)
    valid = (row_pos < info[seq]).astype(f32)
    mismatch = valid * (result - teach_ref[0].astype(f32))
    loss_ref[...] += jnp.sum(mismatch * mismatch)
    d_result = mismatch * scale[0]
    d_branch = d_result.astype(bf16)
    d_normed = jnp.zeros((tile_rows, width), f32)
    for t in range(parts):
        d_hidden = dot(d_branch, w_ref[t, :, 2 * part :], NN)
        d_both = jnp.concatenate([d_hidden * slope_ref[t], d_hidden * silu_ref[t]], axis=1)
        d_both = d_both.astype(bf16)
        dw_acc[t, :, : 2 * part] += dot(normed, d_both, TN)
        dw_acc[t, :, 2 * part :] += dot(d_branch, hidden_ref[t], TN)
        d_normed = d_normed + dot(d_both, w_ref[t, :, : 2 * part], NT)
    dgain_ref[...] += jnp.sum(d_normed * unit, axis=0, keepdims=True)
    d_unit = d_normed * gain
    d_middle = d_result + inverse * (d_unit - unit * jnp.mean(d_unit * unit, axis=-1, keepdims=True))
    dmid_ref[0] = d_middle
    d_attn = d_middle.astype(bf16)
    datt_ref[0] = dot(wo_ref[...], d_attn, NT).astype(bf16)
    dwo_acc[...] += dot(att, d_attn, NN)

    @pl.when(tile == pl.num_programs(0) - 1)
    def _():
        dw_ref[...] = dw_acc[...].astype(bf16)
        dwo_ref[...] = jnp.zeros(dwo_ref.shape, bf16)
        dwo_ref[:, :width] = dwo_acc[...].astype(bf16)


def feed_forward(ring_size, info, scale, attended_t, tokens, teacher, w_o, gain, weights, out_width):
    seqs, slots, width = tokens.shape
    parts, _, hidden3 = weights.shape
    part = hidden3 // 3
    tile_rows = min(512, slots)
    per_seq = slots // tile_rows
    row_spec = pl.BlockSpec((1, tile_rows, width), lambda i: (i // per_seq, i % per_seq, 0))
    col_spec = pl.BlockSpec((1, width, tile_rows), lambda i: (i // per_seq, 0, i % per_seq))

    def whole(*shape):
        return pl.BlockSpec(shape, lambda i: (0,) * len(shape), pipeline_mode=pl.Buffered(1))

    def kept(*shape):
        return pl.BlockSpec(shape, lambda i: (0,) * len(shape))

    rows = seqs * slots
    return pl.pallas_call(
        functools.partial(feed_forward_kernel, ring_size),
        grid=(seqs * per_seq,),
        in_specs=[SMEM_SPEC, SMEM_SPEC, col_spec, row_spec, row_spec]
        + [whole(width, width), whole(1, width), whole(parts, width, hidden3)],
        out_specs=[row_spec, row_spec, col_spec]
        + [kept(parts, width, hidden3), kept(width, out_width), kept(1, width), kept(1, 128)],
        out_shape=[
            jax.ShapeDtypeStruct((seqs, slots, width), f32),
            jax.ShapeDtypeStruct((seqs, slots, width), f32),
            jax.ShapeDtypeStruct((seqs, width, slots), bf16),
            jax.ShapeDtypeStruct((parts, width, hidden3), bf16),
            jax.ShapeDtypeStruct((width, out_width), bf16),
            jax.ShapeDtypeStruct((1, width), f32),
            jax.ShapeDtypeStruct((1, 128), f32),
        ],
        scratch_shapes=[
            pltpu.VMEM((parts, tile_rows, part), f32),
            pltpu.VMEM((parts, tile_rows, part), f32),
            pltpu.VMEM((parts, tile_rows, part), bf16),
            pltpu.VMEM((parts, width, hidden3), f32),
            pltpu.VMEM((width, width), f32),
        ],
        compiler_params=PARAMS,
        cost_estimate=pl.CostEstimate(
            flops=6 * rows * width * (parts * hidden3 + width),
            transcendentals=rows * parts * part,
            bytes_accessed=rows * width * 20 + parts * width * hidden3 * 4,
        ),
        name="feed_forward",
    )(info, scale, attended_t, tokens, teacher, w_o, gain, weights)


RING = ("ctx", "tp")


def swap(value, mask):
    size = lax.axis_size(RING)
    return lax.ppermute(value, RING, [(i, i ^ mask) for i in range(size)])


def mirror(value):
    size = lax.axis_size(RING)
    return lax.ppermute(value, RING, [(i, size - 1 - i) for i in range(size)])


def mirror_odd(value):
    moved = mirror(value[1::2])
    seqs = value.shape[0]
    return jnp.concatenate(
        [moved[s // 2][None] if s % 2 else value[s][None] for s in range(seqs)], axis=0
    )


def move_back(value):
    moved = mirror(value[1::2].astype(bf16)).astype(f32)
    seqs = value.shape[0]
    return jnp.concatenate(
        [moved[s // 2][None] if s % 2 else value[s][None] for s in range(seqs)], axis=0
    )


def add_low(*parts):
    total = parts[0].astype(f32)
    for part in parts[1:]:
        total = total + part.astype(f32)
    return total.astype(bf16)


def gather_fsdp(value):
    if lax.axis_size("fsdp") != 2:
        return lax.all_gather(value, "fsdp", axis=0, tiled=False)
    other = lax.ppermute(value, "fsdp", [(0, 1), (1, 0)])
    at_zero = lax.axis_index("fsdp") == 0
    return jnp.stack([jnp.where(at_zero, value, other), jnp.where(at_zero, other, value)])


def pick_half(value, axis, index):
    half = value.shape[axis] // 2
    return lax.dynamic_slice_in_dim(value, index * half, half, axis)


def join_halves(mine, other, axis, index):
    return jnp.where(
        index == 0,
        jnp.concatenate([mine, other], axis=axis),
        jnp.concatenate([other, mine], axis=axis),
    )


def reduce_steps(value, own):
    fsdp_size, rows, columns = value.shape
    outer = lax.axis_size(RING) // 4
    core = own % 2
    column = (own // 2) % 2
    plane = own // 4
    value = value.astype(bf16)
    value = add_low(pick_half(value, 2, core), swap(pick_half(value, 2, 1 - core), 1))
    value = yield value
    if fsdp_size == 2:
        here = lax.axis_index("fsdp")
        away = lax.dynamic_index_in_dim(value, 1 - here, 0, False)
        mine = lax.dynamic_index_in_dim(value, here, 0, False)
        value = add_low(mine, lax.ppermute(away, "fsdp", [(0, 1), (1, 0)]))
    else:
        value = lax.psum_scatter(value, "fsdp", scatter_dimension=0, tiled=False)
    value = yield value
    value = add_low(pick_half(value, 1, column), swap(pick_half(value, 1, 1 - column), 2))
    value = yield value
    piece = rows // outer

    def rows_of(index):
        return lax.dynamic_slice_in_dim(value, index * piece, piece, 0)

    mine = add_low(
        rows_of(plane), *[swap(rows_of(plane ^ k), 4 * k) for k in range(1, outer)]
    )
    mine = yield mine
    whole = jnp.zeros((rows, columns // 4), bf16)
    whole = lax.dynamic_update_slice_in_dim(whole, mine, plane * piece, 0)
    for k in range(1, outer):
        whole = lax.dynamic_update_slice_in_dim(whole, swap(mine, 4 * k), (plane ^ k) * piece, 0)
    whole = yield whole
    whole = join_halves(whole, swap(whole, 2), 1, column)
    whole = yield whole
    yield join_halves(whole, swap(whole, 1), 1, core)


def sum_steps(value):
    mask = 1
    while mask < lax.axis_size(RING):
        value = yield value + swap(value, mask)
        mask *= 2
    if lax.axis_size("fsdp") == 2:
        value = value + lax.ppermute(value, "fsdp", [(0, 1), (1, 0)])
    else:
        value = lax.psum(value, "fsdp")
    yield value


def advance(steps, value):
    try:
        return steps.send(value)
    except StopIteration:
        return value


def run_steps(steps, value=None):
    while True:
        try:
            value = steps.send(value)
        except StopIteration:
            return value


def shards(
    tokens,
    teacher,
    lengths,
    gain_one,
    w_query,
    w_key,
    w_value,
    w_out,
    gain_two,
    w_gate,
    w_up,
    w_down,
):
    seqs, slots, width = tokens.shape
    kv_width = KV_HEADS * HEAD_DIM
    qkv_width = width + 2 * kv_width
    gain_at = qkv_width
    pack_width = -(-(gain_at + 2) // 128) * 128
    grad_width = -(-(qkv_width + 2) // 512) * 512
    half = w_query.shape[0]
    hidden_part = w_gate.shape[1]
    fsdp_size = lax.axis_size("fsdp")
    tp_size = lax.axis_size("tp")
    ring_size = lax.axis_size(RING)
    outer = ring_size // 4

    tokens_here = mirror_odd(tokens)
    count_total = jnp.sum(gather_fsdp(lengths)).astype(f32)
    packed = jnp.concatenate(
        [
            w_query,
            w_key,
            w_value,
            gain_one[:, None],
            gain_two[:, None],
            jnp.zeros((half, pack_width - gain_at - 2), bf16),
        ],
        axis=1,
    )
    packed = gather_fsdp(packed)
    packed = packed.reshape(width, pack_width)
    w_qkv = packed[:, :qkv_width]
    g_one = packed[:, gain_at].astype(f32)
    g_two = packed[:, gain_at + 1].astype(f32)
    ffn_pack = jnp.concatenate([w_gate, w_up, w_down.T], axis=1)

    own = lax.axis_index(RING).astype(jnp.int32)
    blocks = jnp.stack([block_of(own, s, ring_size) for s in range(seqs)])
    positions = blocks[:, None] * slots + jnp.arange(slots, dtype=jnp.int32)[None]
    cosine, sine = rope_tables(positions)
    info = jnp.concatenate([lengths.astype(jnp.int32), own[None]])

    inputs = tokens_here.astype(f32)
    normed = norm_rows(inputs, g_one).astype(bf16)
    qkv = jnp.einsum("df,sld->sfl", w_qkv, normed, preferred_element_type=f32)
    qk = qkv[:, : width + kv_width].reshape(seqs, HEADS + KV_HEADS, HEAD_DIM, slots)
    qk = rotate_cols(qk, cosine, sine).astype(bf16)
    queries = qk[:, :HEADS]
    values = qkv[:, width + kv_width :].astype(bf16).reshape(seqs, KV_HEADS, HEAD_DIM, slots)

    kv = {0: jnp.concatenate([qk[:, HEADS:], values], axis=2)}

    def outgoing(mask):
        return jnp.where(own < (own ^ mask), kv[0][0::2], kv[0][1::2])

    coming = {mask: swap(outgoing(mask), mask) for mask in [1, 2] + [4 * k for k in range(1, outer)]}
    calls = [(0,), (1, 2, 4)]
    for k in range(1, outer - 1):
        calls.append((4 * k - 1, 4 * k + 1, 4 * k + 2, 4 * k + 4))
    calls.append((4 * outer - 5, 4 * outer - 3, 4 * outer - 2, 4 * outer - 1))
    query_rows, *state = attend(ring_size, calls[0], info, queries, [kv[0]], None, False)
    for number, masks in enumerate(calls[1:], 1):
        if masks[-1] not in coming:
            coming[masks[-1]] = swap(coming[masks[-1] - 1], 1)
        later = [ffn_pack] if number == 1 else [w_out, teacher] if number == 2 else []
        *arrived, first_state = lax.optimization_barrier(
            [coming[m] for m in masks] + later + [state[0]]
        )
        if number == 1:
            ffn_all = lax.all_gather(arrived.pop(), ("tp", "fsdp"), axis=0, tiled=False)
            ffn_all = ffn_all.reshape(tp_size, width, 3 * hidden_part)
        if number == 2:
            teacher_here = mirror_odd(arrived.pop())
            w_o = gather_fsdp(arrived.pop()).reshape(width, width)
        kv.update(zip(masks, arrived))
        state = [first_state, state[1]]
        for mask in masks:
            if mask % 4 == 0:
                coming[mask + 2] = swap(kv[mask], 2)
                coming[mask + 1] = swap(kv[mask], 1)
            elif mask % 4 == 2 and mask + 1 not in coming:
                coming[mask + 1] = swap(kv[mask], 1)
        state = attend(
            ring_size, masks, info, query_rows, arrived, state, number == len(calls) - 1
        )
    attended, lse = state
    attended_t = attended.reshape(seqs, width, slots)

    slots_all = seqs * fsdp_size * slots * ring_size
    scale = (slots_all / count_total)[None]
    out_width = -(-width // 512) * 512
    tile_info = jnp.concatenate([lengths.astype(jnp.int32), jnp.full((1,), slots, jnp.int32), own[None]])
    result, d_middle, d_attended_t, d_ffn, d_out_w, d_gain_two, squared_part = feed_forward(
        ring_size, tile_info, scale, attended_t, tokens_here, teacher_here, w_o, g_two[None],
        ffn_all, out_width
    )
    d_attended_t = d_attended_t.reshape(seqs, HEADS, HEAD_DIM, slots)
    d_ffn = d_ffn.reshape(tp_size * fsdp_size, half, 3 * hidden_part)
    d_ffn = lax.psum_scatter(d_ffn, ("tp", "fsdp"), scatter_dimension=0, tiled=False)
    d_out_w = d_out_w.reshape(fsdp_size, half, out_width)
    output = move_back(result)
    out_steps = reduce_steps(d_out_w, own)
    loss_steps = sum_steps(squared_part)
    d_out_w = next(out_steps)
    loss_sum = next(loss_steps)

    calls = [(4 * outer - 2, 4 * outer - 1)]
    for k in reversed(range(1, outer)):
        calls.append((4 * k, 4 * k + 1, 4 * k - 2, 4 * k - 1))
    calls.append((0, 1))
    operands = [queries, d_attended_t, attended, lse]
    core_sums = {}
    sums = {}
    d_kv_terms = []
    for number, masks in enumerate(calls):
        last = number == len(calls) - 1
        if number:
            if number >= 2:
                due = list(calls[number - 2][::2])
            else:
                due = []
            held = [core_sums[m] for m in due] + [d_out_w, loss_sum]
            if number == 2:
                held.append(output)
            if number == 3:
                held.append(d_ffn)
            held = list(lax.optimization_barrier([info] + held))
            info = held.pop(0)
            if number == 3:
                d_ffn = lax.psum(held.pop(), "ctx")
            if number == 2:
                output = held.pop()
            loss_sum = advance(loss_steps, held.pop())
            d_out_w = advance(out_steps, held.pop()) if number < 5 else held.pop()
            for mask, value in zip(due, held):
                core_sums[mask] = value
                if mask % 4:
                    sums[mask - 2] = swap(value, 2)
                else:
                    d_kv_terms.append((mask, swap(add_low(value, sums[mask]), mask)))
        parts, outs = attend_back(
            ring_size, masks, info, [kv[m] for m in masks], operands, number == 0, last
        )
        parts = list(parts)
        for place in range(0, 0 if last else len(masks), 2):
            core_sums[masks[place]] = add_low(parts[place], swap(parts[place + 1], 1))
        if number == 0:
            operands = [outs[1], outs[2], outs[0]]
        else:
            operands = operands[:2] + [outs[0]]
    d_query = outs[0]
    for mask in calls[-2][::2]:
        if mask % 4:
            sums[mask - 2] = swap(core_sums[mask], 2)
        else:
            d_kv_terms.append((mask, swap(add_low(core_sums[mask], sums[mask]), mask)))
    d_kv_terms += [(2, sums[0]), (1, swap(parts[1], 1))]
    d_ffn, parts[0] = lax.optimization_barrier((d_ffn, parts[0]))
    d_kv_halves = []
    for parity in range(2):
        total = parts[0][parity::2].astype(f32)
        for mask, term in d_kv_terms:
            from_it = (own > (own ^ mask)) == (parity == 1)
            total = total + jnp.where(from_it, term.astype(f32), 0.0)
        d_kv_halves.append(total)
    d_kv = jnp.stack(d_kv_halves, axis=1).reshape((seqs,) + parts[0].shape[1:])
    loss_sum = run_steps(loss_steps, loss_sum)
    loss_value = loss_sum[0, 0] / (count_total * width)
    d_ffn = d_ffn.astype(f32)

    d_qk = jnp.concatenate([d_query, d_kv[:, :, :HEAD_DIM]], axis=1)
    d_qk = rotate_cols(d_qk, cosine, -sine).astype(bf16).reshape(seqs, width + kv_width, slots)
    d_values = d_kv[:, :, HEAD_DIM:].astype(bf16).reshape(seqs, kv_width, slots)
    d_qkv = jnp.concatenate([d_qk, d_values], axis=1)
    d_normed = jnp.einsum("sfl,df->sld", d_qkv, w_qkv, preferred_element_type=f32)
    d_qkv_w = jnp.einsum("sld,sfl->df", normed, d_qkv, preferred_element_type=f32)
    norm_one_pull = jax.vjp(norm_rows, inputs, g_one)[1]
    d_inputs_norm, d_gain_one = norm_one_pull(d_normed)
    tokens_grad = d_middle + d_inputs_norm
    back = tokens_grad[1::2].astype(bf16)
    cut = 2 * width // 3 // 128 * 128
    back_parts = [mirror(back[..., :cut]), back[..., cut:]]
    d_packed = jnp.concatenate(
        [
            d_qkv_w,
            d_gain_one[:, None],
            d_gain_two.T,
            jnp.zeros((width, grad_width - qkv_width - 2), f32),
        ],
        axis=1,
    )
    steps = reduce_steps(d_packed.reshape(fsdp_size, half, grad_width), own)
    d_packed = next(steps)
    d_packed = steps.send(d_packed)
    d_packed = steps.send(d_packed)
    back_parts[0], d_packed = lax.optimization_barrier((back_parts[0], d_packed))
    d_packed = steps.send(d_packed)
    d_packed = steps.send(d_packed)
    back_parts[1], d_packed = lax.optimization_barrier((back_parts[1], d_packed))
    back = jnp.concatenate([back_parts[0], mirror(back_parts[1])], axis=2).astype(f32)
    tokens_grad = jnp.stack([tokens_grad[0::2], back], axis=1).reshape(tokens_grad.shape)
    piece = d_packed.shape[1]
    d_packed = run_steps(steps, jnp.concatenate([d_packed, d_out_w], axis=1))
    pieces = d_packed.reshape(half, 4, piece + d_out_w.shape[1])
    d_packed = pieces[:, :, :piece].reshape(half, grad_width).astype(f32)
    d_out_w = pieces[:, :, piece:].reshape(half, out_width).astype(f32)
    return (
        output,
        loss_value,
        tokens_grad,
        d_packed[:, qkv_width],
        d_packed[:, :width],
        d_packed[:, width : width + kv_width],
        d_packed[:, width + kv_width : qkv_width],
        d_out_w[:, :width],
        d_packed[:, qkv_width + 1],
        d_ffn[:, :hidden_part],
        d_ffn[:, hidden_part : 2 * hidden_part],
        d_ffn[:, 2 * hidden_part :].T,
    )


def solution(mesh):
    slots_spec = P("fsdp", ("ctx", "tp"), None)
    rows_spec = P("fsdp", None)
    return jax.shard_map(
        shards,
        mesh=mesh,
        in_specs=(
            slots_spec,
            slots_spec,
            P("fsdp"),
            P("fsdp"),
            rows_spec,
            rows_spec,
            rows_spec,
            rows_spec,
            P("fsdp"),
            P("fsdp", "tp"),
            P("fsdp", "tp"),
            P("tp", "fsdp"),
        ),
        out_specs=(
            slots_spec,
            P(),
            slots_spec,
            P("fsdp"),
            rows_spec,
            rows_spec,
            rows_spec,
            rows_spec,
            P("fsdp"),
            P("fsdp", "tp"),
            P("fsdp", "tp"),
            P("tp", "fsdp"),
        ),
        check_vma=False,
    )
```

```python
import functools

import jax
import jax.numpy as jnp
from jax import lax
from jax.experimental import pallas as pl
from jax.experimental.pallas import tpu as pltpu
from jax.sharding import PartitionSpec as P

HEADS = 9
KV_HEADS = 3
GROUP = HEADS // KV_HEADS
HEAD_DIM = 64
AUG = HEAD_DIM + 16

EPS = 1e-05
ROPE_BASE = 10000.0
NEG = -1e30
LOG2E = 1.4426950408889634
EXP2_SCALE = LOG2E * HEAD_DIM ** (-0.5)

f32 = jnp.float32
bf16 = jnp.bfloat16
NN = ((1,), (0,))
TN = ((0,), (0,))
NT = ((1,), (1,))


def dot(left, right, dims):
    return lax.dot_general(left, right, (dims, ((), ())), preferred_element_type=f32)


def norm_rows(values, gain):
    return values * lax.rsqrt(jnp.mean(values * values, axis=-1, keepdims=True) + EPS) * gain


def rope_tables(positions):
    half_width = HEAD_DIM // 2
    frequency = ROPE_BASE ** (-(jnp.arange(half_width, dtype=f32) * 2.0) / HEAD_DIM)
    angles = frequency[None, None, :, None] * positions.astype(f32)[:, None, None, :]
    return (jnp.cos(angles), jnp.sin(angles))


def rotate_cols(values, cosine, sine):
    half_width = HEAD_DIM // 2
    lower = values[..., :half_width, :]
    upper = values[..., half_width:, :]
    return jnp.concatenate([lower * cosine - upper * sine, upper * cosine + lower * sine], axis=-2)


def three_pieces(row):
    first = row.astype(bf16)
    rest = row - first.astype(f32)
    second = rest.astype(bf16)
    third = (rest - second.astype(f32)).astype(bf16)
    return (first, second, third)


def penalty_row(block_start, width, length):
    key_pos = block_start + lax.broadcasted_iota(jnp.int32, (1, width), 1)
    return jnp.where(key_pos < length, 0.0, NEG).astype(bf16)


def extra_rows(rows, width):
    wide = jnp.zeros((16, width), f32)
    index = lax.broadcasted_iota(jnp.int32, (16, width), 0)
    for place, row in enumerate(rows):
        wide = jnp.where(index == place, row.astype(f32), wide)
    return wide.astype(bf16)


def block_of(device, seq, ring_size):
    return jnp.where(seq % 2 == 1, ring_size - 1 - device, device)


def needed(device, mask, seq):
    if mask == 0:
        return seq >= 0
    return (device ^ mask > device) == (seq % 2 == 1)


def pair_up(masks):
    groups = []
    for mask in masks:
        for group in groups:
            if len(group) == 1 and mask and masks[group[0]].bit_length() == mask.bit_length():
                group.append(masks.index(mask))
                break
        else:
            groups.append([masks.index(mask)])
    return groups


def forward_kernel(ring_size, masks, first, last, *refs):
    count = len(masks)
    info, q_ref = refs[:2]
    kv_refs = refs[2 : 2 + count]
    rest = refs[2 + count :]
    slots = kv_refs[0].shape[-1]
    cols = GROUP * slots
    if first:
        qa_ref, max_ref, acc_ref = rest
    else:
        qa_ref = q_ref
        if last:
            max_in, acc_in, out_ref, lse_ref, max_ref, acc_ref = rest
        else:
            max_in, acc_in, max_ref, acc_ref = rest
        max_ref[...] = max_in[...]
        acc_ref[...] = acc_in[...]
    device = info[info.shape[0] - 1]

    def step(seq, keys, values, penalty, diagonal):
        wide = keys.shape[1]
        key_cols = jnp.concatenate([keys, extra_rows([penalty], wide)], axis=0)
        value_ones = extra_rows([jnp.ones((1, wide), f32)], wide)
        value_cols = jnp.concatenate([values, value_ones], axis=0)
        scores = dot(key_cols, qa_ref[seq, 0], TN) * EXP2_SCALE
        if diagonal:
            key_at = lax.broadcasted_iota(jnp.int32, (slots, cols), 0)
            query_at = lax.broadcasted_iota(jnp.int32, (slots, cols), 1) % slots
            scores = jnp.where(key_at <= query_at, scores, NEG)
        old_max = max_ref[seq, 0]
        new_max = jnp.maximum(old_max, jnp.max(scores, axis=0, keepdims=True))
        weights = jnp.exp2(scores - new_max).astype(bf16)
        max_ref[seq, 0] = new_max
        acc_ref[seq, 0] = acc_ref[seq, 0] * jnp.exp2(old_max - new_max) + dot(value_cols, weights, NN)

    def work(seq, carry):
        if first:
            heads = [q_ref[seq, h] for h in range(GROUP)]
            qa_ref[seq, 0, 0:HEAD_DIM] = jnp.concatenate(heads, axis=1)
            qa_ref[seq, 0, HEAD_DIM:AUG] = extra_rows([jnp.ones((1, cols), f32)], cols)
            max_ref[seq] = jnp.full(max_ref.shape[1:], NEG, f32)
            acc_ref[seq] = jnp.zeros(acc_ref.shape[1:], f32)
        for group in pair_up(masks):
            mask = masks[group[0]]
            blocks = [block_of(device ^ masks[place], seq, ring_size) for place in group]
            at = seq // 2 if mask else seq
            start = functools.reduce(jnp.minimum, blocks) * slots

            @pl.when(needed(device, mask, seq) & (start < info[seq]))
            def _():
                penalty = [penalty_row(block * slots, slots, info[seq]) for block in blocks]
                keys = [kv_refs[place][at, 0, 0:HEAD_DIM] for place in group]
                values = [kv_refs[place][at, 0, HEAD_DIM:] for place in group]
                step(
                    seq,
                    jnp.concatenate(keys, axis=1),
                    jnp.concatenate(values, axis=1),
                    jnp.concatenate(penalty, axis=1),
                    mask == 0,
                )

        if last:
            total = acc_ref[seq, 0, HEAD_DIM : HEAD_DIM + 1]
            heads_out = acc_ref[seq, 0, 0:HEAD_DIM] / total
            lse_ref[seq, 0] = (max_ref[seq, 0] + jnp.log2(total)) * (1.0 / EXP2_SCALE)
            for h in range(GROUP):
                out_ref[seq, h] = heads_out[:, h * slots : (h + 1) * slots].astype(bf16)
        return carry

    lax.fori_loop(0, qa_ref.shape[0], work, 0)


def backward_kernel(ring_size, masks, first, last, *refs):
    count = len(masks)
    info = refs[0]
    kv_refs = refs[1 : 1 + count]
    rest = refs[1 + count :]
    slots = kv_refs[0].shape[-1]
    cols = GROUP * slots
    if first:
        q_ref, do_ref, o_ref, lse_ref = rest[:4]
        dkv_refs = rest[4 : 4 + count]
        acc_ref, qa_ref, da_ref = rest[4 + count :]
    else:
        qa_ref, da_ref, acc_in = rest[:3]
        dkv_refs = rest[3 : 3 + count]
        if last:
            dq_ref, acc_ref = rest[3 + count :]
        else:
            (acc_ref,) = rest[3 + count :]
        acc_ref[...] = acc_in[...]
    device = info[info.shape[0] - 1]

    def prepare(seq):
        grads = jnp.concatenate([do_ref[seq, h] for h in range(GROUP)], axis=1)
        heads_out = jnp.concatenate([o_ref[seq, h] for h in range(GROUP)], axis=1)
        delta = jnp.sum(grads.astype(f32) * heads_out.astype(f32), axis=0, keepdims=True)
        heads = [q_ref[seq, h] for h in range(GROUP)]
        qa_ref[seq, 0, 0:HEAD_DIM] = jnp.concatenate(heads, axis=1)
        qa_ref[seq, 0, HEAD_DIM:AUG] = extra_rows(
            three_pieces(-lse_ref[seq, 0]) + (jnp.ones((1, cols), f32),), cols
        )
        da_ref[seq, 0, 0:HEAD_DIM] = grads
        da_ref[seq, 0, HEAD_DIM:AUG] = extra_rows(three_pieces(-delta), cols)
        acc_ref[seq] = jnp.zeros(acc_ref.shape[1:], f32)

    def step(seq, keys, values, penalty, diagonal):
        wide = keys.shape[1]
        ones_key = jnp.ones((1, wide), f32)
        key_cols = jnp.concatenate([keys, extra_rows([ones_key] * 3 + [penalty], wide)], axis=0)
        value_cols = jnp.concatenate([values, extra_rows([ones_key] * 3, wide)], axis=0)
        scores = dot(qa_ref[seq, 0], key_cols, TN) * EXP2_SCALE
        if diagonal:
            query_at = lax.broadcasted_iota(jnp.int32, (cols, slots), 0) % slots
            key_at = lax.broadcasted_iota(jnp.int32, (cols, slots), 1)
            scores = jnp.where(key_at <= query_at, scores, NEG)
        weights = jnp.exp2(scores)
        d_scores = (weights * dot(da_ref[seq, 0], value_cols, TN)).astype(bf16)
        d_value = dot(da_ref[seq, 0, 0:HEAD_DIM], weights.astype(bf16), NN)
        d_key = dot(qa_ref[seq, 0, 0:HEAD_DIM], d_scores, NN) * (HEAD_DIM ** (-0.5))
        acc_ref[seq, 0] += dot(keys, d_scores, NT)
        return (d_key.astype(bf16), d_value.astype(bf16))

    def work(seq, carry):
        if first:
            prepare(seq)
        active = block_of(device, seq, ring_size) * slots < info[seq]
        for group in pair_up(masks):
            mask = masks[group[0]]
            blocks = [block_of(device ^ masks[place], seq, ring_size) for place in group]
            turn = needed(device, mask, seq)
            at = seq // 2 if mask else seq

            @pl.when(turn & active)
            def _():
                penalty = [penalty_row(block * slots, slots, info[seq]) for block in blocks]
                keys = [kv_refs[place][at, 0, 0:HEAD_DIM] for place in group]
                values = [kv_refs[place][at, 0, HEAD_DIM:] for place in group]
                d_key, d_value = step(
                    seq,
                    jnp.concatenate(keys, axis=1),
                    jnp.concatenate(values, axis=1),
                    jnp.concatenate(penalty, axis=1),
                    mask == 0,
                )
                for number, place in enumerate(group):
                    part = slice(number * slots, (number + 1) * slots)
                    dkv_refs[place][at, 0, 0:HEAD_DIM] = d_key[:, part]
                    dkv_refs[place][at, 0, HEAD_DIM:] = d_value[:, part]

            @pl.when(turn & jnp.logical_not(active))
            def _():
                for place in group:
                    dkv_refs[place][at] = jnp.zeros(dkv_refs[place].shape[1:], bf16)

        if last:
            d_query = acc_ref[seq, 0] * (HEAD_DIM ** (-0.5))
            for h in range(GROUP):
                dq_ref[seq, h] = d_query[:, h * slots : (h + 1) * slots]
        return carry

    lax.fori_loop(0, qa_ref.shape[0], work, 0)


def head_spec(seqs, rows, lanes, heads=1):
    return pl.BlockSpec((seqs, heads, rows, lanes), lambda group: (0, group, 0, 0))


def kv_specs(kvs):
    return [head_spec(kv.shape[0], kv.shape[2], kv.shape[3]) for kv in kvs]


SMEM_SPEC = pl.BlockSpec(memory_space=pltpu.SMEM)
PARAMS = pltpu.CompilerParams(vmem_limit_bytes=60 * 2**20)


def call_cost(kv_shape, count, products):
    seqs, groups, _, slots = kv_shape
    pairs = seqs * groups * GROUP * slots * slots * count
    return pl.CostEstimate(
        flops=pairs * HEAD_DIM * products * 4,
        transcendentals=pairs,
        bytes_accessed=seqs * groups * count * 4 * HEAD_DIM * slots,
    )


def attend(ring_size, masks, info, queries, kvs, state, last):
    first = state is None
    groups, slots = kvs[0].shape[1], kvs[0].shape[3]
    seqs = queries.shape[0]
    cols = GROUP * slots
    wide_spec = head_spec(seqs, AUG, cols)
    row_spec = head_spec(seqs, 1, cols)
    wide_shape = (seqs, groups, AUG, cols)
    row_shape = jax.ShapeDtypeStruct((seqs, groups, 1, cols), f32)
    state_specs = [row_spec, wide_spec]
    state_shapes = [row_shape, jax.ShapeDtypeStruct(wide_shape, f32)]
    query_spec = wide_spec
    scratch = []
    if first:
        query_spec = head_spec(seqs, HEAD_DIM, slots, GROUP)
        out_specs = [wide_spec] + state_specs
        out_shape = [jax.ShapeDtypeStruct(wide_shape, bf16)] + state_shapes
    elif last:
        out_specs = [head_spec(seqs, HEAD_DIM, slots, GROUP), row_spec]
        out_shape = [jax.ShapeDtypeStruct((seqs, groups * GROUP, HEAD_DIM, slots), bf16), row_shape]
        scratch = [pltpu.VMEM((seqs, 1, 1, cols), f32), pltpu.VMEM((seqs, 1, AUG, cols), f32)]
    else:
        out_specs = state_specs
        out_shape = state_shapes
    return pl.pallas_call(
        functools.partial(forward_kernel, ring_size, masks, first, last),
        grid=(groups,),
        in_specs=[SMEM_SPEC, query_spec]
        + kv_specs(kvs)
        + ([] if first else state_specs),
        out_specs=out_specs,
        out_shape=out_shape,
        scratch_shapes=scratch,
        compiler_params=PARAMS,
        cost_estimate=call_cost(kvs[0].shape, len(masks), 4),
        name="attend",
    )(info, queries, *kvs, *([] if first else state))


def attend_back(ring_size, masks, info, kvs, operands, first, last):
    groups, slots = kvs[0].shape[1], kvs[0].shape[3]
    seqs = operands[0].shape[0]
    cols = GROUP * slots
    heads_spec = head_spec(seqs, HEAD_DIM, slots, GROUP)
    wide_spec = head_spec(seqs, AUG, cols)
    acc_spec = head_spec(seqs, HEAD_DIM, cols)
    kv_shapes = [jax.ShapeDtypeStruct(kv.shape, bf16) for kv in kvs]
    wide_shape = jax.ShapeDtypeStruct((seqs, groups, AUG, cols), bf16)
    acc_shape = jax.ShapeDtypeStruct((seqs, groups, HEAD_DIM, cols), f32)
    scratch = []
    if first:
        operand_specs = [heads_spec] * 3 + [head_spec(seqs, 1, cols)]
        out_specs = [acc_spec, wide_spec, wide_spec]
        out_shape = [acc_shape, wide_shape, wide_shape]
    else:
        operand_specs = [wide_spec, wide_spec, acc_spec]
        if last:
            out_specs = [heads_spec]
            out_shape = [jax.ShapeDtypeStruct((seqs, groups * GROUP, HEAD_DIM, slots), f32)]
            scratch = [pltpu.VMEM((seqs, 1, HEAD_DIM, cols), f32)]
        else:
            out_specs = [acc_spec]
            out_shape = [acc_shape]
    outs = pl.pallas_call(
        functools.partial(backward_kernel, ring_size, masks, first, last),
        grid=(groups,),
        in_specs=[SMEM_SPEC] + kv_specs(kvs) + operand_specs,
        out_specs=kv_specs(kvs) + out_specs,
        out_shape=kv_shapes + out_shape,
        scratch_shapes=scratch,
        compiler_params=PARAMS,
        cost_estimate=call_cost(kvs[0].shape, len(masks), 10),
        name="attend_back",
    )(info, *kvs, *operands)
    return (outs[: len(masks)], outs[len(masks) :])


def feed_forward_kernel(
    ring_size, info, scale, att_ref, tok_ref, teach_ref, wo_ref, gain_ref, w_ref,
    out_ref, dmid_ref, datt_ref, dw_ref, dwo_ref, dgain_ref, loss_ref,
    slope_ref, silu_ref, hidden_ref, dw_acc, dwo_acc,
):
    tile = pl.program_id(0)
    parts, width, hidden3 = w_ref.shape
    part = hidden3 // 3
    tile_rows = tok_ref.shape[1]
    slots = info[info.shape[0] - 2]
    device = info[info.shape[0] - 1]
    seq = tile * tile_rows // slots
    first_pos = block_of(device, seq, ring_size) * slots + tile * tile_rows % slots

    @pl.when(tile == 0)
    def _():
        dw_acc[...] = jnp.zeros(dw_acc.shape, f32)
        dwo_acc[...] = jnp.zeros(dwo_acc.shape, f32)
        dgain_ref[...] = jnp.zeros(dgain_ref.shape, f32)
        loss_ref[...] = jnp.zeros(loss_ref.shape, f32)

    gain = gain_ref[...]
    att = att_ref[0]
    middle = tok_ref[0].astype(f32) + dot(att, wo_ref[...], TN)
    inverse = lax.rsqrt(jnp.mean(middle * middle, axis=-1, keepdims=True) + EPS)
    unit = middle * inverse
    normed = (unit * gain).astype(bf16)
    branch = jnp.zeros((tile_rows, width), f32)
    for t in range(parts):
        both = dot(normed, w_ref[t, :, : 2 * part], NN)
        gate = both[:, :part]
        up = both[:, part:]
        sigmoid = jax.nn.sigmoid(gate)
        silu = gate * sigmoid
        hidden = (silu * up).astype(bf16)
        slope_ref[t] = up * sigmoid * (1.0 + gate * (1.0 - sigmoid))
        silu_ref[t] = silu
        hidden_ref[t] = hidden
        branch = branch + dot(hidden, w_ref[t, :, 2 * part :], NT)
    result = middle + branch
    out_ref[0] = result
    row_pos = first_pos + lax.broadcasted_iota(jnp.int32, (tile_rows, 1), 0)
    valid = (row_pos < info[seq]).astype(f32)
    mismatch = valid * (result - teach_ref[0].astype(f32))
    loss_ref[...] += jnp.sum(mismatch * mismatch)
    d_result = mismatch * scale[0]
    d_branch = d_result.astype(bf16)
    d_normed = jnp.zeros((tile_rows, width), f32)
    for t in range(parts):
        d_hidden = dot(d_branch, w_ref[t, :, 2 * part :], NN)
        d_both = jnp.concatenate([d_hidden * slope_ref[t], d_hidden * silu_ref[t]], axis=1)
        d_both = d_both.astype(bf16)
        dw_acc[t, :, : 2 * part] += dot(normed, d_both, TN)
        dw_acc[t, :, 2 * part :] += dot(d_branch, hidden_ref[t], TN)
        d_normed = d_normed + dot(d_both, w_ref[t, :, : 2 * part], NT)
    dgain_ref[...] += jnp.sum(d_normed * unit, axis=0, keepdims=True)
    d_unit = d_normed * gain
    d_middle = d_result + inverse * (d_unit - unit * jnp.mean(d_unit * unit, axis=-1, keepdims=True))
    dmid_ref[0] = d_middle
    d_attn = d_middle.astype(bf16)
    datt_ref[0] = dot(wo_ref[...], d_attn, NT).astype(bf16)
    dwo_acc[...] += dot(att, d_attn, NN)

    @pl.when(tile == pl.num_programs(0) - 1)
    def _():
        dw_ref[...] = dw_acc[...].astype(bf16)
        dwo_ref[...] = jnp.zeros(dwo_ref.shape, bf16)
        dwo_ref[:, :width] = dwo_acc[...].astype(bf16)


def feed_forward(ring_size, info, scale, attended_t, tokens, teacher, w_o, gain, weights, out_width):
    seqs, slots, width = tokens.shape
    parts, _, hidden3 = weights.shape
    part = hidden3 // 3
    tile_rows = min(512, slots)
    per_seq = slots // tile_rows
    row_spec = pl.BlockSpec((1, tile_rows, width), lambda i: (i // per_seq, i % per_seq, 0))
    col_spec = pl.BlockSpec((1, width, tile_rows), lambda i: (i // per_seq, 0, i % per_seq))

    def whole(*shape):
        return pl.BlockSpec(shape, lambda i: (0,) * len(shape), pipeline_mode=pl.Buffered(1))

    def kept(*shape):
        return pl.BlockSpec(shape, lambda i: (0,) * len(shape))

    rows = seqs * slots
    return pl.pallas_call(
        functools.partial(feed_forward_kernel, ring_size),
        grid=(seqs * per_seq,),
        in_specs=[SMEM_SPEC, SMEM_SPEC, col_spec, row_spec, row_spec]
        + [whole(width, width), whole(1, width), whole(parts, width, hidden3)],
        out_specs=[row_spec, row_spec, col_spec]
        + [kept(parts, width, hidden3), kept(width, out_width), kept(1, width), kept(1, 128)],
        out_shape=[
            jax.ShapeDtypeStruct((seqs, slots, width), f32),
            jax.ShapeDtypeStruct((seqs, slots, width), f32),
            jax.ShapeDtypeStruct((seqs, width, slots), bf16),
            jax.ShapeDtypeStruct((parts, width, hidden3), bf16),
            jax.ShapeDtypeStruct((width, out_width), bf16),
            jax.ShapeDtypeStruct((1, width), f32),
            jax.ShapeDtypeStruct((1, 128), f32),
        ],
        scratch_shapes=[
            pltpu.VMEM((parts, tile_rows, part), f32),
            pltpu.VMEM((parts, tile_rows, part), f32),
            pltpu.VMEM((parts, tile_rows, part), bf16),
            pltpu.VMEM((parts, width, hidden3), f32),
            pltpu.VMEM((width, width), f32),
        ],
        compiler_params=PARAMS,
        cost_estimate=pl.CostEstimate(
            flops=6 * rows * width * (parts * hidden3 + width),
            transcendentals=rows * parts * part,
            bytes_accessed=rows * width * 20 + parts * width * hidden3 * 4,
        ),
        name="feed_forward",
    )(info, scale, attended_t, tokens, teacher, w_o, gain, weights)


RING = ("ctx", "tp")


def swap(value, mask):
    size = lax.axis_size(RING)
    return lax.ppermute(value, RING, [(i, i ^ mask) for i in range(size)])


def mirror(value):
    size = lax.axis_size(RING)
    return lax.ppermute(value, RING, [(i, size - 1 - i) for i in range(size)])


def mirror_odd(value):
    moved = mirror(value[1::2])
    seqs = value.shape[0]
    return jnp.concatenate(
        [moved[s // 2][None] if s % 2 else value[s][None] for s in range(seqs)], axis=0
    )


def move_back(value):
    moved = mirror(value[1::2].astype(bf16)).astype(f32)
    seqs = value.shape[0]
    return jnp.concatenate(
        [moved[s // 2][None] if s % 2 else value[s][None] for s in range(seqs)], axis=0
    )


def add_low(*parts):
    total = parts[0].astype(f32)
    for part in parts[1:]:
        total = total + part.astype(f32)
    return total.astype(bf16)


def gather_fsdp(value):
    if lax.axis_size("fsdp") != 2:
        return lax.all_gather(value, "fsdp", axis=0, tiled=False)
    other = lax.ppermute(value, "fsdp", [(0, 1), (1, 0)])
    at_zero = lax.axis_index("fsdp") == 0
    return jnp.stack([jnp.where(at_zero, value, other), jnp.where(at_zero, other, value)])


def pick_half(value, axis, index):
    half = value.shape[axis] // 2
    return lax.dynamic_slice_in_dim(value, index * half, half, axis)


def join_halves(mine, other, axis, index):
    return jnp.where(
        index == 0,
        jnp.concatenate([mine, other], axis=axis),
        jnp.concatenate([other, mine], axis=axis),
    )


def reduce_steps(value, own):
    fsdp_size, rows, columns = value.shape
    outer = lax.axis_size(RING) // 4
    core = own % 2
    column = (own // 2) % 2
    plane = own // 4
    value = value.astype(bf16)
    value = add_low(pick_half(value, 2, core), swap(pick_half(value, 2, 1 - core), 1))
    value = yield value
    if fsdp_size == 2:
        here = lax.axis_index("fsdp")
        away = lax.dynamic_index_in_dim(value, 1 - here, 0, False)
        mine = lax.dynamic_index_in_dim(value, here, 0, False)
        value = add_low(mine, lax.ppermute(away, "fsdp", [(0, 1), (1, 0)]))
    else:
        value = lax.psum_scatter(value, "fsdp", scatter_dimension=0, tiled=False)
    value = yield value
    value = add_low(pick_half(value, 1, column), swap(pick_half(value, 1, 1 - column), 2))
    value = yield value
    piece = rows // outer

    def rows_of(index):
        return lax.dynamic_slice_in_dim(value, index * piece, piece, 0)

    mine = add_low(
        rows_of(plane), *[swap(rows_of(plane ^ k), 4 * k) for k in range(1, outer)]
    )
    mine = yield mine
    whole = jnp.zeros((rows, columns // 4), bf16)
    whole = lax.dynamic_update_slice_in_dim(whole, mine, plane * piece, 0)
    for k in range(1, outer):
        whole = lax.dynamic_update_slice_in_dim(whole, swap(mine, 4 * k), (plane ^ k) * piece, 0)
    whole = yield whole
    whole = join_halves(whole, swap(whole, 2), 1, column)
    whole = yield whole
    yield join_halves(whole, swap(whole, 1), 1, core)


def sum_steps(value):
    mask = 1
    while mask < lax.axis_size(RING):
        value = yield value + swap(value, mask)
        mask *= 2
    if lax.axis_size("fsdp") == 2:
        value = value + lax.ppermute(value, "fsdp", [(0, 1), (1, 0)])
    else:
        value = lax.psum(value, "fsdp")
    yield value


def advance(steps, value):
    try:
        return steps.send(value)
    except StopIteration:
        return value


def run_steps(steps, value=None):
    while True:
        try:
            value = steps.send(value)
        except StopIteration:
            return value


def shards(
    tokens,
    teacher,
    lengths,
    gain_one,
    w_query,
    w_key,
    w_value,
    w_out,
    gain_two,
    w_gate,
    w_up,
    w_down,
):
    seqs, slots, width = tokens.shape
    kv_width = KV_HEADS * HEAD_DIM
    qkv_width = width + 2 * kv_width
    gain_at = qkv_width
    pack_width = -(-(gain_at + 2) // 128) * 128
    grad_width = -(-(qkv_width + 2) // 512) * 512
    half = w_query.shape[0]
    hidden_part = w_gate.shape[1]
    fsdp_size = lax.axis_size("fsdp")
    tp_size = lax.axis_size("tp")
    ring_size = lax.axis_size(RING)
    outer = ring_size // 4

    tokens_here = mirror_odd(tokens)
    count_total = jnp.sum(gather_fsdp(lengths)).astype(f32)
    packed = jnp.concatenate(
        [
            w_query,
            w_key,
            w_value,
            gain_one[:, None],
            gain_two[:, None],
            jnp.zeros((half, pack_width - gain_at - 2), bf16),
        ],
        axis=1,
    )
    packed = gather_fsdp(packed)
    packed = packed.reshape(width, pack_width)
    w_qkv = packed[:, :qkv_width]
    g_one = packed[:, gain_at].astype(f32)
    g_two = packed[:, gain_at + 1].astype(f32)
    ffn_pack = jnp.concatenate([w_gate, w_up, w_down.T], axis=1)

    own = lax.axis_index(RING).astype(jnp.int32)
    blocks = jnp.stack([block_of(own, s, ring_size) for s in range(seqs)])
    positions = blocks[:, None] * slots + jnp.arange(slots, dtype=jnp.int32)[None]
    cosine, sine = rope_tables(positions)
    info = jnp.concatenate([lengths.astype(jnp.int32), own[None]])

    inputs = tokens_here.astype(f32)
    normed = norm_rows(inputs, g_one).astype(bf16)
    qkv = jnp.einsum("df,sld->sfl", w_qkv, normed, preferred_element_type=f32)
    qk = qkv[:, : width + kv_width].reshape(seqs, HEADS + KV_HEADS, HEAD_DIM, slots)
    qk = rotate_cols(qk, cosine, sine).astype(bf16)
    queries = qk[:, :HEADS]
    values = qkv[:, width + kv_width :].astype(bf16).reshape(seqs, KV_HEADS, HEAD_DIM, slots)

    kv = {0: jnp.concatenate([qk[:, HEADS:], values], axis=2)}

    def outgoing(mask):
        return jnp.where(own < (own ^ mask), kv[0][0::2], kv[0][1::2])

    coming = {mask: swap(outgoing(mask), mask) for mask in [1, 2] + [4 * k for k in range(1, outer)]}
    calls = [(0,), (1, 2, 4)]
    for k in range(1, outer - 1):
        calls.append((4 * k - 1, 4 * k + 1, 4 * k + 2, 4 * k + 4))
    calls.append((4 * outer - 5, 4 * outer - 3, 4 * outer - 2, 4 * outer - 1))
    query_rows, *state = attend(ring_size, calls[0], info, queries, [kv[0]], None, False)
    for number, masks in enumerate(calls[1:], 1):
        if masks[-1] not in coming:
            coming[masks[-1]] = swap(coming[masks[-1] - 1], 1)
        later = {2: [ffn_pack], 3: [w_out, teacher]}.get(number, [])
        *arrived, first_state = lax.optimization_barrier(
            [coming[m] for m in masks] + later + [state[0]]
        )
        if number == 2:
            ffn_all = lax.all_gather(arrived.pop(), ("tp", "fsdp"), axis=0, tiled=False)
            ffn_all = ffn_all.reshape(tp_size, width, 3 * hidden_part)
        if number == 3:
            teacher_here = mirror_odd(arrived.pop())
            w_o = gather_fsdp(arrived.pop()).reshape(width, width)
        kv.update(zip(masks, arrived))
        state = [first_state, state[1]]
        for mask in masks:
            if mask % 4 == 0:
                coming[mask + 2] = swap(kv[mask], 2)
                coming[mask + 1] = swap(kv[mask], 1)
            elif mask % 4 == 2 and mask + 1 not in coming:
                coming[mask + 1] = swap(kv[mask], 1)
        state = attend(
            ring_size, masks, info, query_rows, arrived, state, number == len(calls) - 1
        )
    attended, lse = state
    attended_t = attended.reshape(seqs, width, slots)

    slots_all = seqs * fsdp_size * slots * ring_size
    scale = (slots_all / count_total)[None]
    out_width = -(-width // 512) * 512
    tile_info = jnp.concatenate([lengths.astype(jnp.int32), jnp.full((1,), slots, jnp.int32), own[None]])
    result, d_middle, d_attended_t, d_ffn, d_out_w, d_gain_two, squared_part = feed_forward(
        ring_size, tile_info, scale, attended_t, tokens_here, teacher_here, w_o, g_two[None],
        ffn_all, out_width
    )
    d_attended_t = d_attended_t.reshape(seqs, HEADS, HEAD_DIM, slots)
    d_ffn = d_ffn.reshape(tp_size * fsdp_size, half, 3 * hidden_part)
    d_ffn = lax.psum_scatter(d_ffn, ("tp", "fsdp"), scatter_dimension=0, tiled=False)
    d_out_w = d_out_w.reshape(fsdp_size, half, out_width)
    output = move_back(result)
    out_steps = reduce_steps(d_out_w, own)
    loss_steps = sum_steps(squared_part)
    d_out_w = next(out_steps)
    loss_sum = next(loss_steps)

    calls = [(4 * outer - 2, 4 * outer - 1)]
    for k in reversed(range(1, outer)):
        calls.append((4 * k, 4 * k + 1, 4 * k - 2, 4 * k - 1))
    calls.append((0, 1))
    operands = [queries, d_attended_t, attended, lse]
    core_sums = {}
    sums = {}
    d_kv_terms = []
    for number, masks in enumerate(calls):
        last = number == len(calls) - 1
        if number:
            if number >= 2:
                due = list(calls[number - 2][::2])
            else:
                due = []
            held = [core_sums[m] for m in due] + [d_out_w, loss_sum]
            if number == 2:
                held.append(output)
            if number == 3:
                held.append(d_ffn)
            held = list(lax.optimization_barrier([info] + held))
            info = held.pop(0)
            if number == 3:
                d_ffn = lax.psum(held.pop(), "ctx")
            if number == 2:
                output = held.pop()
            loss_sum = advance(loss_steps, held.pop())
            d_out_w = advance(out_steps, held.pop()) if number < 5 else held.pop()
            for mask, value in zip(due, held):
                core_sums[mask] = value
                if mask % 4:
                    sums[mask - 2] = swap(value, 2)
                else:
                    d_kv_terms.append((mask, swap(add_low(value, sums[mask]), mask)))
        parts, outs = attend_back(
            ring_size, masks, info, [kv[m] for m in masks], operands, number == 0, last
        )
        parts = list(parts)
        for place in range(0, 0 if last else len(masks), 2):
            core_sums[masks[place]] = add_low(parts[place], swap(parts[place + 1], 1))
        if number == 0:
            operands = [outs[1], outs[2], outs[0]]
        else:
            operands = operands[:2] + [outs[0]]
    d_query = outs[0]
    for mask in calls[-2][::2]:
        if mask % 4:
            sums[mask - 2] = swap(core_sums[mask], 2)
        else:
            d_kv_terms.append((mask, swap(add_low(core_sums[mask], sums[mask]), mask)))
    d_kv_terms += [(2, sums[0]), (1, swap(parts[1], 1))]
    d_ffn, parts[0] = lax.optimization_barrier((d_ffn, parts[0]))
    d_kv_halves = []
    for parity in range(2):
        total = parts[0][parity::2].astype(f32)
        for mask, term in d_kv_terms:
            from_it = (own > (own ^ mask)) == (parity == 1)
            total = total + jnp.where(from_it, term.astype(f32), 0.0)
        d_kv_halves.append(total)
    d_kv = jnp.stack(d_kv_halves, axis=1).reshape((seqs,) + parts[0].shape[1:])
    loss_sum = run_steps(loss_steps, loss_sum)
    loss_value = loss_sum[0, 0] / (count_total * width)
    d_ffn = d_ffn.astype(f32)

    d_qk = jnp.concatenate([d_query, d_kv[:, :, :HEAD_DIM]], axis=1)
    d_qk = rotate_cols(d_qk, cosine, -sine).astype(bf16).reshape(seqs, width + kv_width, slots)
    d_values = d_kv[:, :, HEAD_DIM:].astype(bf16).reshape(seqs, kv_width, slots)
    d_qkv = jnp.concatenate([d_qk, d_values], axis=1)
    d_normed = jnp.einsum("sfl,df->sld", d_qkv, w_qkv, preferred_element_type=f32)
    d_qkv_w = jnp.einsum("sld,sfl->df", normed, d_qkv, preferred_element_type=f32)
    norm_one_pull = jax.vjp(norm_rows, inputs, g_one)[1]
    d_inputs_norm, d_gain_one = norm_one_pull(d_normed)
    tokens_grad = d_middle + d_inputs_norm
    back = tokens_grad[1::2].astype(bf16)
    cut = 2 * width // 3 // 128 * 128
    back_parts = [mirror(back[..., :cut]), back[..., cut:]]
    d_packed = jnp.concatenate(
        [
            d_qkv_w,
            d_gain_one[:, None],
            d_gain_two.T,
            jnp.zeros((width, grad_width - qkv_width - 2), f32),
        ],
        axis=1,
    )
    steps = reduce_steps(d_packed.reshape(fsdp_size, half, grad_width), own)
    d_packed = next(steps)
    d_packed = steps.send(d_packed)
    d_packed = steps.send(d_packed)
    back_parts[0], d_packed = lax.optimization_barrier((back_parts[0], d_packed))
    d_packed = steps.send(d_packed)
    d_packed = steps.send(d_packed)
    back_parts[1], d_packed = lax.optimization_barrier((back_parts[1], d_packed))
    back = jnp.concatenate([back_parts[0], mirror(back_parts[1])], axis=2).astype(f32)
    tokens_grad = jnp.stack([tokens_grad[0::2], back], axis=1).reshape(tokens_grad.shape)
    piece = d_packed.shape[1]
    d_packed = run_steps(steps, jnp.concatenate([d_packed, d_out_w], axis=1))
    pieces = d_packed.reshape(half, 4, piece + d_out_w.shape[1])
    d_packed = pieces[:, :, :piece].reshape(half, grad_width).astype(f32)
    d_out_w = pieces[:, :, piece:].reshape(half, out_width).astype(f32)
    return (
        output,
        loss_value,
        tokens_grad,
        d_packed[:, qkv_width],
        d_packed[:, :width],
        d_packed[:, width : width + kv_width],
        d_packed[:, width + kv_width : qkv_width],
        d_out_w[:, :width],
        d_packed[:, qkv_width + 1],
        d_ffn[:, :hidden_part],
        d_ffn[:, hidden_part : 2 * hidden_part],
        d_ffn[:, 2 * hidden_part :].T,
    )


def solution(mesh):
    slots_spec = P("fsdp", ("ctx", "tp"), None)
    rows_spec = P("fsdp", None)
    return jax.shard_map(
        shards,
        mesh=mesh,
        in_specs=(
            slots_spec,
            slots_spec,
            P("fsdp"),
            P("fsdp"),
            rows_spec,
            rows_spec,
            rows_spec,
            rows_spec,
            P("fsdp"),
            P("fsdp", "tp"),
            P("fsdp", "tp"),
            P("tp", "fsdp"),
        ),
        out_specs=(
            slots_spec,
            P(),
            slots_spec,
            P("fsdp"),
            rows_spec,
            rows_spec,
            rows_spec,
            rows_spec,
            P("fsdp"),
            P("fsdp", "tp"),
            P("fsdp", "tp"),
            P("tp", "fsdp"),
        ),
        check_vma=False,
    )
```

```python
import functools

import jax
import jax.numpy as jnp
from jax import lax
from jax.experimental import pallas as pl
from jax.experimental.pallas import tpu as pltpu
from jax.sharding import PartitionSpec as P

HEADS = 9
KV_HEADS = 3
GROUP = HEADS // KV_HEADS
HEAD_DIM = 64
AUG = HEAD_DIM + 16

EPS = 1e-05
ROPE_BASE = 10000.0
NEG = -1e30
LOG2E = 1.4426950408889634
EXP2_SCALE = LOG2E * HEAD_DIM ** (-0.5)

f32 = jnp.float32
bf16 = jnp.bfloat16
NN = ((1,), (0,))
TN = ((0,), (0,))
NT = ((1,), (1,))


def dot(left, right, dims):
    return lax.dot_general(left, right, (dims, ((), ())), preferred_element_type=f32)


def norm_rows(values, gain):
    return values * lax.rsqrt(jnp.mean(values * values, axis=-1, keepdims=True) + EPS) * gain


def rope_tables(positions):
    half_width = HEAD_DIM // 2
    frequency = ROPE_BASE ** (-(jnp.arange(half_width, dtype=f32) * 2.0) / HEAD_DIM)
    angles = frequency[None, None, :, None] * positions.astype(f32)[:, None, None, :]
    return (jnp.cos(angles), jnp.sin(angles))


def rotate_cols(values, cosine, sine):
    half_width = HEAD_DIM // 2
    lower = values[..., :half_width, :]
    upper = values[..., half_width:, :]
    return jnp.concatenate([lower * cosine - upper * sine, upper * cosine + lower * sine], axis=-2)


def three_pieces(row):
    first = row.astype(bf16)
    rest = row - first.astype(f32)
    second = rest.astype(bf16)
    third = (rest - second.astype(f32)).astype(bf16)
    return (first, second, third)


def penalty_row(block_start, width, length):
    key_pos = block_start + lax.broadcasted_iota(jnp.int32, (1, width), 1)
    return jnp.where(key_pos < length, 0.0, NEG).astype(bf16)


def extra_rows(rows, width):
    wide = jnp.zeros((16, width), f32)
    index = lax.broadcasted_iota(jnp.int32, (16, width), 0)
    for place, row in enumerate(rows):
        wide = jnp.where(index == place, row.astype(f32), wide)
    return wide.astype(bf16)


def block_of(device, seq, ring_size):
    return jnp.where(seq % 2 == 1, ring_size - 1 - device, device)


def needed(device, mask, seq):
    if mask == 0:
        return seq >= 0
    return (device ^ mask > device) == (seq % 2 == 1)


def pair_up(masks):
    groups = []
    for mask in masks:
        for group in groups:
            if len(group) == 1 and mask and masks[group[0]].bit_length() == mask.bit_length():
                group.append(masks.index(mask))
                break
        else:
            groups.append([masks.index(mask)])
    return groups


def forward_kernel(ring_size, masks, first, last, *refs):
    count = len(masks)
    info, q_ref = refs[:2]
    kv_refs = refs[2 : 2 + count]
    rest = refs[2 + count :]
    slots = kv_refs[0].shape[-1]
    cols = GROUP * slots
    if first:
        qa_ref, max_ref, acc_ref = rest
    else:
        qa_ref = q_ref
        if last:
            max_in, acc_in, out_ref, lse_ref, max_ref, acc_ref = rest
        else:
            max_in, acc_in, max_ref, acc_ref = rest
        max_ref[...] = max_in[...]
        acc_ref[...] = acc_in[...]
    device = info[info.shape[0] - 1]

    def step(seq, keys, values, penalty, diagonal):
        wide = keys.shape[1]
        key_cols = jnp.concatenate([keys, extra_rows([penalty], wide)], axis=0)
        value_ones = extra_rows([jnp.ones((1, wide), f32)], wide)
        value_cols = jnp.concatenate([values, value_ones], axis=0)
        scores = dot(key_cols, qa_ref[seq, 0], TN) * EXP2_SCALE
        if diagonal:
            key_at = lax.broadcasted_iota(jnp.int32, (slots, cols), 0)
            query_at = lax.broadcasted_iota(jnp.int32, (slots, cols), 1) % slots
            scores = jnp.where(key_at <= query_at, scores, NEG)
        old_max = max_ref[seq, 0]
        new_max = jnp.maximum(old_max, jnp.max(scores, axis=0, keepdims=True))
        weights = jnp.exp2(scores - new_max).astype(bf16)
        max_ref[seq, 0] = new_max
        acc_ref[seq, 0] = acc_ref[seq, 0] * jnp.exp2(old_max - new_max) + dot(value_cols, weights, NN)

    def work(seq, carry):
        if first:
            heads = [q_ref[seq, h] for h in range(GROUP)]
            qa_ref[seq, 0, 0:HEAD_DIM] = jnp.concatenate(heads, axis=1)
            qa_ref[seq, 0, HEAD_DIM:AUG] = extra_rows([jnp.ones((1, cols), f32)], cols)
            max_ref[seq] = jnp.full(max_ref.shape[1:], NEG, f32)
            acc_ref[seq] = jnp.zeros(acc_ref.shape[1:], f32)
        for group in pair_up(masks):
            mask = masks[group[0]]
            blocks = [block_of(device ^ masks[place], seq, ring_size) for place in group]
            at = seq // 2 if mask else seq
            start = functools.reduce(jnp.minimum, blocks) * slots

            @pl.when(needed(device, mask, seq) & (start < info[seq]))
            def _():
                penalty = [penalty_row(block * slots, slots, info[seq]) for block in blocks]
                keys = [kv_refs[place][at, 0, 0:HEAD_DIM] for place in group]
                values = [kv_refs[place][at, 0, HEAD_DIM:] for place in group]
                step(
                    seq,
                    jnp.concatenate(keys, axis=1),
                    jnp.concatenate(values, axis=1),
                    jnp.concatenate(penalty, axis=1),
                    mask == 0,
                )

        if last:
            total = acc_ref[seq, 0, HEAD_DIM : HEAD_DIM + 1]
            heads_out = acc_ref[seq, 0, 0:HEAD_DIM] / total
            lse_ref[seq, 0] = (max_ref[seq, 0] + jnp.log2(total)) * (1.0 / EXP2_SCALE)
            for h in range(GROUP):
                out_ref[seq, h] = heads_out[:, h * slots : (h + 1) * slots].astype(bf16)
        return carry

    lax.fori_loop(0, qa_ref.shape[0], work, 0)


def backward_kernel(ring_size, masks, first, last, *refs):
    count = len(masks)
    info = refs[0]
    kv_refs = refs[1 : 1 + count]
    rest = refs[1 + count :]
    slots = kv_refs[0].shape[-1]
    cols = GROUP * slots
    if first:
        q_ref, do_ref, o_ref, lse_ref = rest[:4]
        dkv_refs = rest[4 : 4 + count]
        acc_ref, qa_ref, da_ref = rest[4 + count :]
    else:
        qa_ref, da_ref, acc_in = rest[:3]
        dkv_refs = rest[3 : 3 + count]
        if last:
            dq_ref, acc_ref = rest[3 + count :]
        else:
            (acc_ref,) = rest[3 + count :]
        acc_ref[...] = acc_in[...]
    device = info[info.shape[0] - 1]

    def prepare(seq):
        grads = jnp.concatenate([do_ref[seq, h] for h in range(GROUP)], axis=1)
        heads_out = jnp.concatenate([o_ref[seq, h] for h in range(GROUP)], axis=1)
        delta = jnp.sum(grads.astype(f32) * heads_out.astype(f32), axis=0, keepdims=True)
        heads = [q_ref[seq, h] for h in range(GROUP)]
        qa_ref[seq, 0, 0:HEAD_DIM] = jnp.concatenate(heads, axis=1)
        qa_ref[seq, 0, HEAD_DIM:AUG] = extra_rows(
            three_pieces(-lse_ref[seq, 0]) + (jnp.ones((1, cols), f32),), cols
        )
        da_ref[seq, 0, 0:HEAD_DIM] = grads
        da_ref[seq, 0, HEAD_DIM:AUG] = extra_rows(three_pieces(-delta), cols)
        acc_ref[seq] = jnp.zeros(acc_ref.shape[1:], f32)

    def step(seq, keys, values, penalty, diagonal):
        wide = keys.shape[1]
        ones_key = jnp.ones((1, wide), f32)
        key_cols = jnp.concatenate([keys, extra_rows([ones_key] * 3 + [penalty], wide)], axis=0)
        value_cols = jnp.concatenate([values, extra_rows([ones_key] * 3, wide)], axis=0)
        scores = dot(qa_ref[seq, 0], key_cols, TN) * EXP2_SCALE
        if diagonal:
            query_at = lax.broadcasted_iota(jnp.int32, (cols, slots), 0) % slots
            key_at = lax.broadcasted_iota(jnp.int32, (cols, slots), 1)
            scores = jnp.where(key_at <= query_at, scores, NEG)
        weights = jnp.exp2(scores)
        d_scores = (weights * dot(da_ref[seq, 0], value_cols, TN)).astype(bf16)
        d_value = dot(da_ref[seq, 0, 0:HEAD_DIM], weights.astype(bf16), NN)
        d_key = dot(qa_ref[seq, 0, 0:HEAD_DIM], d_scores, NN) * (HEAD_DIM ** (-0.5))
        acc_ref[seq, 0] += dot(keys, d_scores, NT)
        return (d_key.astype(bf16), d_value.astype(bf16))

    def work(seq, carry):
        if first:
            prepare(seq)
        active = block_of(device, seq, ring_size) * slots < info[seq]
        for group in pair_up(masks):
            mask = masks[group[0]]
            blocks = [block_of(device ^ masks[place], seq, ring_size) for place in group]
            turn = needed(device, mask, seq)
            at = seq // 2 if mask else seq

            @pl.when(turn & active)
            def _():
                penalty = [penalty_row(block * slots, slots, info[seq]) for block in blocks]
                keys = [kv_refs[place][at, 0, 0:HEAD_DIM] for place in group]
                values = [kv_refs[place][at, 0, HEAD_DIM:] for place in group]
                d_key, d_value = step(
                    seq,
                    jnp.concatenate(keys, axis=1),
                    jnp.concatenate(values, axis=1),
                    jnp.concatenate(penalty, axis=1),
                    mask == 0,
                )
                for number, place in enumerate(group):
                    part = slice(number * slots, (number + 1) * slots)
                    dkv_refs[place][at, 0, 0:HEAD_DIM] = d_key[:, part]
                    dkv_refs[place][at, 0, HEAD_DIM:] = d_value[:, part]

            @pl.when(turn & jnp.logical_not(active))
            def _():
                for place in group:
                    dkv_refs[place][at] = jnp.zeros(dkv_refs[place].shape[1:], bf16)

        if last:
            d_query = acc_ref[seq, 0] * (HEAD_DIM ** (-0.5))
            for h in range(GROUP):
                dq_ref[seq, h] = d_query[:, h * slots : (h + 1) * slots]
        return carry

    lax.fori_loop(0, qa_ref.shape[0], work, 0)


def head_spec(seqs, rows, lanes, heads=1):
    return pl.BlockSpec((seqs, heads, rows, lanes), lambda group: (0, group, 0, 0))


def kv_specs(kvs):
    return [head_spec(kv.shape[0], kv.shape[2], kv.shape[3]) for kv in kvs]


SMEM_SPEC = pl.BlockSpec(memory_space=pltpu.SMEM)
PARAMS = pltpu.CompilerParams(vmem_limit_bytes=60 * 2**20)


def call_cost(kv_shape, count, products):
    seqs, groups, _, slots = kv_shape
    pairs = seqs * groups * GROUP * slots * slots * count
    return pl.CostEstimate(
        flops=pairs * HEAD_DIM * products * 4,
        transcendentals=pairs,
        bytes_accessed=seqs * groups * count * 4 * HEAD_DIM * slots,
    )


def attend(ring_size, masks, info, queries, kvs, state, last):
    first = state is None
    groups, slots = kvs[0].shape[1], kvs[0].shape[3]
    seqs = queries.shape[0]
    cols = GROUP * slots
    wide_spec = head_spec(seqs, AUG, cols)
    row_spec = head_spec(seqs, 1, cols)
    wide_shape = (seqs, groups, AUG, cols)
    row_shape = jax.ShapeDtypeStruct((seqs, groups, 1, cols), f32)
    state_specs = [row_spec, wide_spec]
    state_shapes = [row_shape, jax.ShapeDtypeStruct(wide_shape, f32)]
    query_spec = wide_spec
    scratch = []
    if first:
        query_spec = head_spec(seqs, HEAD_DIM, slots, GROUP)
        out_specs = [wide_spec] + state_specs
        out_shape = [jax.ShapeDtypeStruct(wide_shape, bf16)] + state_shapes
    elif last:
        out_specs = [head_spec(seqs, HEAD_DIM, slots, GROUP), row_spec]
        out_shape = [jax.ShapeDtypeStruct((seqs, groups * GROUP, HEAD_DIM, slots), bf16), row_shape]
        scratch = [pltpu.VMEM((seqs, 1, 1, cols), f32), pltpu.VMEM((seqs, 1, AUG, cols), f32)]
    else:
        out_specs = state_specs
        out_shape = state_shapes
    return pl.pallas_call(
        functools.partial(forward_kernel, ring_size, masks, first, last),
        grid=(groups,),
        in_specs=[SMEM_SPEC, query_spec]
        + kv_specs(kvs)
        + ([] if first else state_specs),
        out_specs=out_specs,
        out_shape=out_shape,
        scratch_shapes=scratch,
        compiler_params=PARAMS,
        cost_estimate=call_cost(kvs[0].shape, len(masks), 4),
        name="attend",
    )(info, queries, *kvs, *([] if first else state))


def attend_back(ring_size, masks, info, kvs, operands, first, last):
    groups, slots = kvs[0].shape[1], kvs[0].shape[3]
    seqs = operands[0].shape[0]
    cols = GROUP * slots
    heads_spec = head_spec(seqs, HEAD_DIM, slots, GROUP)
    wide_spec = head_spec(seqs, AUG, cols)
    acc_spec = head_spec(seqs, HEAD_DIM, cols)
    kv_shapes = [jax.ShapeDtypeStruct(kv.shape, bf16) for kv in kvs]
    wide_shape = jax.ShapeDtypeStruct((seqs, groups, AUG, cols), bf16)
    acc_shape = jax.ShapeDtypeStruct((seqs, groups, HEAD_DIM, cols), f32)
    scratch = []
    if first:
        operand_specs = [heads_spec] * 3 + [head_spec(seqs, 1, cols)]
        out_specs = [acc_spec, wide_spec, wide_spec]
        out_shape = [acc_shape, wide_shape, wide_shape]
    else:
        operand_specs = [wide_spec, wide_spec, acc_spec]
        if last:
            out_specs = [heads_spec]
            out_shape = [jax.ShapeDtypeStruct((seqs, groups * GROUP, HEAD_DIM, slots), f32)]
            scratch = [pltpu.VMEM((seqs, 1, HEAD_DIM, cols), f32)]
        else:
            out_specs = [acc_spec]
            out_shape = [acc_shape]
    outs = pl.pallas_call(
        functools.partial(backward_kernel, ring_size, masks, first, last),
        grid=(groups,),
        in_specs=[SMEM_SPEC] + kv_specs(kvs) + operand_specs,
        out_specs=kv_specs(kvs) + out_specs,
        out_shape=kv_shapes + out_shape,
        scratch_shapes=scratch,
        compiler_params=PARAMS,
        cost_estimate=call_cost(kvs[0].shape, len(masks), 10),
        name="attend_back",
    )(info, *kvs, *operands)
    return (outs[: len(masks)], outs[len(masks) :])


def feed_forward_kernel(
    ring_size, info, scale, att_ref, tok_ref, teach_ref, wo_ref, gain_ref, w_ref,
    out_ref, dmid_ref, datt_ref, dw_ref, dwo_ref, dgain_ref, loss_ref,
    slope_ref, silu_ref, hidden_ref, dw_acc, dwo_acc,
):
    tile = pl.program_id(0)
    parts, width, hidden3 = w_ref.shape
    part = hidden3 // 3
    tile_rows = tok_ref.shape[1]
    slots = info[info.shape[0] - 2]
    device = info[info.shape[0] - 1]
    seq = tile * tile_rows // slots
    first_pos = block_of(device, seq, ring_size) * slots + tile * tile_rows % slots

    @pl.when(tile == 0)
    def _():
        dw_acc[...] = jnp.zeros(dw_acc.shape, f32)
        dwo_acc[...] = jnp.zeros(dwo_acc.shape, f32)
        dgain_ref[...] = jnp.zeros(dgain_ref.shape, f32)
        loss_ref[...] = jnp.zeros(loss_ref.shape, f32)

    gain = gain_ref[...]
    att = att_ref[0]
    middle = tok_ref[0].astype(f32) + dot(att, wo_ref[...], TN)
    inverse = lax.rsqrt(jnp.mean(middle * middle, axis=-1, keepdims=True) + EPS)
    unit = middle * inverse
    normed = (unit * gain).astype(bf16)
    branch = jnp.zeros((tile_rows, width), f32)
    for t in range(parts):
        both = dot(normed, w_ref[t, :, : 2 * part], NN)
        gate = both[:, :part]
        up = both[:, part:]
        sigmoid = jax.nn.sigmoid(gate)
        silu = gate * sigmoid
        hidden = (silu * up).astype(bf16)
        slope_ref[t] = up * sigmoid * (1.0 + gate * (1.0 - sigmoid))
        silu_ref[t] = silu
        hidden_ref[t] = hidden
        branch = branch + dot(hidden, w_ref[t, :, 2 * part :], NT)
    result = middle + branch
    out_ref[0] = result
    row_pos = first_pos + lax.broadcasted_iota(jnp.int32, (tile_rows, 1), 0)
    valid = (row_pos < info[seq]).astype(f32)
    mismatch = valid * (result - teach_ref[0].astype(f32))
    loss_ref[...] += jnp.sum(mismatch * mismatch)
    d_result = mismatch * scale[0]
    d_branch = d_result.astype(bf16)
    d_normed = jnp.zeros((tile_rows, width), f32)
    for t in range(parts):
        d_hidden = dot(d_branch, w_ref[t, :, 2 * part :], NN)
        d_both = jnp.concatenate([d_hidden * slope_ref[t], d_hidden * silu_ref[t]], axis=1)
        d_both = d_both.astype(bf16)
        dw_acc[t, :, : 2 * part] += dot(normed, d_both, TN)
        dw_acc[t, :, 2 * part :] += dot(d_branch, hidden_ref[t], TN)
        d_normed = d_normed + dot(d_both, w_ref[t, :, : 2 * part], NT)
    dgain_ref[...] += jnp.sum(d_normed * unit, axis=0, keepdims=True)
    d_unit = d_normed * gain
    d_middle = d_result + inverse * (d_unit - unit * jnp.mean(d_unit * unit, axis=-1, keepdims=True))
    dmid_ref[0] = d_middle
    d_attn = d_middle.astype(bf16)
    datt_ref[0] = dot(wo_ref[...], d_attn, NT).astype(bf16)
    dwo_acc[...] += dot(att, d_attn, NN)

    @pl.when(tile == pl.num_programs(0) - 1)
    def _():
        dw_ref[...] = dw_acc[...].astype(bf16)
        dwo_ref[...] = jnp.zeros(dwo_ref.shape, bf16)
        dwo_ref[:, :width] = dwo_acc[...].astype(bf16)


def feed_forward(ring_size, info, scale, attended_t, tokens, teacher, w_o, gain, weights, out_width):
    seqs, slots, width = tokens.shape
    parts, _, hidden3 = weights.shape
    part = hidden3 // 3
    tile_rows = min(512, slots)
    per_seq = slots // tile_rows
    row_spec = pl.BlockSpec((1, tile_rows, width), lambda i: (i // per_seq, i % per_seq, 0))
    col_spec = pl.BlockSpec((1, width, tile_rows), lambda i: (i // per_seq, 0, i % per_seq))

    def whole(*shape):
        return pl.BlockSpec(shape, lambda i: (0,) * len(shape), pipeline_mode=pl.Buffered(1))

    def kept(*shape):
        return pl.BlockSpec(shape, lambda i: (0,) * len(shape))

    rows = seqs * slots
    return pl.pallas_call(
        functools.partial(feed_forward_kernel, ring_size),
        grid=(seqs * per_seq,),
        in_specs=[SMEM_SPEC, SMEM_SPEC, col_spec, row_spec, row_spec]
        + [whole(width, width), whole(1, width), whole(parts, width, hidden3)],
        out_specs=[row_spec, row_spec, col_spec]
        + [kept(parts, width, hidden3), kept(width, out_width), kept(1, width), kept(1, 128)],
        out_shape=[
            jax.ShapeDtypeStruct((seqs, slots, width), f32),
            jax.ShapeDtypeStruct((seqs, slots, width), f32),
            jax.ShapeDtypeStruct((seqs, width, slots), bf16),
            jax.ShapeDtypeStruct((parts, width, hidden3), bf16),
            jax.ShapeDtypeStruct((width, out_width), bf16),
            jax.ShapeDtypeStruct((1, width), f32),
            jax.ShapeDtypeStruct((1, 128), f32),
        ],
        scratch_shapes=[
            pltpu.VMEM((parts, tile_rows, part), f32),
            pltpu.VMEM((parts, tile_rows, part), f32),
            pltpu.VMEM((parts, tile_rows, part), bf16),
            pltpu.VMEM((parts, width, hidden3), f32),
            pltpu.VMEM((width, width), f32),
        ],
        compiler_params=PARAMS,
        cost_estimate=pl.CostEstimate(
            flops=6 * rows * width * (parts * hidden3 + width),
            transcendentals=rows * parts * part,
            bytes_accessed=rows * width * 20 + parts * width * hidden3 * 4,
        ),
        name="feed_forward",
    )(info, scale, attended_t, tokens, teacher, w_o, gain, weights)


RING = ("ctx", "tp")


def swap(value, mask):
    size = lax.axis_size(RING)
    return lax.ppermute(value, RING, [(i, i ^ mask) for i in range(size)])


def mirror(value):
    size = lax.axis_size(RING)
    return lax.ppermute(value, RING, [(i, size - 1 - i) for i in range(size)])


def mirror_odd(value):
    moved = mirror(value[1::2])
    seqs = value.shape[0]
    return jnp.concatenate(
        [moved[s // 2][None] if s % 2 else value[s][None] for s in range(seqs)], axis=0
    )


def move_back(value):
    moved = mirror(value[1::2].astype(bf16)).astype(f32)
    seqs = value.shape[0]
    return jnp.concatenate(
        [moved[s // 2][None] if s % 2 else value[s][None] for s in range(seqs)], axis=0
    )


def add_low(*parts):
    total = parts[0].astype(f32)
    for part in parts[1:]:
        total = total + part.astype(f32)
    return total.astype(bf16)


def gather_fsdp(value):
    if lax.axis_size("fsdp") != 2:
        return lax.all_gather(value, "fsdp", axis=0, tiled=False)
    other = lax.ppermute(value, "fsdp", [(0, 1), (1, 0)])
    at_zero = lax.axis_index("fsdp") == 0
    return jnp.stack([jnp.where(at_zero, value, other), jnp.where(at_zero, other, value)])


def pick_half(value, axis, index):
    half = value.shape[axis] // 2
    return lax.dynamic_slice_in_dim(value, index * half, half, axis)


def join_halves(mine, other, axis, index):
    return jnp.where(
        index == 0,
        jnp.concatenate([mine, other], axis=axis),
        jnp.concatenate([other, mine], axis=axis),
    )


def reduce_steps(value, own):
    fsdp_size, rows, columns = value.shape
    outer = lax.axis_size(RING) // 4
    core = own % 2
    column = (own // 2) % 2
    plane = own // 4
    value = value.astype(bf16)
    value = add_low(pick_half(value, 2, core), swap(pick_half(value, 2, 1 - core), 1))
    value = yield value
    if fsdp_size == 2:
        here = lax.axis_index("fsdp")
        away = lax.dynamic_index_in_dim(value, 1 - here, 0, False)
        mine = lax.dynamic_index_in_dim(value, here, 0, False)
        value = add_low(mine, lax.ppermute(away, "fsdp", [(0, 1), (1, 0)]))
    else:
        value = lax.psum_scatter(value, "fsdp", scatter_dimension=0, tiled=False)
    value = yield value
    value = add_low(pick_half(value, 1, column), swap(pick_half(value, 1, 1 - column), 2))
    value = yield value
    piece = rows // outer

    def rows_of(index):
        return lax.dynamic_slice_in_dim(value, index * piece, piece, 0)

    mine = add_low(
        rows_of(plane), *[swap(rows_of(plane ^ k), 4 * k) for k in range(1, outer)]
    )
    mine = yield mine
    whole = jnp.zeros((rows, columns // 4), bf16)
    whole = lax.dynamic_update_slice_in_dim(whole, mine, plane * piece, 0)
    for k in range(1, outer):
        whole = lax.dynamic_update_slice_in_dim(whole, swap(mine, 4 * k), (plane ^ k) * piece, 0)
    whole = yield whole
    whole = join_halves(whole, swap(whole, 2), 1, column)
    whole = yield whole
    yield join_halves(whole, swap(whole, 1), 1, core)


def sum_steps(value):
    mask = 1
    while mask < lax.axis_size(RING):
        value = yield value + swap(value, mask)
        mask *= 2
    if lax.axis_size("fsdp") == 2:
        value = value + lax.ppermute(value, "fsdp", [(0, 1), (1, 0)])
    else:
        value = lax.psum(value, "fsdp")
    yield value


def advance(steps, value):
    try:
        return steps.send(value)
    except StopIteration:
        return value


def run_steps(steps, value=None):
    while True:
        try:
            value = steps.send(value)
        except StopIteration:
            return value


def shards(
    tokens,
    teacher,
    lengths,
    gain_one,
    w_query,
    w_key,
    w_value,
    w_out,
    gain_two,
    w_gate,
    w_up,
    w_down,
):
    seqs, slots, width = tokens.shape
    kv_width = KV_HEADS * HEAD_DIM
    qkv_width = width + 2 * kv_width
    gain_at = qkv_width
    pack_width = -(-(gain_at + 2) // 128) * 128
    grad_width = -(-(qkv_width + 2) // 512) * 512
    half = w_query.shape[0]
    hidden_part = w_gate.shape[1]
    fsdp_size = lax.axis_size("fsdp")
    tp_size = lax.axis_size("tp")
    ring_size = lax.axis_size(RING)
    outer = ring_size // 4

    tokens_here = mirror_odd(tokens)
    count_total = jnp.sum(gather_fsdp(lengths)).astype(f32)
    packed = jnp.concatenate(
        [
            w_query,
            w_key,
            w_value,
            gain_one[:, None],
            gain_two[:, None],
            jnp.zeros((half, pack_width - gain_at - 2), bf16),
        ],
        axis=1,
    )
    packed = gather_fsdp(packed)
    packed = packed.reshape(width, pack_width)
    w_qkv = packed[:, :qkv_width]
    g_one = packed[:, gain_at].astype(f32)
    g_two = packed[:, gain_at + 1].astype(f32)
    ffn_pack = jnp.concatenate([w_gate, w_up, w_down.T], axis=1)

    own = lax.axis_index(RING).astype(jnp.int32)
    blocks = jnp.stack([block_of(own, s, ring_size) for s in range(seqs)])
    positions = blocks[:, None] * slots + jnp.arange(slots, dtype=jnp.int32)[None]
    cosine, sine = rope_tables(positions)
    info = jnp.concatenate([lengths.astype(jnp.int32), own[None]])

    inputs = tokens_here.astype(f32)
    normed = norm_rows(inputs, g_one).astype(bf16)
    qkv = jnp.einsum("df,sld->sfl", w_qkv, normed, preferred_element_type=f32)
    qk = qkv[:, : width + kv_width].reshape(seqs, HEADS + KV_HEADS, HEAD_DIM, slots)
    qk = rotate_cols(qk, cosine, sine).astype(bf16)
    queries = qk[:, :HEADS]
    values = qkv[:, width + kv_width :].astype(bf16).reshape(seqs, KV_HEADS, HEAD_DIM, slots)

    kv = {0: jnp.concatenate([qk[:, HEADS:], values], axis=2)}

    def outgoing(mask):
        return jnp.where(own < (own ^ mask), kv[0][0::2], kv[0][1::2])

    coming = {mask: swap(outgoing(mask), mask) for mask in [1, 2] + [4 * k for k in range(1, outer)]}
    calls = [(0,), (1, 2, 4)]
    for k in range(1, outer - 1):
        calls.append((4 * k - 1, 4 * k + 1, 4 * k + 2, 4 * k + 4))
    calls.append((4 * outer - 5, 4 * outer - 3, 4 * outer - 2, 4 * outer - 1))
    query_rows, *state = attend(ring_size, calls[0], info, queries, [kv[0]], None, False)
    for number, masks in enumerate(calls[1:], 1):
        if masks[-1] not in coming:
            before, first_state = lax.optimization_barrier((coming[masks[-1] - 1], state[0]))
            coming[masks[-1] - 1] = before
            state = [first_state, state[1]]
            coming[masks[-1]] = swap(before, 1)
        later = {2: [w_out, ffn_pack], 4: [teacher]}.get(number, [])
        *arrived, first_state = lax.optimization_barrier(
            [coming[m] for m in masks] + later + [state[0]]
        )
        if number == 2:
            ffn_all = lax.all_gather(arrived.pop(), ("tp", "fsdp"), axis=0, tiled=False)
            ffn_all = ffn_all.reshape(tp_size, width, 3 * hidden_part)
        if number == 2:
            w_o = gather_fsdp(arrived.pop()).reshape(width, width)
        if number == 4:
            teacher_odd = mirror(arrived.pop()[1::2])
        kv.update(zip(masks, arrived))
        state = [first_state, state[1]]
        for mask in masks:
            if mask % 4 == 0:
                coming[mask + 2] = swap(kv[mask], 2)
                coming[mask + 1] = swap(kv[mask], 1)
            elif mask % 4 == 2 and mask + 1 not in coming:
                coming[mask + 1] = swap(kv[mask], 1)
        state = attend(
            ring_size, masks, info, query_rows, arrived, state, number == len(calls) - 1
        )
    attended, lse = state
    attended, teacher_odd = lax.optimization_barrier((attended, teacher_odd))
    teacher_here = jnp.stack([teacher[0::2], teacher_odd], axis=1).reshape(teacher.shape)
    attended_t = attended.reshape(seqs, width, slots)

    slots_all = seqs * fsdp_size * slots * ring_size
    scale = (slots_all / count_total)[None]
    out_width = -(-width // 512) * 512
    tile_info = jnp.concatenate([lengths.astype(jnp.int32), jnp.full((1,), slots, jnp.int32), own[None]])
    result, d_middle, d_attended_t, d_ffn, d_out_w, d_gain_two, squared_part = feed_forward(
        ring_size, tile_info, scale, attended_t, tokens_here, teacher_here, w_o, g_two[None],
        ffn_all, out_width
    )
    d_attended_t = d_attended_t.reshape(seqs, HEADS, HEAD_DIM, slots)
    d_ffn = d_ffn.reshape(tp_size * fsdp_size, half, 3 * hidden_part)
    d_ffn = lax.psum_scatter(d_ffn, ("tp", "fsdp"), scatter_dimension=0, tiled=False)
    d_out_w = d_out_w.reshape(fsdp_size, half, out_width)
    output = move_back(result)
    out_steps = reduce_steps(d_out_w, own)
    loss_steps = sum_steps(squared_part)
    d_out_w = next(out_steps)
    loss_sum = next(loss_steps)

    calls = [(4 * outer - 2, 4 * outer - 1)]
    for k in reversed(range(1, outer)):
        calls.append((4 * k, 4 * k + 1, 4 * k - 2, 4 * k - 1))
    calls.append((0, 1))
    operands = [queries, d_attended_t, attended, lse]
    core_sums = {}
    sums = {}
    d_kv_terms = []
    for number, masks in enumerate(calls):
        last = number == len(calls) - 1
        if number:
            if number >= 2:
                due = list(calls[number - 2][::2])
            else:
                due = []
            held = [core_sums[m] for m in due] + [d_out_w, loss_sum]
            if number == 2:
                held.append(output)
            if number == 3:
                held.append(d_ffn)
            held = list(lax.optimization_barrier([info] + held))
            info = held.pop(0)
            if number == 3:
                d_ffn = lax.psum(held.pop(), "ctx")
            if number == 2:
                output = held.pop()
            loss_sum = advance(loss_steps, held.pop())
            d_out_w = advance(out_steps, held.pop()) if number < 5 else held.pop()
            for mask, value in zip(due, held):
                core_sums[mask] = value
                if mask % 4:
                    sums[mask - 2] = swap(value, 2)
                else:
                    d_kv_terms.append((mask, swap(add_low(value, sums[mask]), mask)))
        parts, outs = attend_back(
            ring_size, masks, info, [kv[m] for m in masks], operands, number == 0, last
        )
        parts = list(parts)
        for place in range(0, 0 if last else len(masks), 2):
            core_sums[masks[place]] = add_low(parts[place], swap(parts[place + 1], 1))
        if number == 0:
            operands = [outs[1], outs[2], outs[0]]
        else:
            operands = operands[:2] + [outs[0]]
    d_query = outs[0]
    for mask in calls[-2][::2]:
        if mask % 4:
            sums[mask - 2] = swap(core_sums[mask], 2)
        else:
            d_kv_terms.append((mask, swap(add_low(core_sums[mask], sums[mask]), mask)))
    d_kv_terms += [(2, sums[0]), (1, swap(parts[1], 1))]
    d_ffn, parts[0] = lax.optimization_barrier((d_ffn, parts[0]))
    d_kv_halves = []
    for parity in range(2):
        total = parts[0][parity::2].astype(f32)
        for mask, term in d_kv_terms:
            from_it = (own > (own ^ mask)) == (parity == 1)
            total = total + jnp.where(from_it, term.astype(f32), 0.0)
        d_kv_halves.append(total)
    d_kv = jnp.stack(d_kv_halves, axis=1).reshape((seqs,) + parts[0].shape[1:])
    loss_sum = run_steps(loss_steps, loss_sum)
    loss_value = loss_sum[0, 0] / (count_total * width)
    d_ffn = d_ffn.astype(f32)

    d_qk = jnp.concatenate([d_query, d_kv[:, :, :HEAD_DIM]], axis=1)
    d_qk = rotate_cols(d_qk, cosine, -sine).astype(bf16).reshape(seqs, width + kv_width, slots)
    d_values = d_kv[:, :, HEAD_DIM:].astype(bf16).reshape(seqs, kv_width, slots)
    d_qkv = jnp.concatenate([d_qk, d_values], axis=1)
    d_normed = jnp.einsum("sfl,df->sld", d_qkv, w_qkv, preferred_element_type=f32)
    d_qkv_w = jnp.einsum("sld,sfl->df", normed, d_qkv, preferred_element_type=f32)
    norm_one_pull = jax.vjp(norm_rows, inputs, g_one)[1]
    d_inputs_norm, d_gain_one = norm_one_pull(d_normed)
    tokens_grad = d_middle + d_inputs_norm
    back = tokens_grad[1::2].astype(bf16)
    cut = 2 * width // 3 // 128 * 128
    back_parts = [mirror(back[..., :cut]), back[..., cut:]]
    d_packed = jnp.concatenate(
        [
            d_qkv_w,
            d_gain_one[:, None],
            d_gain_two.T,
            jnp.zeros((width, grad_width - qkv_width - 2), f32),
        ],
        axis=1,
    )
    steps = reduce_steps(d_packed.reshape(fsdp_size, half, grad_width), own)
    d_packed = next(steps)
    d_packed = steps.send(d_packed)
    d_packed = steps.send(d_packed)
    back_parts[0], d_packed = lax.optimization_barrier((back_parts[0], d_packed))
    d_packed = steps.send(d_packed)
    d_packed = steps.send(d_packed)
    back_parts[1], d_packed = lax.optimization_barrier((back_parts[1], d_packed))
    back = jnp.concatenate([back_parts[0], mirror(back_parts[1])], axis=2).astype(f32)
    tokens_grad = jnp.stack([tokens_grad[0::2], back], axis=1).reshape(tokens_grad.shape)
    piece = d_packed.shape[1]
    d_packed = run_steps(steps, jnp.concatenate([d_packed, d_out_w], axis=1))
    pieces = d_packed.reshape(half, 4, piece + d_out_w.shape[1])
    d_packed = pieces[:, :, :piece].reshape(half, grad_width).astype(f32)
    d_out_w = pieces[:, :, piece:].reshape(half, out_width).astype(f32)
    return (
        output,
        loss_value,
        tokens_grad,
        d_packed[:, qkv_width],
        d_packed[:, :width],
        d_packed[:, width : width + kv_width],
        d_packed[:, width + kv_width : qkv_width],
        d_out_w[:, :width],
        d_packed[:, qkv_width + 1],
        d_ffn[:, :hidden_part],
        d_ffn[:, hidden_part : 2 * hidden_part],
        d_ffn[:, 2 * hidden_part :].T,
    )


def solution(mesh):
    slots_spec = P("fsdp", ("ctx", "tp"), None)
    rows_spec = P("fsdp", None)
    return jax.shard_map(
        shards,
        mesh=mesh,
        in_specs=(
            slots_spec,
            slots_spec,
            P("fsdp"),
            P("fsdp"),
            rows_spec,
            rows_spec,
            rows_spec,
            rows_spec,
            P("fsdp"),
            P("fsdp", "tp"),
            P("fsdp", "tp"),
            P("tp", "fsdp"),
        ),
        out_specs=(
            slots_spec,
            P(),
            slots_spec,
            P("fsdp"),
            rows_spec,
            rows_spec,
            rows_spec,
            rows_spec,
            P("fsdp"),
            P("fsdp", "tp"),
            P("fsdp", "tp"),
            P("tp", "fsdp"),
        ),
        check_vma=False,
    )
```
